32 devices in a mesh: dp: 8 (over z, x), mp: 4 (over y, core).
Axes of the slice: x: 2, y: 2, z: 4, core: 2. Of those that a mesh axis runs over, the one named last changes fastest.
Arguments:
- tokens: float32 [32, 196, 512], P('dp'), may hold values from -6 to 6
- cotangent: float32 [32, 196, 512], P('dp'), may hold values from -6 to 6
- counts: int32 [8], P('dp'), may hold values from 2 to 4, as said below
- inwards: float32 [2, 3, 512, 512], P(None, None, 'dp', 'mp'), may hold values from -0.25 to 0.25
- inbias: float32 [2, 2, 512], P(None, None, 'mp'), may hold values from -3 to 3
- relative: float32 [2, 169, 16], P(None, None, 'mp'), may hold values from -3 to 322
- outwards: float32 [2, 512, 512], P(None, 'mp', 'dp'), may hold values from -0.75 to 0.75
- widening: float32 [2, 512, 2048], P(None, 'dp', 'mp'), may hold values from -0.25 to 0.25
- widebias: float32 [2, 2048], P(None, 'mp'), may hold values from -3 to 3
- narrowing: float32 [2, 2048, 512], P(None, 'mp', 'dp'), may hold values from -0.125 to 0.125
- norm_gains: float32 [2, 2, 512], replicated, may hold values from 0.1 to 1.9
- offsets: float32 [2, 4, 512], replicated, may hold values from -3 to 3
- mean_inwards: float32 [2, 3, 512, 512], P(None, None, 'dp', 'mp'), may hold values from -6 to 6
- mean_inbias: float32 [2, 2, 512], P(None, None, 'mp'), may hold values from -6 to 6
- mean_relative: float32 [2, 169, 16], P(None, None, 'mp'), may hold values from -6 to 6
- mean_outwards: float32 [2, 512, 512], P(None, 'mp', 'dp'), may hold values from -6 to 6
- mean_widening: float32 [2, 512, 2048], P(None, 'dp', 'mp'), may hold values from -6 to 6
- mean_widebias: float32 [2, 2048], P(None, 'mp'), may hold values from -6 to 6
- mean_narrowing: float32 [2, 2048, 512], P(None, 'mp', 'dp'), may hold values from -6 to 6
- mean_gains: float32 [2, 2, 512], replicated, may hold values from -6 to 6
- mean_offsets: float32 [2, 4, 512], replicated, may hold values from -6 to 6
- square_inwards: float32 [2, 3, 512, 512], P(None, None, 'dp', 'mp'), may hold values from 0.6272 to 62.72
- square_inbias: float32 [2, 2, 512], P(None, None, 'mp'), may hold values from 0.6272 to 62.72
- square_relative: float32 [2, 169, 16], P(None, None, 'mp'), may hold values from 0.6272 to 6.272
- square_outwards: float32 [2, 512, 512], P(None, 'mp', 'dp'), may hold values from 0.6272 to 6.272
- square_widening: float32 [2, 512, 2048], P(None, 'dp', 'mp'), may hold values from 0.6272 to 6.272
- square_widebias: float32 [2, 2048], P(None, 'mp'), may hold values from 0.6272 to 6.272
- square_narrowing: float32 [2, 2048, 512], P(None, 'mp', 'dp'), may hold values from 0.6272 to 6.272
- square_gains: float32 [2, 2, 512], replicated, may hold values from 0.6272 to 62.72
- square_offsets: float32 [2, 4, 512], replicated, may hold values from 0.6272 to 62.72
Outputs:
- output: float32 [32, 196, 512], P('dp')
- grad_tokens: float32 [32, 196, 512], P('dp')
- grad_inwards: float32 [2, 3, 512, 512], P(None, None, 'dp', 'mp')
- grad_inbias: float32 [2, 2, 512], P(None, None, 'mp')
- grad_relative: float32 [2, 169, 16], P(None, None, 'mp')
- grad_outwards: float32 [2, 512, 512], P(None, 'mp', 'dp')
- grad_widening: float32 [2, 512, 2048], P(None, 'dp', 'mp')
- grad_widebias: float32 [2, 2048], P(None, 'mp')
- grad_narrowing: float32 [2, 2048, 512], P(None, 'mp', 'dp')
- grad_gains: float32 [2, 2, 512], replicated
- grad_offsets: float32 [2, 4, 512], replicated
- next_inwards: float32 [2, 3, 512, 512], P(None, None, 'dp', 'mp')
- next_inbias: float32 [2, 2, 512], P(None, None, 'mp')
- next_relative: float32 [2, 169, 16], P(None, None, 'mp')
- next_outwards: float32 [2, 512, 512], P(None, 'mp', 'dp')
- next_widening: float32 [2, 512, 2048], P(None, 'dp', 'mp')
- next_widebias: float32 [2, 2048], P(None, 'mp')
- next_narrowing: float32 [2, 2048, 512], P(None, 'mp', 'dp')
- next_gains: float32 [2, 2, 512], replicated
- next_offsets: float32 [2, 4, 512], replicated
- nextmean_inwards: float32 [2, 3, 512, 512], P(None, None, 'dp', 'mp')
- nextmean_inbias: float32 [2, 2, 512], P(None, None, 'mp')
- nextmean_relative: float32 [2, 169, 16], P(None, None, 'mp')
- nextmean_outwards: float32 [2, 512, 512], P(None, 'mp', 'dp')
- nextmean_widening: float32 [2, 512, 2048], P(None, 'dp', 'mp')
- nextmean_widebias: float32 [2, 2048], P(None, 'mp')
- nextmean_narrowing: float32 [2, 2048, 512], P(None, 'mp', 'dp')
- nextmean_gains: float32 [2, 2, 512], replicated
- nextmean_offsets: float32 [2, 4, 512], replicated
- nextsquare_inwards: float32 [2, 3, 512, 512], P(None, None, 'dp', 'mp')
- nextsquare_inbias: float32 [2, 2, 512], P(None, None, 'mp')
- nextsquare_relative: float32 [2, 169, 16], P(None, None, 'mp')
- nextsquare_outwards: float32 [2, 512, 512], P(None, 'mp', 'dp')
- nextsquare_widening: float32 [2, 512, 2048], P(None, 'dp', 'mp')
- nextsquare_widebias: float32 [2, 2048], P(None, 'mp')
- nextsquare_narrowing: float32 [2, 2048, 512], P(None, 'mp', 'dp')
- nextsquare_gains: float32 [2, 2, 512], replicated
- nextsquare_offsets: float32 [2, 4, 512], replicated
The draws below stay inside these ranges and needn't reach their ends.
Inputs may be any that keep to these rules, and one draw needn't show every extreme that they name: Each dp index holds counts real images in its first slots; some index holds 4.
All inputs are finite; a program needn't handle non-finite values.
Results may differ from the reference program's by a relative error of at most 0.025.
Values may be sent and summed in bfloat16 or wider, within the bound.
No kernel may reach another device: no remote copies, remote signals or barrier semaphores. Data moves between devices by JAX's collectives and lax.ppermute only.
A program may use at most 128 MiB of HBM per device.

```python
import math
import jax
import jax.numpy as jnp
from jax import lax

D = 512
HEADS = 16
HEAD_DIM = 32
FF = 2048
WIN = 7
SIDE = 14
SHIFT = 3
LAYERS = 2
STEP = 3
SLOTS = 4
IMAGES = 32
TOKENS = 6272
RELPOS = 169
N_DP = 8
N_MP = 4


def draw_counts(key, part):
    lowest = (SLOTS + 1) // 2
    picked = jax.random.randint(jax.random.fold_in(key, 1), (N_DP,), lowest, SLOTS + 1)
    order = jax.random.permutation(jax.random.fold_in(key, 2), N_DP)
    picked = picked.at[order[0]].set(SLOTS)
    picked = picked.at[order[1]].set(lowest)
    return picked.astype(jnp.int32)


def draw_relative(key, part):
    extent = (LAYERS, RELPOS, HEADS)
    result = jnp.clip(jax.random.normal(jax.random.fold_in(key, 16), extent, jnp.float32), -3.0, 3.0)
    return result.astype(jnp.float32)


def level_of(own_key, dims, split, low, high):
    level, own = 1.0, jax.random.fold_in(own_key, 6)
    for position, shards_of in split:
        steps = jnp.exp(jax.random.uniform(jax.random.fold_in(own, position), (shards_of,), jnp.float32, low / len(split), high / len(split)))
        level = level * jnp.repeat(steps, dims[position] // shards_of).reshape([-1 if axis == position else 1 for axis in range(len(dims))])
    return level


def bell_draw(own_key, shape, deviation, limit, pieces=(), held_as=jnp.bfloat16):
    values = deviation * jax.random.normal(own_key, shape, jnp.float32)
    if pieces:
        values = values * level_of(own_key, shape, pieces, -0.22, 0.18)
    return jnp.clip(values, -limit, limit).astype(held_as)


def setup_inputs(seed: int = 0) -> dict:
    streams_of = jax.random.split(jax.random.key(seed), 31)
    return {
        "tokens": bell_draw(streams_of[0], (IMAGES, SIDE * SIDE, D), 1.0, 6.0, ((0, 8),), jnp.float32),
        "cotangent": bell_draw(streams_of[1], (IMAGES, SIDE * SIDE, D), 1.0, 6.0, ((0, 8),), jnp.float32),
        "counts": draw_counts(jax.random.fold_in(streams_of[30], 71), 0),
        "inwards": bell_draw(streams_of[3], (LAYERS, 3, D, D), D ** -0.5, 0.25, ((2, 8), (3, 4)), jnp.float32),
        "inbias": bell_draw(streams_of[4], (LAYERS, 2, D), 0.5, 3.0, ((2, 4),), jnp.float32),
        "relative": draw_relative(jax.random.fold_in(streams_of[30], 71), 0),
        "outwards": bell_draw(streams_of[6], (LAYERS, D, D), (D // 7) ** -0.5, 0.75, ((1, 4), (2, 8)), jnp.float32),
        "widening": bell_draw(streams_of[7], (LAYERS, D, FF), D ** -0.5, 0.25, ((1, 8), (2, 4)), jnp.float32),
        "widebias": bell_draw(streams_of[8], (LAYERS, FF), 0.5, 3.0, ((1, 4),), jnp.float32),
        "narrowing": bell_draw(streams_of[9], (LAYERS, FF, D), FF ** -0.5, 0.125, ((1, 4), (2, 8)), jnp.float32),
        "norm_gains": jnp.clip(1.0 + 0.18 * jax.random.normal(streams_of[10], (LAYERS, 2, D), jnp.float32), 0.1, 1.9),
        "offsets": bell_draw(streams_of[11], (LAYERS, 4, D), 0.5, 3.0, (), jnp.float32),
        "mean_inwards": bell_draw(streams_of[12], (LAYERS, 3, D, D), (0.02 * TOKENS ** 0.5), 6.0, ((2, 8), (3, 4)), jnp.float32),
        "mean_inbias": bell_draw(streams_of[13], (LAYERS, 2, D), (0.02 * TOKENS ** 0.5), 6.0, ((2, 4),), jnp.float32),
        "mean_relative": bell_draw(streams_of[14], (LAYERS, RELPOS, HEADS), (0.02 * TOKENS ** 0.5), 6.0, ((2, 4),), jnp.float32),
        "mean_outwards": bell_draw(streams_of[15], (LAYERS, D, D), (0.02 * TOKENS ** 0.5), 6.0, ((1, 4), (2, 8)), jnp.float32),
        "mean_widening": bell_draw(streams_of[16], (LAYERS, D, FF), (0.02 * TOKENS ** 0.5), 6.0, ((1, 8), (2, 4)), jnp.float32),
        "mean_widebias": bell_draw(streams_of[17], (LAYERS, FF), (0.02 * TOKENS ** 0.5), 6.0, ((1, 4),), jnp.float32),
        "mean_narrowing": bell_draw(streams_of[18], (LAYERS, FF, D), (0.02 * TOKENS ** 0.5), 6.0, ((1, 4), (2, 8)), jnp.float32),
        "mean_gains": bell_draw(streams_of[19], (LAYERS, 2, D), (0.02 * TOKENS ** 0.5), 6.0, (), jnp.float32),
        "mean_offsets": bell_draw(streams_of[20], (LAYERS, 4, D), (0.02 * TOKENS ** 0.5), 6.0, (), jnp.float32),
        "square_inwards": jnp.clip(jnp.exp(math.log(62.72) - 4.6051702 * jax.random.uniform(streams_of[21], (LAYERS, 3, D, D), jnp.float32) ** level_of(streams_of[21], (LAYERS, 3, D, D), ((2, 8), (3, 4)), -0.2, 0.2)), 0.6272, 62.72),
        "square_inbias": jnp.clip(jnp.exp(math.log(62.72) - 4.6051702 * jax.random.uniform(streams_of[22], (LAYERS, 2, D), jnp.float32) ** level_of(streams_of[22], (LAYERS, 2, D), ((2, 4),), -0.2, 0.2)), 0.6272, 62.72),
        "square_relative": jnp.clip(jnp.exp(math.log(6.272) - 2.3025851 * jax.random.uniform(streams_of[23], (LAYERS, RELPOS, HEADS), jnp.float32) ** level_of(streams_of[23], (LAYERS, RELPOS, HEADS), ((2, 4),), -0.2, 0.2)), 0.6272, 6.272),
        "square_outwards": jnp.clip(jnp.exp(math.log(6.272) - 2.3025851 * jax.random.uniform(streams_of[24], (LAYERS, D, D), jnp.float32) ** level_of(streams_of[24], (LAYERS, D, D), ((1, 4), (2, 8)), -0.2, 0.2)), 0.6272, 6.272),
        "square_widening": jnp.clip(jnp.exp(math.log(6.272) - 2.3025851 * jax.random.uniform(streams_of[25], (LAYERS, D, FF), jnp.float32) ** level_of(streams_of[25], (LAYERS, D, FF), ((1, 8), (2, 4)), -0.2, 0.2)), 0.6272, 6.272),
        "square_widebias": jnp.clip(jnp.exp(math.log(6.272) - 2.3025851 * jax.random.uniform(streams_of[26], (LAYERS, FF), jnp.float32) ** level_of(streams_of[26], (LAYERS, FF), ((1, 4),), -0.2, 0.2)), 0.6272, 6.272),
        "square_narrowing": jnp.clip(jnp.exp(math.log(6.272) - 2.3025851 * jax.random.uniform(streams_of[27], (LAYERS, FF, D), jnp.float32) ** level_of(streams_of[27], (LAYERS, FF, D), ((1, 4), (2, 8)), -0.2, 0.2)), 0.6272, 6.272),
        "square_gains": jnp.clip(jnp.exp(jax.random.uniform(streams_of[28], (LAYERS, 2, D), jnp.float32, math.log(0.6272), math.log(62.72))), 0.6272, 62.72),
        "square_offsets": jnp.clip(jnp.exp(jax.random.uniform(streams_of[29], (LAYERS, 4, D), jnp.float32, math.log(0.6272), math.log(62.72))), 0.6272, 62.72),
    }


norm_eps = 1e-05
beta_one = 0.9
beta_two = 0.999
learn_rate = 0.02
decay_rate = 0.05
adam_eps = 1e-08

def product(left, right, form):
    return jnp.einsum(form, left.astype(jnp.float32), right.astype(jnp.float32), precision=lax.Precision.HIGHEST)

def group_sum(partial_value):
    return lax.optimization_barrier(jnp.sum(lax.optimization_barrier(partial_value.astype(jnp.bfloat16)).astype(jnp.float32), axis=0))

def relative_onehot():
    places = jnp.arange(WIN * WIN)
    rowpos = places // WIN
    colpos = places % WIN
    lookup = (rowpos[:, None] - rowpos[None, :] + WIN - 1) * (2 * WIN - 1) + (colpos[:, None] - colpos[None, :] + WIN - 1)
    entries = jnp.arange((2 * WIN - 1) ** 2)
    return (lookup.reshape(-1)[:, None] == entries[None, :]).astype(jnp.float32)

def position_bias(rel_table, onehot):
    head_count = rel_table.shape[1]
    return jnp.dot(onehot, rel_table, precision=lax.Precision.HIGHEST).T.reshape(head_count, WIN * WIN, WIN * WIN)

def shift_mask():
    coords = jnp.arange(SIDE)
    stripe = (coords >= SIDE - WIN).astype(jnp.int32) + (coords >= SIDE - SHIFT).astype(jnp.int32)
    region = stripe[:, None] * 3 + stripe[None, :]
    per_window = region.reshape(SIDE // WIN, WIN, SIDE // WIN, WIN).transpose(0, 2, 1, 3).reshape(-1, WIN * WIN)
    return jnp.where(per_window[:, :, None] != per_window[:, None, :], -100.0, 0.0).astype(jnp.float32)

def to_windows(source, shifted):
    images = source.shape[0]
    channels = source.shape[-1]
    lattice = source.reshape(images, SIDE, SIDE, channels)
    if shifted:
        lattice = jnp.roll(lattice, (-SHIFT, -SHIFT), axis=(1, 2))
    lattice = lattice.reshape(images, SIDE // WIN, WIN, SIDE // WIN, WIN, channels).transpose(0, 1, 3, 2, 4, 5)
    return lattice.reshape(images * (SIDE // WIN) ** 2, WIN * WIN, channels)

def from_windows(windows, images, shifted):
    channels = windows.shape[-1]
    lattice = windows.reshape(images, SIDE // WIN, SIDE // WIN, WIN, WIN, channels).transpose(0, 1, 3, 2, 4, 5)
    lattice = lattice.reshape(images, SIDE, SIDE, channels)
    if shifted:
        lattice = jnp.roll(lattice, (SHIFT, SHIFT), axis=(1, 2))
    return lattice.reshape(images, SIDE * SIDE, channels)

def layer_norm(hidden, gain, offset):
    centered = hidden - lax.optimization_barrier(jnp.mean(hidden, axis=-1, keepdims=True))
    inverse = lax.rsqrt(lax.optimization_barrier(jnp.mean(centered * centered, axis=-1, keepdims=True)) + norm_eps)
    normed = centered * inverse
    return (normed * gain + offset, normed, inverse)

def norm_back(upstream, normed, inverse, gain):
    d_normed = upstream * gain
    d_gain = lax.optimization_barrier(jnp.sum(upstream * normed, axis=(0, 1)))
    d_offset = lax.optimization_barrier(jnp.sum(upstream, axis=(0, 1)))
    d_source = inverse * (d_normed - lax.optimization_barrier(jnp.mean(d_normed, axis=-1, keepdims=True)) - normed * lax.optimization_barrier(jnp.mean(d_normed * normed, axis=-1, keepdims=True)))
    return (d_source, d_gain, d_offset)

def gelu_pair(pre_act):
    cdf = 0.5 * (1.0 + lax.erf(pre_act * 0.7071067811865476))
    density = jnp.exp(-0.5 * pre_act * pre_act) * 0.3989422804014327
    return (pre_act * cdf, cdf + pre_act * density)

def attention_scores(query_bf, key_bf, pos_bias, shifted, product):
    scores = product(query_bf, key_bf, 'wqhc,wkhc->whqk') + pos_bias[None]
    if shifted:
        region_mask = shift_mask()
        pane_count = region_mask.shape[0]
        head_count = scores.shape[1]
        scores = (scores.reshape(-1, pane_count, head_count, WIN * WIN, WIN * WIN) + region_mask[None, :, None]).reshape(scores.shape)
    return scores

def layer_forward(hidden, weights, shifted, groups, reducer, product):
    w_in, in_bias, pos_bias, w_out, w_wide, wide_bias, w_narrow, gains, offsets = weights
    images, tokens_img, model_dim = hidden.shape
    row_count = images * tokens_img
    local_dim = w_in.shape[2]
    head_count = local_dim // HEAD_DIM
    wide_dim = w_wide.shape[1]
    factor = HEAD_DIM ** (-0.5)
    normed_in, unit_in, inv_in = layer_norm(hidden, gains[0], offsets[0])
    attn_in = to_windows(normed_in.astype(jnp.bfloat16), shifted)
    pane_count = attn_in.shape[0]
    projected = product(attn_in, w_in, 'wtd,sde->swte')
    query_bf = ((projected[0] + in_bias[0]) * factor).astype(jnp.bfloat16).reshape(pane_count, WIN * WIN, head_count, HEAD_DIM)
    key_bf = projected[1].astype(jnp.bfloat16).reshape(pane_count, WIN * WIN, head_count, HEAD_DIM)
    value_bf = (projected[2] + in_bias[1]).astype(jnp.bfloat16).reshape(pane_count, WIN * WIN, head_count, HEAD_DIM)
    scores = attention_scores(query_bf, key_bf, pos_bias, shifted, product)
    highest = lax.optimization_barrier(jnp.max(scores, axis=-1, keepdims=True))
    log_total = highest + jnp.log(lax.optimization_barrier(jnp.sum(jnp.exp(scores - highest), axis=-1, keepdims=True)))
    prob_bf = jnp.exp(scores - log_total).astype(jnp.bfloat16)
    mixed = product(prob_bf, value_bf, 'whqk,wkhc->wqhc').reshape(pane_count, WIN * WIN, local_dim)
    mixed_bf = from_windows(mixed, images, shifted).astype(jnp.bfloat16).reshape(row_count, local_dim)
    partial_value = product(mixed_bf.reshape(row_count, groups, local_dim // groups), w_out.reshape(groups, local_dim // groups, model_dim), 'rgk,gkd->grd')
    after_attn = hidden + (reducer(partial_value) + offsets[2]).reshape(hidden.shape)
    normed_mid, unit_mid, inv_mid = layer_norm(after_attn, gains[1], offsets[1])
    mlp_in = normed_mid.astype(jnp.bfloat16).reshape(row_count, model_dim)
    pre_act = product(mlp_in, w_wide, 'rd,df->rf') + wide_bias
    activ_bf = gelu_pair(pre_act)[0].astype(jnp.bfloat16)
    partial_mlp = product(activ_bf.reshape(row_count, groups, wide_dim // groups), w_narrow.reshape(groups, wide_dim // groups, model_dim), 'rgf,gfd->grd')
    result = after_attn + (reducer(partial_mlp) + offsets[3]).reshape(hidden.shape)
    kept = (unit_in, inv_in, attn_in, query_bf, key_bf, value_bf, log_total, mixed_bf, unit_mid, inv_mid, mlp_in, pre_act, activ_bf)
    return (result, kept)

def layer_backward(grad_out, kept, weights, shifted, groups, reducer, product, onehot):
    w_in, in_bias, pos_bias, w_out, w_wide, wide_bias, w_narrow, gains, offsets = weights
    unit_in, inv_in, attn_in, query_bf, key_bf, value_bf, log_total, mixed_bf, unit_mid, inv_mid, mlp_in, pre_act, activ_bf = kept
    images, tokens_img, model_dim = grad_out.shape
    row_count = images * tokens_img
    local_dim = w_in.shape[2]
    head_count = local_dim // HEAD_DIM
    wide_dim = w_wide.shape[1]
    factor = HEAD_DIM ** (-0.5)
    pane_count = attn_in.shape[0]
    grad_rows = grad_out.reshape(row_count, model_dim)
    d_off_mlp = lax.optimization_barrier(jnp.sum(grad_rows, axis=0))
    grad_bf = grad_rows.astype(jnp.bfloat16)
    d_narrow = product(activ_bf, grad_bf, 'rf,rd->fd')
    d_act = product(grad_bf, w_narrow, 'rd,fd->rf')
    d_pre = d_act * gelu_pair(pre_act)[1]
    d_wide_bias = lax.optimization_barrier(jnp.sum(d_pre, axis=0))
    d_pre_bf = d_pre.astype(jnp.bfloat16)
    d_wide = product(mlp_in, d_pre_bf, 'rd,rf->df')
    partial_value = product(d_pre_bf.reshape(row_count, groups, wide_dim // groups), w_wide.reshape(model_dim, groups, wide_dim // groups), 'rgf,dgf->grd')
    d_mid, d_gain_mid, d_off_mid = norm_back(reducer(partial_value).reshape(grad_out.shape), unit_mid, inv_mid, gains[1])
    d_after = grad_out + d_mid
    d_rows = d_after.reshape(row_count, model_dim)
    d_off_attn = lax.optimization_barrier(jnp.sum(d_rows, axis=0))
    d_rows_bf = d_rows.astype(jnp.bfloat16)
    d_out = product(mixed_bf, d_rows_bf, 'rk,rd->kd')
    d_mixed = product(d_rows_bf, w_out, 'rd,kd->rk').astype(jnp.bfloat16)
    d_mixed_bf = to_windows(d_mixed.reshape(images, tokens_img, local_dim), shifted).reshape(pane_count, WIN * WIN, head_count, HEAD_DIM)
    scores = attention_scores(query_bf, key_bf, pos_bias, shifted, product)
    probs = jnp.exp(scores - log_total)
    prob_bf = probs.astype(jnp.bfloat16)
    d_prob = product(d_mixed_bf, value_bf, 'wqhc,wkhc->whqk')
    d_value = product(prob_bf, d_mixed_bf, 'whqk,wqhc->wkhc')
    d_score = probs * (d_prob - lax.optimization_barrier(jnp.sum(probs * d_prob, axis=-1, keepdims=True)))
    d_table = jnp.dot(onehot.T, lax.optimization_barrier(jnp.sum(d_score, axis=0)).reshape(head_count, -1).T, precision=lax.Precision.HIGHEST)
    d_score_bf = d_score.astype(jnp.bfloat16)
    d_query = product(d_score_bf, key_bf, 'whqk,wkhc->wqhc') * factor
    d_key = product(d_score_bf, query_bf, 'whqk,wqhc->wkhc')
    d_proj = jnp.stack([d_query, d_key, d_value]).reshape(3, pane_count, WIN * WIN, local_dim)
    d_in_bias = jnp.stack([lax.optimization_barrier(jnp.sum(d_proj[0], axis=(0, 1))), lax.optimization_barrier(jnp.sum(d_proj[2], axis=(0, 1)))])
    d_proj_bf = d_proj.astype(jnp.bfloat16)
    d_in = product(attn_in, d_proj_bf, 'wtd,swte->sde')
    partial_in = product(d_proj_bf.reshape(3, pane_count, WIN * WIN, groups, local_dim // groups), w_in.reshape(3, model_dim, groups, local_dim // groups), 'swtgk,sdgk->gwtd')
    d_first, d_gain_in, d_off_in = norm_back(from_windows(reducer(partial_in), images, shifted), unit_in, inv_in, gains[0])
    layer_grads = (d_in, d_in_bias, d_table, d_out, d_wide, d_wide_bias, d_narrow, jnp.stack([d_gain_in, d_gain_mid]), jnp.stack([d_off_in, d_off_mid, d_off_attn, d_off_mlp]))
    return (d_after + d_first, layer_grads)

def adam_update(weight, gradient, moment_one, second, decay_on):
    first_new = beta_one * moment_one + (1.0 - beta_one) * gradient
    second_new = beta_two * second + (1.0 - beta_two) * gradient * gradient
    first_hat = first_new / (1.0 - beta_one ** STEP)
    second_hat = second_new / (1.0 - beta_two ** STEP)
    updated = weight - learn_rate * (first_hat / (jnp.sqrt(second_hat) + adam_eps) + decay_on * weight)
    return (updated, first_new, second_new)

def reference(tokens, cotangent, counts, inwards, inbias, relative, outwards, widening, widebias, narrowing, norm_gains, offsets, mean_inwards, mean_inbias, mean_relative, mean_outwards, mean_widening, mean_widebias, mean_narrowing, mean_gains, mean_offsets, square_inwards, square_inbias, square_relative, square_outwards, square_widening, square_widebias, square_narrowing, square_gains, square_offsets):
    params = [inwards, inbias, relative, outwards, widening, widebias, narrowing, norm_gains, offsets]
    first_moments = [mean_inwards, mean_inbias, mean_relative, mean_outwards, mean_widening, mean_widebias, mean_narrowing, mean_gains, mean_offsets]
    second_moments = [square_inwards, square_inbias, square_relative, square_outwards, square_widening, square_widebias, square_narrowing, square_gains, square_offsets]
    onehot = relative_onehot()
    layer_total = inwards.shape[0]
    stacks = []
    for layer in range(layer_total):
        stacks.append((inwards[layer].astype(jnp.bfloat16), inbias[layer], position_bias(relative[layer], onehot), outwards[layer].astype(jnp.bfloat16), widening[layer].astype(jnp.bfloat16), widebias[layer], narrowing[layer].astype(jnp.bfloat16), norm_gains[layer], offsets[layer]))
    image_ids = jnp.arange(tokens.shape[0]).astype(jnp.int32)
    real_mask = (image_ids % SLOTS < counts[image_ids // SLOTS]).astype(jnp.float32)
    channels = tokens.shape[2]
    blocks = (tokens.reshape(N_DP, SLOTS, SIDE * SIDE, channels), cotangent.reshape(N_DP, SLOTS, SIDE * SIDE, channels), real_mask.reshape(N_DP, SLOTS))

    def one_block(totals, block):
        hidden, upstream, real_rows = block
        kept_all = []
        for layer in range(layer_total):
            hidden, kept = layer_forward(hidden, stacks[layer], layer % 2 == 1, N_MP, group_sum, product)
            kept_all.append(kept)
        upstream = upstream * real_rows[:, None, None]
        per_layer = [None] * layer_total
        for layer in reversed(range(layer_total)):
            upstream, per_layer[layer] = layer_backward(upstream, kept_all[layer], stacks[layer], layer % 2 == 1, N_MP, group_sum, product, onehot)
        totals = tuple((totals[member] + jnp.stack([per_layer[layer][member] for layer in range(layer_total)]) for member in range(len(params))))
        return (totals, (hidden * real_rows[:, None, None], upstream))
    zeros = tuple((jnp.zeros(param.shape, jnp.float32) for param in params))
    totals, (outputs, grads_in) = lax.scan(one_block, zeros, blocks)
    output = outputs.reshape(tokens.shape)
    grad_tokens = grads_in.reshape(tokens.shape)
    decays = [decay_rate, 0.0, 0.0, decay_rate, decay_rate, 0.0, decay_rate, 0.0, 0.0]
    results = [adam_update(params[member], totals[member], first_moments[member], second_moments[member], decays[member]) for member in range(len(params))]
    grad_inwards, grad_inbias, grad_relative, grad_outwards, grad_widening, grad_widebias, grad_narrowing, grad_gains, grad_offsets = totals
    next_inwards, nextmean_inwards, nextsquare_inwards = results[0]
    next_inbias, nextmean_inbias, nextsquare_inbias = results[1]
    next_relative, nextmean_relative, nextsquare_relative = results[2]
    next_outwards, nextmean_outwards, nextsquare_outwards = results[3]
    next_widening, nextmean_widening, nextsquare_widening = results[4]
    next_widebias, nextmean_widebias, nextsquare_widebias = results[5]
    next_narrowing, nextmean_narrowing, nextsquare_narrowing = results[6]
    next_gains, nextmean_gains, nextsquare_gains = results[7]
    next_offsets, nextmean_offsets, nextsquare_offsets = results[8]
    return (output, grad_tokens, grad_inwards, grad_inbias, grad_relative, grad_outwards, grad_widening, grad_widebias, grad_narrowing, grad_gains, grad_offsets, next_inwards, next_inbias, next_relative, next_outwards, next_widening, next_widebias, next_narrowing, next_gains, next_offsets, nextmean_inwards, nextmean_inbias, nextmean_relative, nextmean_outwards, nextmean_widening, nextmean_widebias, nextmean_narrowing, nextmean_gains, nextmean_offsets, nextsquare_inwards, nextsquare_inbias, nextsquare_relative, nextsquare_outwards, nextsquare_widening, nextsquare_widebias, nextsquare_narrowing, nextsquare_gains, nextsquare_offsets)
```

```python
import functools

import jax
import jax.numpy as jnp
import numpy as np
from jax import lax
from jax.experimental import pallas as pl
from jax.experimental.pallas import tpu as pltpu
from jax.sharding import Mesh
from jax.sharding import PartitionSpec as P

HEAD_DIM = 32
WIN = 7
SIDE = 14
SHIFT = 3
STEP = 3

norm_eps = 1e-05
beta_one = 0.9
beta_two = 0.999
learn_rate = 0.02
decay_rate = 0.05
adam_eps = 1e-08

CELLS = WIN * WIN
PANES = (SIDE // WIN) ** 2
SLOT = 64
GROUPS = 2
DIRECT_MAX = 8
f32 = jnp.float32
bf16 = jnp.bfloat16


def window_order(shifted):
    grid = np.arange(SIDE * SIDE).reshape(SIDE, SIDE)
    if shifted:
        grid = np.roll(grid, (-SHIFT, -SHIFT), axis=(0, 1))
    side_panes = SIDE // WIN
    return grid.reshape(side_panes, WIN, side_panes, WIN).transpose(0, 2, 1, 3).reshape(-1, CELLS)


def selection(shifted, images):
    order = window_order(shifted)
    pick = np.zeros((PANES, SLOT, SIDE * SIDE), np.float32)
    for pane in range(PANES):
        pick[pane, np.arange(CELLS), order[pane]] = 1.0
    pick = pick.reshape(PANES * SLOT, SIDE * SIDE)
    return np.kron(np.eye(images, dtype=np.float32), pick)


def lookup_onehot():
    places = np.arange(CELLS)
    rowpos, colpos = places // WIN, places % WIN
    lookup = (rowpos[:, None] - rowpos[None, :] + WIN - 1) * (2 * WIN - 1) + (
        colpos[:, None] - colpos[None, :] + WIN - 1
    )
    full = np.full((SLOT, SLOT), -1)
    full[:CELLS, :CELLS] = lookup
    return (np.arange((2 * WIN - 1) ** 2)[:, None] == full.reshape(-1)[None, :]).astype(np.float32)


def pane_mask(shifted):
    pad = np.zeros((SLOT, SLOT), np.float32)
    pad[:, CELLS:] = -1e30
    if not shifted:
        return pad[None]
    coords = np.arange(SIDE)
    stripe = (coords >= SIDE - WIN).astype(int) + (coords >= SIDE - SHIFT).astype(int)
    region = (stripe[:, None] * 3 + stripe[None, :]).reshape(-1)
    side_panes = SIDE // WIN
    per = region.reshape(side_panes, WIN, side_panes, WIN).transpose(0, 2, 1, 3).reshape(-1, CELLS)
    out = np.repeat(pad[None], PANES, axis=0)
    out[:, :CELLS, :CELLS] = np.where(per[:, :, None] != per[:, None, :], -100.0, 0.0)
    return out


def dot(left, right, lc, rc):
    return lax.dot_general(left, right, (((lc,), (rc,)), ((), ())), preferred_element_type=f32)


def unit_norm(hidden):
    centered = hidden - jnp.mean(hidden, axis=-1, keepdims=True)
    inverse = lax.rsqrt(jnp.mean(centered * centered, axis=-1, keepdims=True) + norm_eps)
    return centered * inverse, inverse


def norm_back(upstream, normed, inverse, gain):
    d_normed = upstream * gain
    source = inverse * (
        d_normed
        - jnp.mean(d_normed, axis=-1, keepdims=True)
        - normed * jnp.mean(d_normed * normed, axis=-1, keepdims=True)
    )
    return source, jnp.sum(upstream * normed, axis=0, keepdims=True), jnp.sum(
        upstream, axis=0, keepdims=True
    )


def head_masks(width):
    lane = lax.broadcasted_iota(jnp.int32, (1, width), 1) // HEAD_DIM
    return [lane == head for head in range(width // HEAD_DIM)]


def spread(value, masks):
    zero = jnp.zeros_like(value)
    return jnp.concatenate([jnp.where(mask, value, zero) for mask in masks], axis=0)


def gather_heads(stacked, masks):
    total = None
    for head, mask in enumerate(masks):
        part = jnp.where(mask, stacked[head * SLOT : (head + 1) * SLOT], 0.0)
        total = part if total is None else total + part
    return total


def call(kernel, outs, name, *args):
    return pl.pallas_call(
        kernel,
        out_shape=[jax.ShapeDtypeStruct(shape, dtype) for shape, dtype in outs],
        compiler_params=pltpu.CompilerParams(vmem_limit_bytes=60 * 1024 * 1024),
        name=name,
    )(*args)


def attn_fwd(first, vec, source, weights, bias_qv, pos, pick):
    rows, width = source[0].shape
    win_rows = pick.shape[0]
    panes = win_rows // SLOT
    local = weights[0].shape[1] // 4
    heads = local // HEAD_DIM
    masks_n = pos.shape[0]
    factor = HEAD_DIM ** (-0.5)
    n_src = len(source)

    def kernel(*refs):
        src = refs[:n_src]
        vec_ref, w0, w1, bias_ref, pos_ref, pick_ref = refs[n_src : n_src + 6]
        h_ref, a_ref, q_ref, k_ref, v_ref, prob_ref, mixed_ref, part_ref, mw_ref = refs[n_src + 6 :]
        hidden = src[0][...]
        if not first:
            hidden = hidden + (
                src[1][...].astype(f32) + src[2][...].astype(f32) + vec_ref[2:3, :]
            )
            h_ref[...] = hidden
        else:
            h_ref[...] = jnp.zeros_like(h_ref)
        normed, _ = unit_norm(hidden)
        a = (normed * vec_ref[0:1, :] + vec_ref[1:2, :]).astype(bf16)
        a_ref[...] = a
        a_win = dot(pick_ref[...], a, 1, 0).astype(bf16)
        for g, w in enumerate((w0, w1)):
            proj = dot(a_win, w[:, : 3 * local], 1, 0)
            q = ((proj[:, :local] + bias_ref[0:1, g * local : (g + 1) * local]) * factor).astype(bf16)
            k = proj[:, local : 2 * local].astype(bf16)
            v = (proj[:, 2 * local :] + bias_ref[1:2, g * local : (g + 1) * local]).astype(bf16)
            q_ref[g] = q.reshape(panes, SLOT, local)
            k_ref[g] = k.reshape(panes, SLOT, local)
            v_ref[g] = v.reshape(panes, SLOT, local)
        masks = head_masks(local)

        def step(w, carry):
            for g in range(GROUPS):
                q, k, v = q_ref[g, w], k_ref[g, w], v_ref[g, w]
                score = dot(spread(q, masks), k, 1, 1) + pos_ref[w % masks_n if masks_n > 1 else 0, g]
                top = jnp.max(score, axis=-1, keepdims=True)
                grown = jnp.exp(score - top)
                prob = grown * (1.0 / jnp.sum(grown, axis=-1, keepdims=True))
                prob_ref[w, g] = prob
                mixed = gather_heads(dot(prob.astype(bf16), v, 1, 0), masks)
                mw_ref[w, :, g * local : (g + 1) * local] = mixed.astype(bf16)
            return carry

        lax.fori_loop(0, panes, step, 0)
        mixed = dot(pick_ref[...], mw_ref[...].reshape(win_rows, GROUPS * local), 0, 0).astype(bf16)
        mixed_ref[...] = mixed
        part = None
        for g, w in enumerate((w0, w1)):
            term = dot(mixed[:, g * local : (g + 1) * local], w[:, 3 * local :], 1, 1)
            part = term if part is None else part + term
        part_ref[...] = part.astype(bf16)

    h_shape = (rows, width) if not first else (8, 128)
    outs = [
        (h_shape, f32),
        ((rows, width), bf16),
        ((GROUPS, panes, SLOT, local), bf16),
        ((GROUPS, panes, SLOT, local), bf16),
        ((GROUPS, panes, SLOT, local), bf16),
        ((panes, GROUPS, heads * SLOT, SLOT), f32),
        ((rows, GROUPS * local), bf16),
        ((rows, width), bf16),
    ]
    res = pl.pallas_call(
        kernel,
        out_shape=[jax.ShapeDtypeStruct(shape, dtype) for shape, dtype in outs],
        scratch_shapes=[pltpu.VMEM((panes, SLOT, GROUPS * local), bf16)],
        compiler_params=pltpu.CompilerParams(vmem_limit_bytes=60 * 1024 * 1024),
        name="attn_fwd",
    )(*source, vec, *weights, bias_qv, pos, pick)
    if first:
        res = [source[0]] + list(res[1:])
    return res


def mlp_fwd(hidden, own, recv, vec, weights, wide_bias):
    rows, width = hidden.shape
    local = weights[0].shape[1] // 2

    def kernel(h_ref, own_ref, recv_ref, vec_ref, w0, w1, wb_ref, h1_ref, c_ref, z_ref, s_ref, p_ref):
        h1 = h_ref[...] + (own_ref[...].astype(f32) + recv_ref[...].astype(f32) + vec_ref[2:3, :])
        h1_ref[...] = h1
        normed, _ = unit_norm(h1)
        c = (normed * vec_ref[0:1, :] + vec_ref[1:2, :]).astype(bf16)
        c_ref[...] = c
        part = None
        for g, w in enumerate((w0, w1)):
            u = dot(c, w[:, :local], 1, 0) + wb_ref[g : g + 1, :]
            cdf = 0.5 * (1.0 + lax.erf(u * 0.7071067811865476))
            density = jnp.exp(-0.5 * u * u) * 0.3989422804014327
            z = (u * cdf).astype(bf16)
            z_ref[:, g * local : (g + 1) * local] = z
            s_ref[:, g * local : (g + 1) * local] = (cdf + u * density).astype(bf16)
            term = dot(z, w[:, local:], 1, 1)
            part = term if part is None else part + term
        p_ref[...] = part.astype(bf16)

    outs = [
        ((rows, width), f32),
        ((rows, width), bf16),
        ((rows, GROUPS * local), bf16),
        ((rows, GROUPS * local), bf16),
        ((rows, width), bf16),
    ]
    return call(kernel, outs, "mlp_fwd", hidden, own, recv, vec, *weights, wide_bias)


def mlp_bwd(last, source, vec, slope, weights):
    rows, width = source[0].shape
    local = weights[0].shape[1] // 2
    n_src = len(source)

    def kernel(*refs):
        src = refs[:n_src]
        vec_ref, s_ref, w0, w1 = refs[n_src : n_src + 4]
        g_ref, gb_ref, du_ref, p_ref, sum_ref = refs[n_src + 4 : n_src + 9]
        sum_ref[...] = jnp.zeros_like(sum_ref)
        if last:
            keep = src[4][...]
            grad = src[0][...] * keep
            result = src[1][...] + (src[2][...].astype(f32) + src[3][...].astype(f32) + vec_ref[0:1, :])
            refs[n_src + 9][...] = result * keep
        else:
            normed, inverse = unit_norm(src[3][...])
            upstream = src[1][...].astype(f32) + src[2][...].astype(f32)
            first_grad, d_gain, d_off = norm_back(upstream, normed, inverse, vec_ref[0:1, :])
            grad = src[0][...] + first_grad
            sum_ref[1:2, :] = d_gain
            sum_ref[2:3, :] = d_off
        g_ref[...] = grad
        sum_ref[0:1, :] = jnp.sum(grad, axis=0, keepdims=True)
        grad_b = grad.astype(bf16)
        gb_ref[...] = grad_b
        part = None
        for g, w in enumerate((w0, w1)):
            du = dot(grad_b, w[:, local:], 1, 0) * s_ref[:, g * local : (g + 1) * local].astype(f32)
            sum_ref[3 + g : 4 + g, :local] = jnp.sum(du, axis=0, keepdims=True)
            du_b = du.astype(bf16)
            du_ref[:, g * local : (g + 1) * local] = du_b
            term = dot(du_b, w[:, :local], 1, 1)
            part = term if part is None else part + term
        p_ref[...] = part.astype(bf16)

    outs = [
        ((rows, width), f32),
        ((rows, width), bf16),
        ((rows, GROUPS * local), bf16),
        ((rows, width), bf16),
        ((8, max(width, local)), f32),
    ]
    if last:
        outs.append(((rows, width), f32))
    return call(kernel, outs, "mlp_bwd", *source, vec, slope, *weights)


def mlp_grads(c, du_b, z, grad_b):
    width = c.shape[1]
    local = z.shape[1] // GROUPS

    def kernel(c_ref, du_ref, z_ref, g_ref, o0, o1):
        for g, out in enumerate((o0, o1)):
            cols = slice(g * local, (g + 1) * local)
            out[:, :local] = dot(c_ref[...], du_ref[:, cols], 0, 0).astype(bf16)
            out[:, local:] = dot(g_ref[...], z_ref[:, cols], 0, 0).astype(bf16)

    return call(kernel, [((width, 2 * local), bf16)] * 2, "mlp_grads", c, du_b, z, grad_b)


def attn_bwd(grad, own, recv, h1, vec, weights, q, k, v, prob, pick):
    rows, width = grad.shape
    win_rows = pick.shape[0]
    panes = win_rows // SLOT
    local = weights[0].shape[1] // 4
    heads = local // HEAD_DIM
    factor = HEAD_DIM ** (-0.5)

    def kernel(
        g_ref, own_ref, recv_ref, h1_ref, vec_ref, w0, w1, q_ref, k_ref, v_ref, prob_ref, pick_ref,
        dh_ref, dhb_ref, dp_ref, part_ref, sum_ref, ds_ref, dm_ref, dw_ref, bias_ref,
    ):
        normed, inverse = unit_norm(h1_ref[...])
        upstream = own_ref[...].astype(f32) + recv_ref[...].astype(f32)
        d_mid, d_gain, d_off = norm_back(upstream, normed, inverse, vec_ref[0:1, :])
        dh1 = g_ref[...] + d_mid
        dh_ref[...] = dh1
        sum_ref[...] = jnp.zeros_like(sum_ref)
        sum_ref[0:1, :] = d_gain
        sum_ref[1:2, :] = d_off
        sum_ref[2:3, :] = jnp.sum(dh1, axis=0, keepdims=True)
        dh_b = dh1.astype(bf16)
        dhb_ref[...] = dh_b
        for g, w in enumerate((w0, w1)):
            d_mixed = dot(dh_b, w[:, 3 * local :], 1, 0).astype(bf16)
            d_win = dot(pick_ref[...], d_mixed, 1, 0).astype(bf16)
            dm_ref[g] = d_win.reshape(panes, SLOT, local)
        ds_ref[...] = jnp.zeros_like(ds_ref)
        bias_ref[...] = jnp.zeros_like(bias_ref)
        masks = head_masks(local)

        def step(w, carry):
            for g in range(GROUPS):
                keys, values = k_ref[g, w], v_ref[g, w]
                d_out = spread(dm_ref[g, w], masks)
                queries = spread(q_ref[g, w], masks)
                probs = prob_ref[w, g]
                d_prob = dot(d_out, values, 1, 1)
                d_value = dot(probs.astype(bf16), d_out, 0, 0)
                d_score = probs * (d_prob - jnp.sum(probs * d_prob, axis=-1, keepdims=True))
                ds_ref[g] += d_score
                d_score_b = d_score.astype(bf16)
                d_query = gather_heads(dot(d_score_b, keys, 1, 0), masks) * factor
                d_key = dot(d_score_b, queries, 0, 0)
                base = g * 3 * local
                dw_ref[w, :, base : base + local] = d_query.astype(bf16)
                dw_ref[w, :, base + local : base + 2 * local] = d_key.astype(bf16)
                dw_ref[w, :, base + 2 * local : base + 3 * local] = d_value.astype(bf16)
                bias_ref[0:1, g * local : (g + 1) * local] += jnp.sum(d_query, axis=0, keepdims=True)
                bias_ref[1:2, g * local : (g + 1) * local] += jnp.sum(d_value, axis=0, keepdims=True)
            return carry

        lax.fori_loop(0, panes, step, 0)
        sum_ref[3:4, : GROUPS * local] = bias_ref[0:1, :]
        sum_ref[4:5, : GROUPS * local] = bias_ref[1:2, :]
        d_proj = dot(
            pick_ref[...], dw_ref[...].reshape(win_rows, GROUPS * 3 * local), 0, 0
        ).astype(bf16)
        dp_ref[...] = d_proj
        part = None
        for g, w in enumerate((w0, w1)):
            term = dot(d_proj[:, g * 3 * local : (g + 1) * 3 * local], w[:, : 3 * local], 1, 1)
            part = term if part is None else part + term
        part_ref[...] = part.astype(bf16)

    outs = [
        ((rows, width), f32),
        ((rows, width), bf16),
        ((rows, GROUPS * 3 * local), bf16),
        ((rows, width), bf16),
        ((8, width), f32),
        ((GROUPS, heads * SLOT, SLOT), f32),
    ]
    return pl.pallas_call(
        kernel,
        out_shape=[jax.ShapeDtypeStruct(shape, dtype) for shape, dtype in outs],
        scratch_shapes=[
            pltpu.VMEM((GROUPS, panes, SLOT, local), bf16),
            pltpu.VMEM((panes, SLOT, GROUPS * 3 * local), bf16),
            pltpu.VMEM((8, GROUPS * local), f32),
        ],
        compiler_params=pltpu.CompilerParams(vmem_limit_bytes=60 * 1024 * 1024),
        name="attn_bwd",
    )(grad, own, recv, h1, vec, *weights, q, k, v, prob, pick)


def attn_grads(a, d_proj, mixed, dh_b):
    width = a.shape[1]
    local = mixed.shape[1] // GROUPS

    def kernel(a_ref, dp_ref, m_ref, g_ref, o0, o1):
        for g, out in enumerate((o0, o1)):
            out[:, : 3 * local] = dot(
                a_ref[...], dp_ref[:, g * 3 * local : (g + 1) * 3 * local], 0, 0
            ).astype(bf16)
            out[:, 3 * local :] = dot(
                g_ref[...], m_ref[:, g * local : (g + 1) * local], 0, 0
            ).astype(bf16)

    return call(kernel, [((width, 4 * local), bf16)] * 2, "attn_grads", a, d_proj, mixed, dh_b)


def tail(dh1, own, recv, hidden, vec):
    rows, width = dh1.shape

    def kernel(d_ref, own_ref, recv_ref, h_ref, vec_ref, o_ref, sum_ref):
        normed, inverse = unit_norm(h_ref[...])
        upstream = own_ref[...].astype(f32) + recv_ref[...].astype(f32)
        first_grad, d_gain, d_off = norm_back(upstream, normed, inverse, vec_ref[0:1, :])
        o_ref[...] = d_ref[...] + first_grad
        sum_ref[...] = jnp.zeros_like(sum_ref)
        sum_ref[1:2, :] = d_gain
        sum_ref[2:3, :] = d_off

    return call(kernel, [((rows, width), f32), ((8, width), f32)], "tail", dh1, own, recv, hidden, vec)


def place(blocks, index):
    rows, cols = blocks[0].shape
    count = len(blocks)

    def kernel(index_ref, *refs):
        out = refs[-1]
        for s in range(count):
            start = pl.multiple_of((index_ref[0] ^ s) * rows, rows)
            out[pl.ds(start, rows), :] = refs[s][...]

    return pl.pallas_call(
        kernel,
        in_specs=[pl.BlockSpec(memory_space=pltpu.SMEM)]
        + [pl.BlockSpec(memory_space=pltpu.VMEM)] * count,
        out_shape=jax.ShapeDtypeStruct((rows * count, cols), blocks[0].dtype),
        name="place",
    )(index, *blocks)


def adam_update(weight, gradient, moment_one, second, decay_on):
    first_new = beta_one * moment_one + (1.0 - beta_one) * gradient
    second_new = beta_two * second + (1.0 - beta_two) * gradient * gradient
    first_hat = first_new / (1.0 - beta_one**STEP)
    second_hat = second_new / (1.0 - beta_two**STEP)
    updated = weight - learn_rate * (
        first_hat / (jnp.sqrt(second_hat) + adam_eps) + decay_on * weight
    )
    return (updated, first_new, second_new)


def tree(parts):
    while len(parts) > 1:
        parts = [parts[i] + parts[i + 1] for i in range(0, len(parts), 2)]
    return parts[0]


def body(n_dp, *args):
    (tokens, cotangent, counts), params = args[:3], list(args[3:12])
    first_moments, second_moments = list(args[12:21]), list(args[21:30])
    inwards, inbias, relative, outwards, widening, widebias, narrowing, gains, offsets = params
    layer_total = inwards.shape[0]
    slots, cells, width = tokens.shape
    images = slots // 2
    rows = images * cells
    local = inwards.shape[3]
    hidden_local = widening.shape[2]
    heads = local // HEAD_DIM
    slab = width // n_dp
    direct = n_dp <= DIRECT_MAX and n_dp & (n_dp - 1) == 0
    dp_index = lax.axis_index("dp")
    c_index = lax.axis_index("c")

    def swap(x, axis):
        return lax.ppermute(x, axis, [(0, 1), (1, 0)])

    def xor_dp(x, s):
        return lax.ppermute(x, "dp", [(i, i ^ s) for i in range(n_dp)])

    def gather_all(pieces):
        if not direct:
            return [lax.all_gather(p, "dp", axis=0, tiled=True) for p in pieces]
        index = dp_index.astype(jnp.int32).reshape(1)
        got = [[p] for p in pieces]
        for j, p in enumerate(pieces):
            for s in range(1, n_dp):
                got[j].append(xor_dp(p, s))
        return [place(blocks, index) for blocks in got]

    def scatter_sum(own, recv):
        if not direct:
            total = (own.astype(f32) + recv.astype(f32)).astype(bf16)
            return lax.psum_scatter(total, "dp", scatter_dimension=0, tiled=True).astype(f32)
        parts = []
        for s in range(n_dp):
            start = (dp_index ^ s) * slab
            piece = lax.dynamic_slice_in_dim(own, start, slab, 0).astype(
                f32
            ) + lax.dynamic_slice_in_dim(recv, start, slab, 0).astype(f32)
            parts.append(piece if s == 0 else xor_dp(piece.astype(bf16), s).astype(f32))
        return tree(parts)

    def sum_dp(x):
        if not direct:
            return lax.psum(x, "dp")
        return tree([x if s == 0 else xor_dp(x, s) for s in range(n_dp)])

    shards_a = [
        jnp.concatenate(
            [inwards[l, 0], inwards[l, 1], inwards[l, 2], outwards[l].T], axis=1
        ).astype(bf16)
        for l in range(layer_total)
    ]
    shards_b = [
        jnp.concatenate([widening[l], narrowing[l].T], axis=1).astype(bf16)
        for l in range(layer_total)
    ]
    shards = [s for pair in zip(shards_a, shards_b) for s in pair]
    whole = gather_all(shards)
    weights_a = [(whole[2 * l], swap(whole[2 * l], "c")) for l in range(layer_total)]
    weights_b = [(whole[2 * l + 1], swap(whole[2 * l + 1], "c")) for l in range(layer_total)]

    sizes = [inbias[0].size, relative[0].size, widebias[0].size]
    packed = jnp.concatenate(
        [v for l in range(layer_total) for v in (inbias[l].ravel(), relative[l].ravel(), widebias[l])]
    ).reshape(-1, 4)
    other = swap(packed, "c").reshape(-1)
    packed = packed.reshape(-1)
    lookup = jnp.asarray(lookup_onehot())
    bias_qv, pos, wide_bias = [], [], []
    for l in range(layer_total):
        mask = pane_mask(l % 2 == 1)
        qv, tables, wides = [], [], []
        for source in (packed, other):
            at = l * sum(sizes)
            qv.append(source[at : at + sizes[0]].reshape(2, local))
            tables.append(source[at + sizes[0] : at + sizes[0] + sizes[1]].reshape(-1, heads))
            wides.append(source[at + sizes[0] + sizes[1] : at + sum(sizes)])
        bias_qv.append(jnp.concatenate(qv, axis=1))
        wide_bias.append(jnp.stack(wides))
        table = jnp.concatenate(tables, axis=1)
        spread_bias = jnp.dot(table.T, lookup, precision=lax.Precision.HIGHEST).reshape(
            GROUPS, heads, SLOT, SLOT
        )
        full = spread_bias[None] + jnp.asarray(mask)[:, None, None]
        pos.append(full.reshape(mask.shape[0], GROUPS, heads * SLOT, SLOT))
    picks = [
        jnp.asarray(selection(l % 2 == 1, images), dtype=bf16) for l in range(min(layer_total, 2))
    ]

    mine = lax.dynamic_slice_in_dim(tokens, c_index * images, images, 0).reshape(rows, width)
    cot = lax.dynamic_slice_in_dim(cotangent, c_index * images, images, 0).reshape(rows, width)
    keep = (c_index * images + jnp.arange(images) < counts[0]).astype(f32)
    keep = jnp.repeat(keep, cells).reshape(rows, 1)

    def vec_of(*vectors):
        stack = list(vectors) + [jnp.zeros((width,), f32)] * (8 - len(vectors))
        return jnp.stack(stack)

    saved = []
    source = (mine,)
    for l in range(layer_total):
        vec = vec_of(gains[l, 0], offsets[l, 0], offsets[l - 1, 3])
        hidden, a, q, k, v, prob, mixed, part = attn_fwd(
            l == 0, vec, source, weights_a[l], bias_qv[l], pos[l], picks[l % 2]
        )
        recv = swap(part, "y")
        vec = vec_of(gains[l, 1], offsets[l, 1], offsets[l, 2])
        h1, c, z, slope, part_mlp = mlp_fwd(hidden, part, recv, vec, weights_b[l], wide_bias[l])
        source = (h1, part_mlp, swap(part_mlp, "y"))
        saved.append((hidden, a, q, k, v, prob, mixed, h1, c, z, slope))

    back = (cot,) + source + (keep,)
    sums_mlp, sums_attn, score_sums = [None] * layer_total, [None] * layer_total, [None] * layer_total
    grads_a, grads_b = [None] * layer_total, [None] * layer_total
    sums_tail = [None] * layer_total
    for l in reversed(range(layer_total)):
        hidden, a, q, k, v, prob, mixed, h1, c, z, slope = saved[l]
        last = l == layer_total - 1
        vec = vec_of(offsets[l, 3] if last else gains[l + 1, 0])
        res = mlp_bwd(last, back, vec, slope, weights_b[l])
        grad, grad_b, du_b, part, sums_mlp[l] = res[:5]
        if last:
            out_mine = res[5]
        else:
            sums_tail[l + 1] = sums_mlp[l]
        recv = swap(part, "y")
        own_g, other_g = mlp_grads(c, du_b, z, grad_b)
        grads_b[l] = scatter_sum(own_g, swap(other_g, "c"))
        dh1, dh_b, d_proj, part_in, sums_attn[l], score_sums[l] = attn_bwd(
            grad, part, recv, h1, vec_of(gains[l, 1]), weights_a[l], q, k, v, prob, picks[l % 2]
        )
        back = (dh1, part_in, swap(part_in, "y"), hidden)
        own_g, other_g = attn_grads(a, d_proj, mixed, dh_b)
        grads_a[l] = scatter_sum(own_g, swap(other_g, "c"))
    grad_mine, sums_tail[0] = tail(*back, vec_of(gains[0, 0]))

    def both_halves(x):
        recv = swap(x, "c")
        lower = c_index == 0
        return jnp.concatenate(
            [jnp.where(lower, x, recv), jnp.where(lower, recv, x)], axis=0
        ).reshape(slots, cells, width)

    output = both_halves(out_mine)
    grad_tokens = both_halves(grad_mine)

    own_small, other_small, shared = [], [], []
    for l in range(layer_total):
        tables = jnp.dot(
            lookup,
            score_sums[l].reshape(GROUPS * heads, SLOT * SLOT).T,
            precision=lax.Precision.HIGHEST,
        )
        for g, target in ((0, own_small), (1, other_small)):
            cols = slice(g * local, (g + 1) * local)
            target.append(sums_attn[l][3, cols])
            target.append(sums_attn[l][4, cols])
            target.append(tables[:, g * heads : (g + 1) * heads].ravel())
            target.append(sums_mlp[l][3 + g, :hidden_local])
        shared.append(
            jnp.concatenate(
                [
                    sums_tail[l][1, :width],
                    sums_attn[l][0],
                    sums_tail[l][2, :width],
                    sums_attn[l][1],
                    sums_attn[l][2],
                    sums_mlp[l][0, :width],
                ]
            )
        )
    own_vec = jnp.concatenate(own_small + shared)
    other_vec = jnp.concatenate(other_small + shared)
    pad = -own_vec.size % 1024
    own_vec = jnp.pad(own_vec, (0, pad)).reshape(-1, 128)
    other_vec = jnp.pad(other_vec, (0, pad)).reshape(-1, 128)
    total = sum_dp(own_vec + swap(other_vec, "c")).reshape(-1)
    step = sum(sizes)
    d_inbias = jnp.stack([total[l * step :][: sizes[0]].reshape(2, local) for l in range(layer_total)])
    d_relative = jnp.stack(
        [total[l * step + sizes[0] :][: sizes[1]].reshape(-1, heads) for l in range(layer_total)]
    )
    d_widebias = jnp.stack(
        [total[l * step + sizes[0] + sizes[1] :][: sizes[2]] for l in range(layer_total)]
    )
    at = layer_total * step
    rest = total[at : at + layer_total * 6 * width].reshape(layer_total, 6, width)
    d_gains, d_offsets = rest[:, :2], rest[:, 2:]

    d_inwards = jnp.stack(
        [
            jnp.stack([grads_a[l][:, j * local : (j + 1) * local] for j in range(3)])
            for l in range(layer_total)
        ]
    )
    d_outwards = jnp.stack([grads_a[l][:, 3 * local :].T for l in range(layer_total)])
    d_widening = jnp.stack([grads_b[l][:, :hidden_local] for l in range(layer_total)])
    d_narrowing = jnp.stack([grads_b[l][:, hidden_local:].T for l in range(layer_total)])
    totals = [
        d_inwards,
        d_inbias,
        d_relative,
        d_outwards,
        d_widening,
        d_widebias,
        d_narrowing,
        d_gains,
        d_offsets,
    ]
    decays = [decay_rate, 0.0, 0.0, decay_rate, decay_rate, 0.0, decay_rate, 0.0, 0.0]
    results = [
        adam_update(params[m], totals[m], first_moments[m], second_moments[m], decays[m])
        for m in range(len(params))
    ]
    return (
        output,
        grad_tokens,
        *totals,
        *[r[0] for r in results],
        *[r[1] for r in results],
        *[r[2] for r in results],
    )


def solution(mesh):
    n_dp, n_mp = mesh.shape["dp"], mesh.shape["mp"]
    inner = Mesh(mesh.devices.reshape(n_dp, n_mp // 2, 2), ("dp", "y", "c"))
    mp = ("y", "c")
    batch = P("dp", None, None)
    member_specs = (
        P(None, None, "dp", mp),
        P(None, None, mp),
        P(None, None, mp),
        P(None, mp, "dp"),
        P(None, "dp", mp),
        P(None, mp),
        P(None, mp, "dp"),
        P(),
        P(),
    )
    in_specs = (batch, batch, P("dp")) + member_specs * 3
    out_specs = (batch, batch) + member_specs * 4
    return jax.shard_map(
        functools.partial(body, n_dp),
        mesh=inner,
        in_specs=in_specs,
        out_specs=out_specs,
        check_vma=False,
    )
```

```python
import jax
import jax.numpy as jnp
import numpy as np
from jax import lax
from jax.experimental import pallas as pl
from jax.experimental.pallas import tpu as pltpu
from jax.sharding import Mesh
from jax.sharding import PartitionSpec as P


HEAD_DIM = 32
WIN = 7
SIDE = 14
SHIFT = 3
STEP = 3

norm_eps = 1e-05
beta_one = 0.9
beta_two = 0.999
learn_rate = 0.02
decay_rate = 0.05
adam_eps = 1e-08

CELLS = WIN * WIN
PANES = (SIDE // WIN) ** 2
SLOT = 64
GROUPS = 2
DIRECT_MAX = 8
UNROLL = 2
ROWS = -(-SIDE * SIDE // 8) * 8
VMEM_BYTES = 60 * 1024 * 1024
f32 = jnp.float32
bf16 = jnp.bfloat16


def window_order(shifted):
    grid = np.arange(SIDE * SIDE).reshape(SIDE, SIDE)
    if shifted:
        grid = np.roll(grid, (-SHIFT, -SHIFT), axis=(0, 1))
    side_panes = SIDE // WIN
    return grid.reshape(side_panes, WIN, side_panes, WIN).transpose(0, 2, 1, 3).reshape(-1, CELLS)


def selection(shifted, images):
    source = np.full((images, PANES, SLOT), -1, np.int32)
    for i in range(images):
        source[i, :, :CELLS] = window_order(shifted) + i * ROWS
    wanted = jnp.asarray(source.reshape(-1, 1))
    return (wanted == jnp.arange(images * ROWS, dtype=jnp.int32)[None, :]).astype(bf16)


def lookup_onehot():
    places = np.arange(CELLS)
    rowpos, colpos = places // WIN, places % WIN
    lookup = (rowpos[:, None] - rowpos[None, :] + WIN - 1) * (2 * WIN - 1) + (
        colpos[:, None] - colpos[None, :] + WIN - 1
    )
    full = np.full((SLOT, SLOT), -1, np.int32)
    full[:CELLS, :CELLS] = lookup
    entries = jnp.arange((2 * WIN - 1) ** 2, dtype=jnp.int32)
    return (entries[:, None] == jnp.asarray(full.reshape(1, -1))).astype(f32)


def pane_mask(shifted):
    pad = np.zeros((SLOT, SLOT), np.float32)
    pad[:, CELLS:] = -1e30
    if not shifted:
        return pad[None]
    coords = np.arange(SIDE)
    stripe = (coords >= SIDE - WIN).astype(int) + (coords >= SIDE - SHIFT).astype(int)
    region = (stripe[:, None] * 3 + stripe[None, :]).reshape(-1)
    side_panes = SIDE // WIN
    per = region.reshape(side_panes, WIN, side_panes, WIN).transpose(0, 2, 1, 3).reshape(-1, CELLS)
    out = np.repeat(pad[None], PANES, axis=0)
    out[:, :CELLS, :CELLS] = np.where(per[:, :, None] != per[:, None, :], -100.0, 0.0)
    return out


def dot(left, right, lc, rc):
    return lax.dot_general(left, right, (((lc,), (rc,)), ((), ())), preferred_element_type=f32)


def unit_norm(hidden):
    centered = hidden - jnp.mean(hidden, axis=-1, keepdims=True)
    inverse = lax.rsqrt(jnp.mean(centered * centered, axis=-1, keepdims=True) + norm_eps)
    return centered * inverse, inverse


def norm_back(upstream, normed, inverse, gain):
    d_normed = upstream * gain
    source = inverse * (
        d_normed
        - jnp.mean(d_normed, axis=-1, keepdims=True)
        - normed * jnp.mean(d_normed * normed, axis=-1, keepdims=True)
    )
    return source, jnp.sum(upstream * normed, axis=0, keepdims=True), jnp.sum(
        upstream, axis=0, keepdims=True
    )


def head_masks(width):
    lane = lax.broadcasted_iota(jnp.int32, (1, width), 1) // HEAD_DIM
    return [lane == head for head in range(width // HEAD_DIM)]


def spread(value, masks):
    zero = jnp.zeros_like(value)
    return jnp.concatenate([jnp.where(mask, value, zero) for mask in masks], axis=0)


def gather_heads(stacked, masks):
    total = None
    for head, mask in enumerate(masks):
        part = jnp.where(mask, stacked[head * SLOT : (head + 1) * SLOT], 0.0)
        total = part if total is None else total + part
    return total


def call(kernel, outs, *args, scratch=(), scalars=0):
    specs = [pl.BlockSpec(memory_space=pltpu.SMEM)] * scalars
    specs += [pl.BlockSpec(memory_space=pltpu.VMEM)] * (len(args) - scalars)
    return pl.pallas_call(
        kernel,
        in_specs=specs,
        out_shape=[jax.ShapeDtypeStruct(shape, dtype) for shape, dtype in outs],
        scratch_shapes=[pltpu.VMEM(shape, dtype) for shape, dtype in scratch],
        compiler_params=pltpu.CompilerParams(vmem_limit_bytes=VMEM_BYTES),
    )(*args)


def load_images(place_ref, images_ref, buffer, images):
    cells, width = images_ref.shape[1:]
    for i in range(images):
        buffer[i * ROWS : i * ROWS + cells, :] = images_ref[place_ref[0] * images + i]
        buffer[i * ROWS + cells : (i + 1) * ROWS, :] = jnp.zeros((ROWS - cells, width), f32)


def store_images(value, out, images):
    cells = out.shape[1]
    for i in range(images):
        out[i] = value[i * ROWS : i * ROWS + cells, :]


def attn_fwd(layer, gains, offsets, source, weights, bias_qv, pos, pick):
    first = layer == 0
    win_rows, rows = pick.shape
    width = weights[0].shape[0]
    panes = win_rows // SLOT
    local = weights[0].shape[1] // 4
    heads = local // HEAD_DIM
    masks_n = pos.shape[0]
    factor = HEAD_DIM ** (-0.5)
    n_src = len(source)

    def kernel(*refs):
        src = refs[:n_src]
        gain_ref, off_ref, w0, w1, bias_ref, pos_ref, pick_ref = refs[n_src : n_src + 7]
        h_ref, a_ref, q_ref, k_ref, v_ref, prob_ref, mixed_ref, part_ref, mw_ref = refs[n_src + 7 :]
        if first:
            load_images(src[0], src[1], h_ref, rows // ROWS)
            hidden = h_ref[...]
        else:
            hidden = src[0][...] + (
                src[1][...].astype(f32) + src[2][...].astype(f32) + off_ref[layer - 1, 3:4]
            )
            h_ref[...] = hidden
        normed, _ = unit_norm(hidden)
        a = (normed * gain_ref[layer, 0:1] + off_ref[layer, 0:1]).astype(bf16)
        a_ref[...] = a
        a_win = dot(pick_ref[...], a, 1, 0).astype(bf16)
        for g, w in enumerate((w0, w1)):
            proj = dot(a_win, w[:, : 3 * local], 1, 0)
            q = ((proj[:, :local] + bias_ref[0:1, g * local : (g + 1) * local]) * factor).astype(bf16)
            k = proj[:, local : 2 * local].astype(bf16)
            v = (proj[:, 2 * local :] + bias_ref[1:2, g * local : (g + 1) * local]).astype(bf16)
            q_ref[g] = q.reshape(panes, SLOT, local)
            k_ref[g] = k.reshape(panes, SLOT, local)
            v_ref[g] = v.reshape(panes, SLOT, local)
        masks = head_masks(local)

        def step(w, carry):
            for g in range(GROUPS):
                q, k, v = q_ref[g, w], k_ref[g, w], v_ref[g, w]
                score = dot(spread(q, masks), k, 1, 1) + pos_ref[w % masks_n if masks_n > 1 else 0, g]
                top = jnp.max(score, axis=-1, keepdims=True)
                grown = jnp.exp(score - top)
                prob = grown * (1.0 / jnp.sum(grown, axis=-1, keepdims=True))
                prob_ref[w, g] = prob
                mixed = gather_heads(dot(prob.astype(bf16), v, 1, 0), masks)
                mw_ref[w, :, g * local : (g + 1) * local] = mixed.astype(bf16)
            return carry

        lax.fori_loop(0, panes, step, 0, unroll=UNROLL)
        mixed = dot(pick_ref[...], mw_ref[...].reshape(win_rows, GROUPS * local), 0, 0).astype(bf16)
        mixed_ref[...] = mixed
        part = None
        for g, w in enumerate((w0, w1)):
            term = dot(mixed[:, g * local : (g + 1) * local], w[:, 3 * local :], 1, 1)
            part = term if part is None else part + term
        part_ref[...] = part.astype(bf16)

    outs = [
        ((rows, width), f32),
        ((rows, width), bf16),
        ((GROUPS, panes, SLOT, local), bf16),
        ((GROUPS, panes, SLOT, local), bf16),
        ((GROUPS, panes, SLOT, local), bf16),
        ((panes, GROUPS, heads * SLOT, SLOT), f32),
        ((rows, GROUPS * local), bf16),
        ((rows, width), bf16),
    ]
    return call(
        kernel,
        outs,
        *source,
        gains,
        offsets,
        *weights,
        bias_qv,
        pos,
        pick,
        scratch=[((panes, SLOT, GROUPS * local), bf16)],
        scalars=1 if first else 0,
    )


def mlp_fwd(layer, hidden, own, recv, gains, offsets, weights, wide_bias):
    rows, width = hidden.shape
    local = weights[0].shape[1] // 2

    def kernel(
        h_ref, own_ref, recv_ref, gain_ref, off_ref, w0, w1, wb_ref, h1_ref, c_ref, z_ref, s_ref, p_ref
    ):
        h1 = h_ref[...] + (own_ref[...].astype(f32) + recv_ref[...].astype(f32) + off_ref[layer, 2:3])
        h1_ref[...] = h1
        normed, _ = unit_norm(h1)
        c = (normed * gain_ref[layer, 1:2] + off_ref[layer, 1:2]).astype(bf16)
        c_ref[...] = c
        part = None
        for g, w in enumerate((w0, w1)):
            u = dot(c, w[:, :local], 1, 0) + wb_ref[g : g + 1, :]
            cdf = 0.5 * (1.0 + lax.erf(u * 0.7071067811865476))
            density = jnp.exp(-0.5 * u * u) * 0.3989422804014327
            z = (u * cdf).astype(bf16)
            z_ref[:, g * local : (g + 1) * local] = z
            s_ref[:, g * local : (g + 1) * local] = (cdf + u * density).astype(bf16)
            term = dot(z, w[:, local:], 1, 1)
            part = term if part is None else part + term
        p_ref[...] = part.astype(bf16)

    outs = [
        ((rows, width), f32),
        ((rows, width), bf16),
        ((rows, GROUPS * local), bf16),
        ((rows, GROUPS * local), bf16),
        ((rows, width), bf16),
    ]
    return call(kernel, outs, hidden, own, recv, gains, offsets, *weights, wide_bias)


def mlp_bwd(layer, last, source, gains, offsets, slope, weights):
    rows, width = source[3].shape
    local = weights[0].shape[1] // 2
    n_src = len(source)

    def kernel(*refs):
        src = refs[:n_src]
        gain_ref, off_ref, s_ref, w0, w1 = refs[n_src : n_src + 5]
        g_ref, gb_ref, du_ref, p_ref, sum_ref = refs[n_src + 5 : n_src + 10]
        sum_ref[...] = jnp.zeros_like(sum_ref)
        if last:
            place_ref, count_ref = src[:2]
            images = rows // ROWS
            load_images(place_ref, src[2], g_ref, images)
            result = src[3][...] + (src[4][...].astype(f32) + src[5][...].astype(f32) + off_ref[layer, 3:4])
            out_ref = refs[n_src + 10]
            cells = out_ref.shape[1]
            for i in range(images):
                keep = jnp.where(place_ref[0] * images + i < count_ref[0], 1.0, 0.0)
                out_ref[i] = result[i * ROWS : i * ROWS + cells, :] * keep
                g_ref[i * ROWS : (i + 1) * ROWS, :] = g_ref[i * ROWS : (i + 1) * ROWS, :] * keep
            grad = g_ref[...]
        else:
            normed, inverse = unit_norm(src[3][...])
            upstream = src[1][...].astype(f32) + src[2][...].astype(f32)
            first_grad, d_gain, d_off = norm_back(
                upstream, normed, inverse, gain_ref[layer + 1, 0:1]
            )
            grad = src[0][...] + first_grad
            sum_ref[1:2, :] = d_gain
            sum_ref[2:3, :] = d_off
            g_ref[...] = grad
        sum_ref[0:1, :] = jnp.sum(grad, axis=0, keepdims=True)
        grad_b = grad.astype(bf16)
        gb_ref[...] = grad_b
        part = None
        for g, w in enumerate((w0, w1)):
            du = dot(grad_b, w[:, local:], 1, 0) * s_ref[:, g * local : (g + 1) * local].astype(f32)
            sum_ref[3 + g : 4 + g, :local] = jnp.sum(du, axis=0, keepdims=True)
            du_b = du.astype(bf16)
            du_ref[:, g * local : (g + 1) * local] = du_b
            term = dot(du_b, w[:, :local], 1, 1)
            part = term if part is None else part + term
        p_ref[...] = part.astype(bf16)

    outs = [
        ((rows, width), f32),
        ((rows, width), bf16),
        ((rows, GROUPS * local), bf16),
        ((rows, width), bf16),
        ((8, width), f32),
    ]
    if last:
        outs.append(((rows // ROWS, source[2].shape[1], width), f32))
    return call(kernel, outs, *source, gains, offsets, slope, *weights, scalars=2 if last else 0)


def grad_outs(width, cols, halves):
    if not halves:
        return [((width, cols), bf16)] * 2
    half = width // halves
    return [((half, cols), bf16), ((half, cols), bf16), ((halves, half, cols), bf16)]


def cut(full, outs, place_ref, halves, slab):
    if not halves:
        outs[0][...] = full[...]
        return
    deep = full.shape[0] // (halves * slab)
    for x in range(halves):
        for z in range(deep):
            block = (z ^ place_ref[1]) * halves + (x ^ place_ref[2])
            start = pl.multiple_of(block * slab, slab)
            target = outs[x] if len(outs) > 1 else outs[0].at[x]
            target[z * slab : (z + 1) * slab, :] = full[pl.ds(start, slab), :]


def mlp_grads(place, c, du_b, z, grad_b, halves, slab):
    width = c.shape[1]
    local = z.shape[1] // GROUPS

    def kernel(place_ref, c_ref, du_ref, z_ref, g_ref, *outs):
        full = outs[-1]
        for g, out in enumerate((outs[:-2], outs[-2:-1])):
            cols = slice(g * local, (g + 1) * local)
            full[:, :local] = dot(c_ref[...], du_ref[:, cols], 0, 0).astype(bf16)
            full[:, local:] = dot(g_ref[...], z_ref[:, cols], 0, 0).astype(bf16)
            cut(full, out, place_ref, halves, slab)

    return call(
        kernel,
        grad_outs(width, 2 * local, halves),
        place,
        c,
        du_b,
        z,
        grad_b,
        scratch=[((width, 2 * local), bf16)],
        scalars=1,
    )


def attn_bwd(layer, grad, own, recv, h1, gains, weights, q, k, v, prob, pick):
    rows, width = grad.shape
    win_rows = pick.shape[0]
    panes = win_rows // SLOT
    local = weights[0].shape[1] // 4
    heads = local // HEAD_DIM
    factor = HEAD_DIM ** (-0.5)

    def kernel(
        g_ref, own_ref, recv_ref, h1_ref, gain_ref, w0, w1, q_ref, k_ref, v_ref, prob_ref, pick_ref,
        dh_ref, dhb_ref, dp_ref, part_ref, sum_ref, ds_ref, dm_ref, dw_ref, bias_ref,
    ):
        normed, inverse = unit_norm(h1_ref[...])
        upstream = own_ref[...].astype(f32) + recv_ref[...].astype(f32)
        d_mid, d_gain, d_off = norm_back(upstream, normed, inverse, gain_ref[layer, 1:2])
        dh1 = g_ref[...] + d_mid
        dh_ref[...] = dh1
        sum_ref[...] = jnp.zeros_like(sum_ref)
        sum_ref[0:1, :] = d_gain
        sum_ref[1:2, :] = d_off
        sum_ref[2:3, :] = jnp.sum(dh1, axis=0, keepdims=True)
        dh_b = dh1.astype(bf16)
        dhb_ref[...] = dh_b
        for g, w in enumerate((w0, w1)):
            d_mixed = dot(dh_b, w[:, 3 * local :], 1, 0).astype(bf16)
            d_win = dot(pick_ref[...], d_mixed, 1, 0).astype(bf16)
            dm_ref[g] = d_win.reshape(panes, SLOT, local)
        ds_ref[...] = jnp.zeros_like(ds_ref)
        bias_ref[...] = jnp.zeros_like(bias_ref)
        masks = head_masks(local)

        def step(w, carry):
            for g in range(GROUPS):
                keys, values = k_ref[g, w], v_ref[g, w]
                d_out = spread(dm_ref[g, w], masks)
                queries = spread(q_ref[g, w], masks)
                probs = prob_ref[w, g]
                d_prob = dot(d_out, values, 1, 1)
                d_value = dot(probs.astype(bf16), d_out, 0, 0)
                d_score = probs * (d_prob - jnp.sum(probs * d_prob, axis=-1, keepdims=True))
                ds_ref[g] += d_score
                d_score_b = d_score.astype(bf16)
                d_query = gather_heads(dot(d_score_b, keys, 1, 0), masks) * factor
                d_key = dot(d_score_b, queries, 0, 0)
                base = g * 3 * local
                dw_ref[w, :, base : base + local] = d_query.astype(bf16)
                dw_ref[w, :, base + local : base + 2 * local] = d_key.astype(bf16)
                dw_ref[w, :, base + 2 * local : base + 3 * local] = d_value.astype(bf16)
                bias_ref[0:1, g * local : (g + 1) * local] += jnp.sum(d_query, axis=0, keepdims=True)
                bias_ref[1:2, g * local : (g + 1) * local] += jnp.sum(d_value, axis=0, keepdims=True)
            return carry

        lax.fori_loop(0, panes, step, 0, unroll=UNROLL)
        sum_ref[3:4, : GROUPS * local] = bias_ref[0:1, :]
        sum_ref[4:5, : GROUPS * local] = bias_ref[1:2, :]
        d_proj = dot(
            pick_ref[...], dw_ref[...].reshape(win_rows, GROUPS * 3 * local), 0, 0
        ).astype(bf16)
        dp_ref[...] = d_proj
        part = None
        for g, w in enumerate((w0, w1)):
            term = dot(d_proj[:, g * 3 * local : (g + 1) * 3 * local], w[:, : 3 * local], 1, 1)
            part = term if part is None else part + term
        part_ref[...] = part.astype(bf16)

    outs = [
        ((rows, width), f32),
        ((rows, width), bf16),
        ((rows, GROUPS * 3 * local), bf16),
        ((rows, width), bf16),
        ((8, width), f32),
        ((GROUPS, heads * SLOT, SLOT), f32),
    ]
    return call(
        kernel,
        outs,
        grad,
        own,
        recv,
        h1,
        gains,
        *weights,
        q,
        k,
        v,
        prob,
        pick,
        scratch=[
            ((GROUPS, panes, SLOT, local), bf16),
            ((panes, SLOT, GROUPS * 3 * local), bf16),
            ((8, GROUPS * local), f32),
        ],
    )


def attn_grads(place, a, d_proj, mixed, dh_b, halves, slab):
    width = a.shape[1]
    local = mixed.shape[1] // GROUPS

    def kernel(place_ref, a_ref, dp_ref, m_ref, g_ref, *outs):
        full = outs[-1]
        for g, out in enumerate((outs[:-2], outs[-2:-1])):
            full[:, : 3 * local] = dot(
                a_ref[...], dp_ref[:, g * 3 * local : (g + 1) * 3 * local], 0, 0
            ).astype(bf16)
            full[:, 3 * local :] = dot(
                g_ref[...], m_ref[:, g * local : (g + 1) * local], 0, 0
            ).astype(bf16)
            cut(full, out, place_ref, halves, slab)

    return call(
        kernel,
        grad_outs(width, 4 * local, halves),
        place,
        a,
        d_proj,
        mixed,
        dh_b,
        scratch=[((width, 4 * local), bf16)],
        scalars=1,
    )


def tail(dh1, own, recv, hidden, gains, cells):
    rows, width = dh1.shape
    images = rows // ROWS

    def kernel(d_ref, own_ref, recv_ref, h_ref, gain_ref, o_ref, sum_ref):
        normed, inverse = unit_norm(h_ref[...])
        upstream = own_ref[...].astype(f32) + recv_ref[...].astype(f32)
        first_grad, d_gain, d_off = norm_back(upstream, normed, inverse, gain_ref[0, 0:1])
        store_images(d_ref[...] + first_grad, o_ref, images)
        sum_ref[...] = jnp.zeros_like(sum_ref)
        sum_ref[1:2, :] = d_gain
        sum_ref[2:3, :] = d_off

    outs = [((images, cells, width), f32), ((8, width), f32)]
    return call(kernel, outs, dh1, own, recv, hidden, gains)


def order(blocks, place, member):
    rows, cols = blocks[0].shape

    def kernel(place_ref, *refs):
        out = refs[-1]
        for s in range(len(blocks)):
            start = pl.multiple_of((place_ref[member] ^ s) * rows, rows)
            out[pl.ds(start, rows), :] = refs[s][...]

    outs = [((rows * len(blocks), cols), blocks[0].dtype)]
    return call(kernel, outs, place, *blocks, scalars=1)[0]


def pack(inwards, outwards, widening, narrowing):
    layers, _, slab, local = inwards.shape
    hidden = widening.shape[2]

    def kernel(in_ref, out_ref, wide_ref, narrow_ref, *packed):
        for l in range(layers):
            part_a, part_b = packed[2 * l : 2 * l + 2]
            for j in range(3):
                part_a[:, j * local : (j + 1) * local] = in_ref[l, j].astype(bf16)
            part_a[:, 3 * local :] = out_ref[l].astype(bf16)
            part_b[:, :hidden] = wide_ref[l].astype(bf16)
            part_b[:, hidden:] = narrow_ref[l].astype(bf16)

    outs = [((slab, 4 * local), bf16), ((slab, 2 * hidden), bf16)] * layers
    return call(kernel, outs, inwards, outwards, widening, narrowing)


def adam_pair(parts, first, second, turned):
    layers = len(parts)
    counts = [len(p) for p in parts]
    flat = [p for layer in parts for p in layer]
    stacked = first[0].ndim == 4

    def kernel(*refs):
        blocks, rest = refs[: len(flat)], refs[len(flat) :]
        one, two, out_one, out_two = rest[:3], rest[3:6], rest[6:10], rest[10:14]
        at = 0

        def update(index, gradient, ins, outs):
            weight, mean, square = (r[index] for r in ins)
            new = adam_update(weight, gradient, mean, square, decay_rate)
            outs[0][index] = gradient
            for ref, value in zip(outs[1:], new):
                ref[index] = value

        for l in range(layers):
            terms = [blocks[at + i][...].astype(f32) for i in range(counts[l])]
            at += counts[l]
            total = tree(terms)
            split = total.shape[1] - turned
            if stacked:
                piece = split // one[0].shape[1]
                for j in range(one[0].shape[1]):
                    update((l, j), total[:, j * piece : (j + 1) * piece], one, out_one)
            else:
                update((l,), total[:, :split], one, out_one)
            update((l,), total[:, split:], two, out_two)

    outs = [(first[0].shape, f32)] * 4 + [(second[0].shape, f32)] * 4
    res = call(kernel, outs, *flat, *first, *second)
    return res[:4], res[4:]


def small_rows(layers, heads):
    per = 8 + heads
    return per, -(-layers * per // 8) * 8


def small_pack(sums_mlp, sums_attn, sums_tail, tables, local):
    layers = len(tables)
    heads = tables[0].shape[0] // GROUPS
    entries = tables[0].shape[1]
    width = sums_mlp[0].shape[1]
    per, rows = small_rows(layers, heads)

    def kernel(*refs):
        ins, outs = refs[:-GROUPS], refs[-GROUPS:]
        for g, out in enumerate(outs):
            out[...] = jnp.zeros_like(out)
            for l in range(layers):
                mlp, attn, late, table = ins[4 * l : 4 * l + 4]
                base = l * per
                out[base : base + 1, :] = late[1:2, :]
                out[base + 1 : base + 2, :] = attn[0:1, :]
                out[base + 2 : base + 3, :] = late[2:3, :]
                out[base + 3 : base + 4, :] = attn[1:2, :]
                out[base + 4 : base + 5, :] = attn[2:3, :]
                out[base + 5 : base + 6, :] = mlp[0:1, :]
                out[base + 6 : base + 7, :] = mlp[3 + g : 4 + g, :]
                out[base + 7 : base + 8, :local] = attn[3:4, g * local : (g + 1) * local]
                out[base + 7 : base + 8, local : 2 * local] = attn[4:5, g * local : (g + 1) * local]
                out[base + 8 : base + 8 + heads, :entries] = table[g * heads : (g + 1) * heads, :]

    flat = [v for quad in zip(sums_mlp, sums_attn, sums_tail, tables) for v in quad]
    return call(kernel, [((rows, width), f32)] * GROUPS, *flat)


def small_adam(total, states):
    layers, _, local = states[0][0].shape
    heads, entries = states[1][0].shape[1:]
    hidden = states[2][0].shape[1]
    width = states[3][0].shape[2]
    per, _ = small_rows(layers, heads)

    def kernel(total_ref, *refs):
        ins, outs = refs[:15], refs[15:]

        def update(member, index, gradient):
            weight, mean, square = (r[index] for r in ins[3 * member : 3 * member + 3])
            new = (gradient,) + adam_update(weight, gradient, mean, square, 0.0)
            for ref, value in zip(outs[4 * member : 4 * member + 4], new):
                ref[index] = value

        for l in range(layers):
            base = l * per
            for row in range(2):
                update(
                    0,
                    (l, slice(row, row + 1)),
                    total_ref[base + 7 : base + 8, row * local : (row + 1) * local],
                )
            update(1, (l,), total_ref[base + 8 : base + 8 + heads, :entries])
            update(2, (slice(l, l + 1),), total_ref[base + 6 : base + 7, :hidden])
            update(3, (l,), total_ref[base : base + 2, :width])
            update(4, (l,), total_ref[base + 2 : base + 6, :width])

    outs = [(state[0].shape, f32) for state in states for _ in range(4)]
    res = call(kernel, outs, total, *[v for state in states for v in state])
    return [res[4 * m : 4 * m + 4] for m in range(5)]


def adam_update(weight, gradient, moment_one, second, decay_on):
    first_new = beta_one * moment_one + (1.0 - beta_one) * gradient
    second_new = beta_two * second + (1.0 - beta_two) * gradient * gradient
    first_hat = first_new / (1.0 - beta_one**STEP)
    second_hat = second_new / (1.0 - beta_two**STEP)
    updated = weight - learn_rate * (
        first_hat / (jnp.sqrt(second_hat) + adam_eps) + decay_on * weight
    )
    return (updated, first_new, second_new)


def turn(x):
    return jnp.swapaxes(x, 1, 2)


def tree(parts):
    while len(parts) > 1:
        parts = [parts[i] + parts[i + 1] for i in range(0, len(parts), 2)]
    return parts[0]


def step(*args):
    (tokens, cotangent, counts), params = args[:3], list(args[3:12])
    first_moments, second_moments = list(args[12:21]), list(args[21:30])
    inwards, inbias, relative, outwards, widening, widebias, narrowing, gains, offsets = params
    layer_total = inwards.shape[0]
    slots, cells, _ = tokens.shape
    images = slots // 2
    local = inwards.shape[3]
    hidden_local = widening.shape[2]
    heads = local // HEAD_DIM
    slab = inwards.shape[2]
    n_x = lax.axis_size("x")
    n_z = lax.axis_size("z")
    direct = n_x == 2 and n_x * n_z <= DIRECT_MAX and n_z & (n_z - 1) == 0
    halves = n_x if direct else 0
    c_index = lax.axis_index("c")
    place = jnp.stack(
        [
            c_index,
            lax.axis_index("z"),
            lax.axis_index("x"),
            lax.axis_index("z") * n_x + lax.axis_index("x"),
        ]
    ).astype(jnp.int32)
    dp = ("z", "x")

    def swap(x, axis):
        return lax.ppermute(x, axis, [(0, 1), (1, 0)])

    def xor_z(x, s):
        return lax.ppermute(x, "z", [(i, i ^ s) for i in range(n_z)])

    def xor_dp(x, s):
        return lax.ppermute(x, dp, [(i, i ^ s) for i in range(n_x * n_z)])

    def gather_now(p):
        if not direct:
            return lax.all_gather(p, dp, axis=0, tiled=True)
        blocks = [p] + [xor_dp(p, s) for s in range(1, n_x * n_z)]
        return order(blocks, place, 3)

    def gather_staged(p):
        if not direct:
            return lax.all_gather(p, dp, axis=0, tiled=True)
        away = swap(p, "x")
        pair = order([p, away], place, 2)
        blocks = [pair] + [xor_z(pair, s) for s in range(1, n_z)]
        return order(blocks, place, 1)

    def scatter_terms(own, other):
        recv = swap(other, "c")
        if not direct:
            total = (own[0].astype(f32) + recv.astype(f32)).astype(bf16)
            return [lax.psum_scatter(total, dp, scatter_dimension=0, tiled=True)]
        away = (own[1].astype(f32) + recv[1].astype(f32)).astype(bf16)
        back = swap(away, "x")
        near = (own[0].astype(f32) + recv[0].astype(f32) + back.astype(f32)).astype(bf16)
        return [near[:slab]] + [xor_z(near[s * slab : (s + 1) * slab], s) for s in range(1, n_z)]

    def sum_dp(x):
        if not direct:
            return lax.psum(x, dp)
        x = x + swap(x, "x")
        return tree([x if s == 0 else xor_z(x, s) for s in range(n_z)])

    shards = pack(inwards, turn(outwards), widening, turn(narrowing))
    whole = []
    for i, shard in enumerate(shards):
        full = gather_staged(shard) if i else gather_now(shard)
        whole.append((full, swap(full, "c")))
    weights_a, weights_b = whole[0::2], whole[1::2]

    sizes = [inbias[0].size, relative[0].size, widebias[0].size]
    packed = jnp.concatenate(
        [v for l in range(layer_total) for v in (inbias[l].ravel(), relative[l].ravel(), widebias[l])]
    ).reshape(-1, 4)
    other = swap(packed, "c").reshape(-1)
    packed = packed.reshape(-1)
    lookup = lookup_onehot()
    bias_qv, pos, wide_bias = [], [], []
    for l in range(layer_total):
        mask = pane_mask(l % 2 == 1)
        qv, tables, wides = [], [], []
        for source in (packed, other):
            at = l * sum(sizes)
            qv.append(source[at : at + sizes[0]].reshape(2, local))
            tables.append(source[at + sizes[0] : at + sizes[0] + sizes[1]].reshape(-1, heads))
            wides.append(source[at + sizes[0] + sizes[1] : at + sum(sizes)])
        bias_qv.append(jnp.concatenate(qv, axis=1))
        wide_bias.append(jnp.stack(wides))
        table = jnp.concatenate(tables, axis=1)
        spread_bias = jnp.dot(table.T, lookup, precision=lax.Precision.HIGHEST).reshape(
            GROUPS, heads, SLOT, SLOT
        )
        full = spread_bias[None] + jnp.asarray(mask)[:, None, None]
        pos.append(full.reshape(mask.shape[0], GROUPS, heads * SLOT, SLOT))
    picks = [
        selection(l % 2 == 1, images) for l in range(min(layer_total, 2))
    ]

    saved = []
    source = (place, tokens)
    for l in range(layer_total):
        hidden, a, q, k, v, prob, mixed, part = attn_fwd(
            l, gains, offsets, source, weights_a[l], bias_qv[l], pos[l], picks[l % 2]
        )
        recv = swap(part, "y")
        h1, c, z, slope, part_mlp = mlp_fwd(
            l, hidden, part, recv, gains, offsets, weights_b[l], wide_bias[l]
        )
        source = (h1, part_mlp, swap(part_mlp, "y"))
        saved.append((hidden, a, q, k, v, prob, mixed, h1, c, z, slope))

    back = (place, counts, cotangent) + source
    sums_mlp, sums_attn, score_sums = [None] * layer_total, [None] * layer_total, [None] * layer_total
    grads_a, grads_b = [None] * layer_total, [None] * layer_total
    sums_tail = [None] * layer_total
    for l in reversed(range(layer_total)):
        hidden, a, q, k, v, prob, mixed, h1, c, z, slope = saved[l]
        last = l == layer_total - 1
        res = mlp_bwd(l, last, back, gains, offsets, slope, weights_b[l])
        grad, grad_b, du_b, part, sums_mlp[l] = res[:5]
        if last:
            out_mine = res[5]
        else:
            sums_tail[l + 1] = sums_mlp[l]
        recv = swap(part, "y")
        pair = mlp_grads(place, c, du_b, z, grad_b, halves, slab)
        grads_b[l] = scatter_terms(pair[:-1], pair[-1])
        dh1, dh_b, d_proj, part_in, sums_attn[l], score_sums[l] = attn_bwd(
            l, grad, part, recv, h1, gains, weights_a[l], q, k, v, prob, picks[l % 2]
        )
        back = (dh1, part_in, swap(part_in, "y"), hidden)
        pair = attn_grads(place, a, d_proj, mixed, dh_b, halves, slab)
        grads_a[l] = scatter_terms(pair[:-1], pair[-1])
    grad_mine, sums_tail[0] = tail(*back, gains, cells)

    def both_halves(x):
        recv = swap(x, "c")
        lower = c_index == 0
        return jnp.concatenate([jnp.where(lower, x, recv), jnp.where(lower, recv, x)], axis=0)

    output = both_halves(out_mine)
    grad_tokens = both_halves(grad_mine)

    tables = []
    for l in range(layer_total):
        tables.append(
            lax.dot_general(
                score_sums[l].reshape(GROUPS * heads, SLOT * SLOT),
                lookup,
                (((1,), (1,)), ((), ())),
                precision=lax.Precision.HIGHEST,
            )
        )
    own_rows, other_rows = small_pack(sums_mlp, sums_attn, sums_tail, tables, local)
    other_rows = swap(other_rows, "c")
    total = sum_dp(own_rows + other_rows)

    def states(m):
        return params[m], first_moments[m], second_moments[m]

    results = [None] * len(params)
    results[4], results[6] = adam_pair(
        grads_b, states(4), [turn(v) for v in states(6)], hidden_local
    )
    results[0], results[3] = adam_pair(grads_a, states(0), [turn(v) for v in states(3)], local)
    results[3], results[6] = [turn(v) for v in results[3]], [turn(v) for v in results[6]]
    small = [states(1), [turn(v) for v in states(2)], states(5), states(7), states(8)]
    for m, result in zip((1, 2, 5, 7, 8), small_adam(total, small)):
        results[m] = [turn(v) for v in result] if m == 2 else result
    return (output, grad_tokens) + tuple(r[kind] for kind in range(4) for r in results)


def solution(mesh):
    n_dp, n_mp = mesh.shape["dp"], mesh.shape["mp"]
    inner = Mesh(
        mesh.devices.reshape(n_dp // 2, 2, n_mp // 2, 2), ("z", "x", "y", "c")
    )
    dp = ("z", "x")
    mp = ("y", "c")
    batch = P(dp, None, None)
    member_specs = (
        P(None, None, dp, mp),
        P(None, None, mp),
        P(None, None, mp),
        P(None, mp, dp),
        P(None, dp, mp),
        P(None, mp),
        P(None, mp, dp),
        P(),
        P(),
    )
    in_specs = (batch, batch, P(dp)) + member_specs * 3
    out_specs = (batch, batch) + member_specs * 4
    return jax.shard_map(step, mesh=inner, in_specs=in_specs, out_specs=out_specs, check_vma=False)
```

```python
import jax
import jax.numpy as jnp
import numpy as np
from jax import lax
from jax.experimental import pallas as pl
from jax.experimental.pallas import tpu as pltpu
from jax.sharding import Mesh
from jax.sharding import PartitionSpec as P


HEAD_DIM = 32
WIN = 7
SIDE = 14
SHIFT = 3
STEP = 3

norm_eps = 1e-05
beta_one = 0.9
beta_two = 0.999
learn_rate = 0.02
decay_rate = 0.05
adam_eps = 1e-08

CELLS = WIN * WIN
PANES = (SIDE // WIN) ** 2
SLOT = 64
GROUPS = 2
DIRECT_MAX = 8
UNROLL = 2
ROWS = -(-SIDE * SIDE // 8) * 8
VMEM_BYTES = 60 * 1024 * 1024
f32 = jnp.float32
bf16 = jnp.bfloat16


def window_order(shifted):
    grid = np.arange(SIDE * SIDE).reshape(SIDE, SIDE)
    if shifted:
        grid = np.roll(grid, (-SHIFT, -SHIFT), axis=(0, 1))
    side_panes = SIDE // WIN
    return grid.reshape(side_panes, WIN, side_panes, WIN).transpose(0, 2, 1, 3).reshape(-1, CELLS)


def selection(shifted, images):
    source = np.full((images, PANES, SLOT), -1, np.int32)
    for i in range(images):
        source[i, :, :CELLS] = window_order(shifted) + i * ROWS
    wanted = jnp.asarray(source.reshape(-1, 1))
    return (wanted == jnp.arange(images * ROWS, dtype=jnp.int32)[None, :]).astype(bf16)


def lookup_onehot():
    places = np.arange(CELLS)
    rowpos, colpos = places // WIN, places % WIN
    lookup = (rowpos[:, None] - rowpos[None, :] + WIN - 1) * (2 * WIN - 1) + (
        colpos[:, None] - colpos[None, :] + WIN - 1
    )
    full = np.full((SLOT, SLOT), -1, np.int32)
    full[:CELLS, :CELLS] = lookup
    entries = jnp.arange((2 * WIN - 1) ** 2, dtype=jnp.int32)
    return (entries[:, None] == jnp.asarray(full.reshape(1, -1))).astype(bf16)


def pane_mask(shifted):
    pad = np.zeros((SLOT, SLOT), np.float32)
    pad[:, CELLS:] = -1e30
    if not shifted:
        return pad[None]
    coords = np.arange(SIDE)
    stripe = (coords >= SIDE - WIN).astype(int) + (coords >= SIDE - SHIFT).astype(int)
    region = (stripe[:, None] * 3 + stripe[None, :]).reshape(-1)
    side_panes = SIDE // WIN
    per = region.reshape(side_panes, WIN, side_panes, WIN).transpose(0, 2, 1, 3).reshape(-1, CELLS)
    out = np.repeat(pad[None], PANES, axis=0)
    out[:, :CELLS, :CELLS] = np.where(per[:, :, None] != per[:, None, :], -100.0, 0.0)
    return out


def dot(left, right, lc, rc):
    return lax.dot_general(left, right, (((lc,), (rc,)), ((), ())), preferred_element_type=f32)


def unit_norm(hidden):
    centered = hidden - jnp.mean(hidden, axis=-1, keepdims=True)
    inverse = lax.rsqrt(jnp.mean(centered * centered, axis=-1, keepdims=True) + norm_eps)
    return centered * inverse, inverse


def norm_back(upstream, normed, inverse, gain):
    d_normed = upstream * gain
    source = inverse * (
        d_normed
        - jnp.mean(d_normed, axis=-1, keepdims=True)
        - normed * jnp.mean(d_normed * normed, axis=-1, keepdims=True)
    )
    return source, jnp.sum(upstream * normed, axis=0, keepdims=True), jnp.sum(
        upstream, axis=0, keepdims=True
    )


def head_masks(width):
    lane = lax.broadcasted_iota(jnp.int32, (1, width), 1) // HEAD_DIM
    return [lane == head for head in range(width // HEAD_DIM)]


def spread(value, masks):
    zero = jnp.zeros_like(value)
    return jnp.concatenate([jnp.where(mask, value, zero) for mask in masks], axis=0)


def gather_heads(stacked, masks):
    total = None
    for head, mask in enumerate(masks):
        part = jnp.where(mask, stacked[head * SLOT : (head + 1) * SLOT], 0.0)
        total = part if total is None else total + part
    return total


def call(kernel, outs, *args, scratch=(), scalars=0):
    specs = [pl.BlockSpec(memory_space=pltpu.SMEM)] * scalars
    specs += [pl.BlockSpec(memory_space=pltpu.VMEM)] * (len(args) - scalars)
    return pl.pallas_call(
        kernel,
        in_specs=specs,
        out_shape=[jax.ShapeDtypeStruct(shape, dtype) for shape, dtype in outs],
        scratch_shapes=[pltpu.VMEM(shape, dtype) for shape, dtype in scratch],
        compiler_params=pltpu.CompilerParams(vmem_limit_bytes=VMEM_BYTES),
    )(*args)


def load_images(images_ref, buffer, images):
    cells, width = images_ref.shape[1:]
    for i in range(images):
        buffer[i * ROWS : i * ROWS + cells, :] = images_ref[i]
        buffer[i * ROWS + cells : (i + 1) * ROWS, :] = jnp.zeros((ROWS - cells, width), f32)


def store_images(value, out, images):
    cells = out.shape[1]
    for i in range(images):
        out[i] = value[i * ROWS : i * ROWS + cells, :]


def attn_fwd(layer, gains, offsets, source, weights, biases, pos, pick):
    first = layer == 0
    win_rows, rows = pick.shape
    *weights, at = weights
    width = weights[0].shape[0]
    panes = win_rows // SLOT
    local = biases[0].shape[2]
    heads = local // HEAD_DIM
    masks_n = pos.shape[0]
    factor = HEAD_DIM ** (-0.5)
    n_src = len(source)

    def kernel(*refs):
        src = refs[:n_src]
        gain_ref, off_ref, w0, w1, b0, b1, pos_ref, pick_ref = refs[n_src : n_src + 8]
        h_ref, a_ref, q_ref, k_ref, v_ref, prob_ref, mixed_ref, part_ref, mw_ref = refs[n_src + 8 :]
        if first:
            load_images(src[0], h_ref, rows // ROWS)
            hidden = h_ref[...]
        else:
            hidden = src[0][...] + (
                src[1][...].astype(f32) + src[2][...].astype(f32) + off_ref[layer - 1, 3:4]
            )
            h_ref[...] = hidden
        normed, _ = unit_norm(hidden)
        a = (normed * gain_ref[layer, 0:1] + off_ref[layer, 0:1]).astype(bf16)
        a_ref[...] = a
        a_win = dot(pick_ref[...], a, 1, 0).astype(bf16)
        for g, (w, bias_ref) in enumerate(((w0, b0), (w1, b1))):
            proj = dot(a_win, w[:, at : at + 3 * local], 1, 0)
            q = ((proj[:, :local] + bias_ref[layer, 0:1]) * factor).astype(bf16)
            k = proj[:, local : 2 * local].astype(bf16)
            v = (proj[:, 2 * local :] + bias_ref[layer, 1:2]).astype(bf16)
            q_ref[g] = q.reshape(panes, SLOT, local)
            k_ref[g] = k.reshape(panes, SLOT, local)
            v_ref[g] = v.reshape(panes, SLOT, local)
        masks = head_masks(local)

        def step(w, carry):
            for g in range(GROUPS):
                q, k, v = q_ref[g, w], k_ref[g, w], v_ref[g, w]
                score = dot(spread(q, masks), k, 1, 1) + pos_ref[w % masks_n if masks_n > 1 else 0, g]
                top = jnp.max(score, axis=-1, keepdims=True)
                grown = jnp.exp(score - top)
                prob = grown * (1.0 / jnp.sum(grown, axis=-1, keepdims=True))
                prob_ref[w, g] = prob
                mixed = gather_heads(dot(prob.astype(bf16), v, 1, 0), masks)
                mw_ref[w, :, g * local : (g + 1) * local] = mixed.astype(bf16)
            return carry

        lax.fori_loop(0, panes, step, 0, unroll=UNROLL)
        mixed = dot(pick_ref[...], mw_ref[...].reshape(win_rows, GROUPS * local), 0, 0).astype(bf16)
        mixed_ref[...] = mixed
        part = None
        for g, w in enumerate((w0, w1)):
            term = dot(mixed[:, g * local : (g + 1) * local], w[:, at + 3 * local : at + 4 * local], 1, 1)
            part = term if part is None else part + term
        part_ref[...] = part.astype(bf16)

    outs = [
        ((rows, width), f32),
        ((rows, width), bf16),
        ((GROUPS, panes, SLOT, local), bf16),
        ((GROUPS, panes, SLOT, local), bf16),
        ((GROUPS, panes, SLOT, local), bf16),
        ((panes, GROUPS, heads * SLOT, SLOT), f32),
        ((rows, GROUPS * local), bf16),
        ((rows, width), bf16),
    ]
    return call(
        kernel,
        outs,
        *source,
        gains,
        offsets,
        *weights,
        *biases,
        pos,
        pick,
        scratch=[((panes, SLOT, GROUPS * local), bf16)],
    )


def mlp_fwd(layer, hidden, own, recv, gains, offsets, weights, wide_biases):
    *weights, at = weights
    rows, width = hidden.shape
    local = wide_biases[0].shape[1]

    def kernel(
        h_ref, own_ref, recv_ref, gain_ref, off_ref, w0, w1, b0, b1, h1_ref, c_ref, z_ref, s_ref, p_ref
    ):
        h1 = h_ref[...] + (own_ref[...].astype(f32) + recv_ref[...].astype(f32) + off_ref[layer, 2:3])
        h1_ref[...] = h1
        normed, _ = unit_norm(h1)
        c = (normed * gain_ref[layer, 1:2] + off_ref[layer, 1:2]).astype(bf16)
        c_ref[...] = c
        part = None
        for g, (w, bias_ref) in enumerate(((w0, b0), (w1, b1))):
            u = dot(c, w[:, at : at + local], 1, 0) + bias_ref[layer : layer + 1, :]
            cdf = 0.5 * (1.0 + lax.erf(u * 0.7071067811865476))
            density = jnp.exp(-0.5 * u * u) * 0.3989422804014327
            z = (u * cdf).astype(bf16)
            z_ref[:, g * local : (g + 1) * local] = z
            s_ref[:, g * local : (g + 1) * local] = (cdf + u * density).astype(bf16)
            term = dot(z, w[:, at + local : at + 2 * local], 1, 1)
            part = term if part is None else part + term
        p_ref[...] = part.astype(bf16)

    outs = [
        ((rows, width), f32),
        ((rows, width), bf16),
        ((rows, GROUPS * local), bf16),
        ((rows, GROUPS * local), bf16),
        ((rows, width), bf16),
    ]
    return call(kernel, outs, hidden, own, recv, gains, offsets, *weights, *wide_biases)


def mlp_bwd(layer, last, source, gains, offsets, slope, weights):
    *weights, at = weights
    rows, width = source[3].shape
    local = slope.shape[1] // GROUPS
    n_src = len(source)

    def kernel(*refs):
        src = refs[:n_src]
        gain_ref, off_ref, s_ref, w0, w1 = refs[n_src : n_src + 5]
        g_ref, gb_ref, du_ref, p_ref, sum_ref = refs[n_src + 5 : n_src + 10]
        sum_ref[...] = jnp.zeros_like(sum_ref)
        if last:
            place_ref, count_ref = src[:2]
            images = rows // ROWS
            load_images(src[2], g_ref, images)
            result = src[3][...] + (src[4][...].astype(f32) + src[5][...].astype(f32) + off_ref[layer, 3:4])
            out_ref = refs[n_src + 10]
            cells = out_ref.shape[1]
            for i in range(images):
                keep = jnp.where(place_ref[0] * images + i < count_ref[0], 1.0, 0.0)
                out_ref[i] = result[i * ROWS : i * ROWS + cells, :] * keep
                g_ref[i * ROWS : (i + 1) * ROWS, :] = g_ref[i * ROWS : (i + 1) * ROWS, :] * keep
            grad = g_ref[...]
        else:
            normed, inverse = unit_norm(src[3][...])
            upstream = src[1][...].astype(f32) + src[2][...].astype(f32)
            first_grad, d_gain, d_off = norm_back(
                upstream, normed, inverse, gain_ref[layer + 1, 0:1]
            )
            grad = src[0][...] + first_grad
            sum_ref[1:2, :] = d_gain
            sum_ref[2:3, :] = d_off
            g_ref[...] = grad
        sum_ref[0:1, :] = jnp.sum(grad, axis=0, keepdims=True)
        grad_b = grad.astype(bf16)
        gb_ref[...] = grad_b
        part = None
        for g, w in enumerate((w0, w1)):
            du = dot(grad_b, w[:, at + local : at + 2 * local], 1, 0) * s_ref[:, g * local : (g + 1) * local].astype(f32)
            sum_ref[3 + g : 4 + g, :local] = jnp.sum(du, axis=0, keepdims=True)
            du_b = du.astype(bf16)
            du_ref[:, g * local : (g + 1) * local] = du_b
            term = dot(du_b, w[:, at : at + local], 1, 1)
            part = term if part is None else part + term
        p_ref[...] = part.astype(bf16)

    outs = [
        ((rows, width), f32),
        ((rows, width), bf16),
        ((rows, GROUPS * local), bf16),
        ((rows, width), bf16),
        ((8, width), f32),
    ]
    if last:
        outs.append(((rows // ROWS, source[2].shape[1], width), f32))
    return call(kernel, outs, *source, gains, offsets, slope, *weights, scalars=2 if last else 0)


def grad_outs(width, cols, halves):
    if not halves:
        return [((width, cols), bf16)] * 2
    half = width // halves
    return [((half, cols), bf16), ((half, cols), bf16), ((halves, half, cols), bf16)]


def cut(full, outs, place_ref, halves, slab):
    if not halves:
        outs[0][...] = full[...]
        return
    deep = full.shape[0] // (halves * slab)
    for x in range(halves):
        for z in range(deep):
            block = (z ^ place_ref[1]) * halves + (x ^ place_ref[2])
            start = pl.multiple_of(block * slab, slab)
            target = outs[x] if len(outs) > 1 else outs[0].at[x]
            target[z * slab : (z + 1) * slab, :] = full[pl.ds(start, slab), :]


def mlp_grads(place, c, du_b, z, grad_b, halves, slab):
    width = c.shape[1]
    local = z.shape[1] // GROUPS

    def kernel(place_ref, c_ref, du_ref, z_ref, g_ref, *outs):
        full = outs[-1]
        for g, out in enumerate((outs[:-2], outs[-2:-1])):
            cols = slice(g * local, (g + 1) * local)
            full[:, :local] = dot(c_ref[...], du_ref[:, cols], 0, 0).astype(bf16)
            full[:, local:] = dot(g_ref[...], z_ref[:, cols], 0, 0).astype(bf16)
            cut(full, out, place_ref, halves, slab)

    return call(
        kernel,
        grad_outs(width, 2 * local, halves),
        place,
        c,
        du_b,
        z,
        grad_b,
        scratch=[((width, 2 * local), bf16)],
        scalars=1,
    )


def attn_bwd(layer, grad, own, recv, h1, gains, weights, q, k, v, prob, pick):
    rows, width = grad.shape
    win_rows = pick.shape[0]
    panes = win_rows // SLOT
    *weights, at = weights
    local = q.shape[3]
    heads = local // HEAD_DIM
    factor = HEAD_DIM ** (-0.5)

    def kernel(
        g_ref, own_ref, recv_ref, h1_ref, gain_ref, w0, w1, q_ref, k_ref, v_ref, prob_ref, pick_ref,
        dh_ref, dhb_ref, dp_ref, part_ref, sum_ref, ds_ref, dm_ref, dw_ref, bias_ref,
    ):
        normed, inverse = unit_norm(h1_ref[...])
        upstream = own_ref[...].astype(f32) + recv_ref[...].astype(f32)
        d_mid, d_gain, d_off = norm_back(upstream, normed, inverse, gain_ref[layer, 1:2])
        dh1 = g_ref[...] + d_mid
        dh_ref[...] = dh1
        sum_ref[...] = jnp.zeros_like(sum_ref)
        sum_ref[0:1, :] = d_gain
        sum_ref[1:2, :] = d_off
        sum_ref[2:3, :] = jnp.sum(dh1, axis=0, keepdims=True)
        dh_b = dh1.astype(bf16)
        dhb_ref[...] = dh_b
        for g, w in enumerate((w0, w1)):
            d_mixed = dot(dh_b, w[:, at + 3 * local : at + 4 * local], 1, 0).astype(bf16)
            d_win = dot(pick_ref[...], d_mixed, 1, 0).astype(bf16)
            dm_ref[g] = d_win.reshape(panes, SLOT, local)
        ds_ref[...] = jnp.zeros_like(ds_ref)
        bias_ref[...] = jnp.zeros_like(bias_ref)
        masks = head_masks(local)

        def step(w, carry):
            for g in range(GROUPS):
                keys, values = k_ref[g, w], v_ref[g, w]
                d_out = spread(dm_ref[g, w], masks)
                queries = spread(q_ref[g, w], masks)
                probs = prob_ref[w, g]
                d_prob = dot(d_out, values, 1, 1)
                d_value = dot(probs.astype(bf16), d_out, 0, 0)
                d_score = probs * (d_prob - jnp.sum(probs * d_prob, axis=-1, keepdims=True))
                ds_ref[g] += d_score
                d_score_b = d_score.astype(bf16)
                d_query = gather_heads(dot(d_score_b, keys, 1, 0), masks) * factor
                d_key = dot(d_score_b, queries, 0, 0)
                base = g * 3 * local
                dw_ref[w, :, base : base + local] = d_query.astype(bf16)
                dw_ref[w, :, base + local : base + 2 * local] = d_key.astype(bf16)
                dw_ref[w, :, base + 2 * local : base + 3 * local] = d_value.astype(bf16)
                bias_ref[0:1, g * local : (g + 1) * local] += jnp.sum(d_query, axis=0, keepdims=True)
                bias_ref[1:2, g * local : (g + 1) * local] += jnp.sum(d_value, axis=0, keepdims=True)
            return carry

        lax.fori_loop(0, panes, step, 0)
        sum_ref[3:4, : GROUPS * local] = bias_ref[0:1, :]
        sum_ref[4:5, : GROUPS * local] = bias_ref[1:2, :]
        d_proj = dot(
            pick_ref[...], dw_ref[...].reshape(win_rows, GROUPS * 3 * local), 0, 0
        ).astype(bf16)
        dp_ref[...] = d_proj
        part = None
        for g, w in enumerate((w0, w1)):
            term = dot(d_proj[:, g * 3 * local : (g + 1) * 3 * local], w[:, at : at + 3 * local], 1, 1)
            part = term if part is None else part + term
        part_ref[...] = part.astype(bf16)

    outs = [
        ((rows, width), f32),
        ((rows, width), bf16),
        ((rows, GROUPS * 3 * local), bf16),
        ((rows, width), bf16),
        ((8, width), f32),
        ((GROUPS, heads * SLOT, SLOT), f32),
    ]
    return call(
        kernel,
        outs,
        grad,
        own,
        recv,
        h1,
        gains,
        *weights,
        q,
        k,
        v,
        prob,
        pick,
        scratch=[
            ((GROUPS, panes, SLOT, local), bf16),
            ((panes, SLOT, GROUPS * 3 * local), bf16),
            ((8, GROUPS * local), f32),
        ],
    )


def attn_grads(place, a, d_proj, mixed, dh_b, halves, slab):
    width = a.shape[1]
    local = mixed.shape[1] // GROUPS

    def kernel(place_ref, a_ref, dp_ref, m_ref, g_ref, *outs):
        full = outs[-1]
        for g, out in enumerate((outs[:-2], outs[-2:-1])):
            full[:, : 3 * local] = dot(
                a_ref[...], dp_ref[:, g * 3 * local : (g + 1) * 3 * local], 0, 0
            ).astype(bf16)
            full[:, 3 * local :] = dot(
                g_ref[...], m_ref[:, g * local : (g + 1) * local], 0, 0
            ).astype(bf16)
            cut(full, out, place_ref, halves, slab)

    return call(
        kernel,
        grad_outs(width, 4 * local, halves),
        place,
        a,
        d_proj,
        mixed,
        dh_b,
        scratch=[((width, 4 * local), bf16)],
        scalars=1,
    )


def tail(dh1, own, recv, hidden, gains, cells):
    rows, width = dh1.shape
    images = rows // ROWS

    def kernel(d_ref, own_ref, recv_ref, h_ref, gain_ref, o_ref, sum_ref):
        normed, inverse = unit_norm(h_ref[...])
        upstream = own_ref[...].astype(f32) + recv_ref[...].astype(f32)
        first_grad, d_gain, d_off = norm_back(upstream, normed, inverse, gain_ref[0, 0:1])
        store_images(d_ref[...] + first_grad, o_ref, images)
        sum_ref[...] = jnp.zeros_like(sum_ref)
        sum_ref[1:2, :] = d_gain
        sum_ref[2:3, :] = d_off

    outs = [((images, cells, width), f32), ((8, width), f32)]
    return call(kernel, outs, dh1, own, recv, hidden, gains)


def order(blocks, place, member):
    rows, cols = blocks[0].shape

    def kernel(place_ref, *refs):
        out = refs[-1]
        for s in range(len(blocks)):
            start = pl.multiple_of((place_ref[member] ^ s) * rows, rows)
            out[pl.ds(start, rows), :] = refs[s][...]

    outs = [((rows * len(blocks), cols), blocks[0].dtype)]
    return call(kernel, outs, place, *blocks, scalars=1)[0]


def pack(inwards, outwards, widening, narrowing):
    layers, _, slab, local = inwards.shape
    hidden = widening.shape[2]

    def kernel(in_ref, out_ref, wide_ref, narrow_ref, *packed):
        for l in range(layers):
            part_a, part_b = packed[2 * l : 2 * l + 2]
            for j in range(3):
                part_a[:, j * local : (j + 1) * local] = in_ref[l, j].astype(bf16)
            part_a[:, 3 * local :] = out_ref[l].astype(bf16)
            part_b[:, :hidden] = wide_ref[l].astype(bf16)
            part_b[:, hidden:] = narrow_ref[l].astype(bf16)

    outs = [((slab, 4 * local), bf16), ((slab, 2 * hidden), bf16)] * layers
    return call(kernel, outs, inwards, outwards, widening, narrowing)


def adam_all(parts, states):
    layers = len(parts)
    count = len(parts[0])
    flat = [p for terms in parts for p in terms]

    def kernel(*refs):
        blocks, refs = refs[: len(flat)], refs[len(flat) :]
        ins, outs = refs[:12], refs[12:]

        def update(member, index, gradient):
            weight, mean, square = (r[index] for r in ins[3 * member : 3 * member + 3])
            new = (gradient,) + adam_update(weight, gradient, mean, square, decay_rate)
            for ref, value in zip(outs[4 * member : 4 * member + 4], new):
                ref[index] = value

        for l in range(layers):
            total = tree([blocks[l * count + i][...].astype(f32) for i in range(count)])
            at = 0
            for member in range(4):
                shape = ins[3 * member].shape
                for j in range(shape[1] if len(shape) == 4 else 1):
                    index = (l, j) if len(shape) == 4 else (l,)
                    update(member, index, total[:, at : at + shape[-1]])
                    at += shape[-1]

    outs = [(state[0].shape, f32) for state in states for _ in range(4)]
    res = call(kernel, outs, *flat, *[v for state in states for v in state])
    return [res[4 * m : 4 * m + 4] for m in range(4)]


def join(place, own, recv):
    images, cells, width = own.shape

    def kernel(place_ref, own_ref, recv_ref, out_ref):
        lower = place_ref[0] == 0
        for i in range(images):
            mine, theirs = own_ref[i], recv_ref[i]
            out_ref[:, i, :] = jnp.where(lower, mine, theirs)
            out_ref[:, images + i, :] = jnp.where(lower, theirs, mine)

    outs = [((cells, 2 * images, width), f32)]
    return call(kernel, outs, place, own, recv, scalars=1)[0]


def small_rows(layers, heads):
    per = 8 + heads
    return per, -(-layers * per // 8) * 8


def small_pack(sums_mlp, sums_attn, sums_tail, tables, local):
    layers = len(tables)
    heads = tables[0].shape[0] // GROUPS
    entries = tables[0].shape[1]
    width = sums_mlp[0].shape[1]
    per, rows = small_rows(layers, heads)

    def kernel(*refs):
        ins, outs = refs[:-GROUPS], refs[-GROUPS:]
        for g, out in enumerate(outs):
            out[...] = jnp.zeros_like(out)
            for l in range(layers):
                mlp, attn, late, table = ins[4 * l : 4 * l + 4]
                base = l * per
                out[base : base + 1, :] = late[1:2, :]
                out[base + 1 : base + 2, :] = attn[0:1, :]
                out[base + 2 : base + 3, :] = late[2:3, :]
                out[base + 3 : base + 4, :] = attn[1:2, :]
                out[base + 4 : base + 5, :] = attn[2:3, :]
                out[base + 5 : base + 6, :] = mlp[0:1, :]
                out[base + 6 : base + 7, :] = mlp[3 + g : 4 + g, :]
                out[base + 7 : base + 8, :local] = attn[3:4, g * local : (g + 1) * local]
                out[base + 7 : base + 8, local : 2 * local] = attn[4:5, g * local : (g + 1) * local]
                out[base + 8 : base + 8 + heads, :entries] = table[g * heads : (g + 1) * heads, :]

    flat = [v for quad in zip(sums_mlp, sums_attn, sums_tail, tables) for v in quad]
    return call(kernel, [((rows, width), f32)] * GROUPS, *flat)


def small_adam(total, states):
    layers, _, local = states[0][0].shape
    heads, entries = states[1][0].shape[1:]
    hidden = states[2][0].shape[1]
    width = states[3][0].shape[2]
    per, _ = small_rows(layers, heads)

    def kernel(total_ref, *refs):
        ins, outs = refs[:15], refs[15:]

        def update(member, index, gradient):
            weight, mean, square = (r[index] for r in ins[3 * member : 3 * member + 3])
            new = (gradient,) + adam_update(weight, gradient, mean, square, 0.0)
            for ref, value in zip(outs[4 * member : 4 * member + 4], new):
                ref[index] = value

        for l in range(layers):
            base = l * per
            for row in range(2):
                update(
                    0,
                    (l, slice(row, row + 1)),
                    total_ref[base + 7 : base + 8, row * local : (row + 1) * local],
                )
            update(1, (l,), total_ref[base + 8 : base + 8 + heads, :entries])
            update(2, (slice(l, l + 1),), total_ref[base + 6 : base + 7, :hidden])
            update(3, (l,), total_ref[base : base + 2, :width])
            update(4, (l,), total_ref[base + 2 : base + 6, :width])

    outs = [(state[0].shape, f32) for state in states for _ in range(4)]
    res = call(kernel, outs, total, *[v for state in states for v in state])
    return [res[4 * m : 4 * m + 4] for m in range(5)]


def adam_update(weight, gradient, moment_one, second, decay_on):
    first_new = beta_one * moment_one + (1.0 - beta_one) * gradient
    second_new = beta_two * second + (1.0 - beta_two) * gradient * gradient
    first_hat = first_new / (1.0 - beta_one**STEP)
    second_hat = second_new / (1.0 - beta_two**STEP)
    updated = weight - learn_rate * (
        first_hat / (jnp.sqrt(second_hat) + adam_eps) + decay_on * weight
    )
    return (updated, first_new, second_new)


def turn(x):
    return jnp.swapaxes(x, 1, 2)


def tree(parts):
    while len(parts) > 1:
        parts = [parts[i] + parts[i + 1] for i in range(0, len(parts), 2)]
    return parts[0]


def step(*args):
    (tokens, cotangent, counts), params = args[:3], list(args[3:12])
    first_moments, second_moments = list(args[12:21]), list(args[21:30])
    inwards, inbias, relative, outwards, widening, widebias, narrowing, gains, offsets = params
    layer_total = inwards.shape[0]
    slots, cells, _ = tokens.shape
    images = slots // 2
    local = inwards.shape[3]
    heads = local // HEAD_DIM
    slab = inwards.shape[2]
    n_x = lax.axis_size("x")
    n_z = lax.axis_size("z")
    direct = n_x == 2 and n_x * n_z <= DIRECT_MAX and n_z & (n_z - 1) == 0
    halves = n_x if direct else 0
    c_index = lax.axis_index("c")
    place = jnp.stack(
        [
            c_index,
            lax.axis_index("z"),
            lax.axis_index("x"),
            lax.axis_index("z") * n_x + lax.axis_index("x"),
        ]
    ).astype(jnp.int32)
    dp = ("z", "x")

    def swap(x, axis):
        return lax.ppermute(x, axis, [(0, 1), (1, 0)])

    def xor_z(x, s):
        return lax.ppermute(x, "z", [(i, i ^ s) for i in range(n_z)])

    def xor_dp(x, s):
        return lax.ppermute(x, dp, [(i, i ^ s) for i in range(n_x * n_z)])

    def gather_now(p):
        if not direct:
            return lax.all_gather(p, dp, axis=0, tiled=True)
        blocks = [p] + [xor_dp(p, s) for s in range(1, n_x * n_z)]
        return order(blocks, place, 3)

    def gather_staged(p):
        if not direct:
            return lax.all_gather(p, dp, axis=0, tiled=True)
        away = swap(p, "x")
        pair = order([p, away], place, 2)
        blocks = [pair] + [xor_z(pair, s) for s in range(1, n_z)]
        return order(blocks, place, 1)

    def scatter_half(own, other):
        recv = swap(other, "c")
        if not direct:
            return (own[0].astype(f32) + recv.astype(f32)).astype(bf16)
        away = (own[1].astype(f32) + recv[1].astype(f32)).astype(bf16)
        back = swap(away, "x")
        return own[0].astype(f32) + recv[0].astype(f32) + back.astype(f32)

    def scatter_rest(halves_of):
        near = jnp.concatenate(halves_of, axis=1).astype(bf16)
        if not direct:
            return [lax.psum_scatter(near, dp, scatter_dimension=0, tiled=True)]
        return [near[:slab]] + [xor_z(near[s * slab : (s + 1) * slab], s) for s in range(1, n_z)]

    def sum_dp(x):
        if not direct:
            return lax.psum(x, dp)
        x = x + swap(x, "x")
        return tree([x if s == 0 else xor_z(x, s) for s in range(n_z)])

    shards = pack(inwards, turn(outwards), widening, turn(narrowing))
    whole = []
    for i, shard in enumerate(shards):
        full = gather_staged(shard) if i else gather_now(shard)
        whole.append((full, swap(full, "c"), 0))
    weights_a, weights_b = whole[0::2], whole[1::2]

    tables = turn(relative)
    biases = (inbias, swap(inbias, "c"))
    wide_biases = (widebias, swap(widebias, "c"))
    tables = jnp.concatenate([tables, swap(tables, "c")], axis=1)
    lookup = lookup_onehot()
    pos = []
    for l in range(layer_total):
        mask = pane_mask(l % 2 == 1)
        upper = lax.reduce_precision(tables[l], 8, 7)
        middle = lax.reduce_precision(tables[l] - upper, 8, 7)
        terms = jnp.concatenate([upper, middle, tables[l] - upper - middle], axis=0)
        terms = dot(terms.astype(bf16), lookup, 1, 0).reshape(3, -1, SLOT * SLOT)
        spread_bias = (terms[0] + terms[1] + terms[2]).reshape(GROUPS, heads, SLOT, SLOT)
        full = spread_bias[None] + jnp.asarray(mask)[:, None, None]
        pos.append(full.reshape(mask.shape[0], GROUPS, heads * SLOT, SLOT))
    picks = [
        selection(l % 2 == 1, images) for l in range(min(layer_total, 2))
    ]

    saved = []
    source = (lax.dynamic_slice_in_dim(tokens, c_index * images, images, 0),)
    for l in range(layer_total):
        hidden, a, q, k, v, prob, mixed, part = attn_fwd(
            l, gains, offsets, source, weights_a[l], biases, pos[l], picks[l % 2]
        )
        recv = swap(part, "y")
        h1, c, z, slope, part_mlp = mlp_fwd(
            l, hidden, part, recv, gains, offsets, weights_b[l], wide_biases
        )
        source = (h1, part_mlp, swap(part_mlp, "y"))
        saved.append((hidden, a, q, k, v, prob, mixed, h1, c, z, slope))

    cot_mine = lax.dynamic_slice_in_dim(cotangent, c_index * images, images, 0)
    back = (place, counts, cot_mine) + source
    sums_mlp, sums_attn, score_sums = [None] * layer_total, [None] * layer_total, [None] * layer_total
    grads = [None] * layer_total
    sums_tail = [None] * layer_total
    for l in reversed(range(layer_total)):
        hidden, a, q, k, v, prob, mixed, h1, c, z, slope = saved[l]
        last = l == layer_total - 1
        res = mlp_bwd(l, last, back, gains, offsets, slope, weights_b[l])
        grad, grad_b, du_b, part, sums_mlp[l] = res[:5]
        if last:
            out_mine = res[5]
        else:
            sums_tail[l + 1] = sums_mlp[l]
        recv = swap(part, "y")
        pair = mlp_grads(place, c, du_b, z, grad_b, halves, slab)
        half_b = scatter_half(pair[:-1], pair[-1])
        dh1, dh_b, d_proj, part_in, sums_attn[l], score_sums[l] = attn_bwd(
            l, grad, part, recv, h1, gains, weights_a[l], q, k, v, prob, picks[l % 2]
        )
        back = (dh1, part_in, swap(part_in, "y"), hidden)
        pair = attn_grads(place, a, d_proj, mixed, dh_b, halves, slab)
        half_a = scatter_half(pair[:-1], pair[-1])
        grads[l] = scatter_rest([half_a, half_b])
    grad_mine, sums_tail[0] = tail(*back, gains, cells)

    def both_halves(x):
        recv = swap(x, "c")
        return jnp.swapaxes(join(place, x, recv), 0, 1)

    output = both_halves(out_mine)
    grad_tokens = both_halves(grad_mine)

    tables = []
    for l in range(layer_total):
        flat = score_sums[l].reshape(GROUPS * heads, SLOT * SLOT)
        upper = lax.reduce_precision(flat, 8, 7)
        both = jnp.concatenate([upper, flat - upper], axis=0).astype(bf16)
        both = dot(both, lookup, 1, 1)
        tables.append(both[: GROUPS * heads] + both[GROUPS * heads :])
    own_rows, other_rows = small_pack(sums_mlp, sums_attn, sums_tail, tables, local)
    other_rows = swap(other_rows, "c")
    total = sum_dp(own_rows + other_rows)

    def states(m):
        return params[m], first_moments[m], second_moments[m]

    results = [None] * len(params)
    matrices = [states(0), [turn(v) for v in states(3)], states(4), [turn(v) for v in states(6)]]
    updated = adam_all(grads, matrices)
    for m, result in zip((0, 3, 4, 6), updated):
        results[m] = [turn(v) for v in result] if m in (3, 6) else result
    small = [states(1), [turn(v) for v in states(2)], states(5), states(7), states(8)]
    updated = small_adam(total, small)
    for m, result in zip((1, 2, 5, 7, 8), updated):
        results[m] = [turn(v) for v in result] if m == 2 else result
    return (output, grad_tokens) + tuple(r[kind] for kind in range(4) for r in results)


def solution(mesh):
    n_dp, n_mp = mesh.shape["dp"], mesh.shape["mp"]
    inner = Mesh(
        mesh.devices.reshape(n_dp // 2, 2, n_mp // 2, 2), ("z", "x", "y", "c")
    )
    dp = ("z", "x")
    mp = ("y", "c")
    batch = P(dp, None, None)
    member_specs = (
        P(None, None, dp, mp),
        P(None, None, mp),
        P(None, None, mp),
        P(None, mp, dp),
        P(None, dp, mp),
        P(None, mp),
        P(None, mp, dp),
        P(),
        P(),
    )
    in_specs = (batch, batch, P(dp)) + member_specs * 3
    out_specs = (batch, batch) + member_specs * 4
    return jax.shard_map(step, mesh=inner, in_specs=in_specs, out_specs=out_specs, check_vma=False)
```

```python
import jax
import jax.numpy as jnp
import numpy as np
from jax import lax
from jax.experimental import pallas as pl
from jax.experimental.pallas import tpu as pltpu
from jax.sharding import Mesh
from jax.sharding import PartitionSpec as P


HEAD_DIM = 32
WIN = 7
SIDE = 14
SHIFT = 3
STEP = 3

norm_eps = 1e-05
beta_one = 0.9
beta_two = 0.999
learn_rate = 0.02
decay_rate = 0.05
adam_eps = 1e-08

CELLS = WIN * WIN
PANES = (SIDE // WIN) ** 2
SLOT = 64
GROUPS = 2
DIRECT_MAX = 8
UNROLL = 2
ROWS = -(-SIDE * SIDE // 8) * 8
VMEM_BYTES = 60 * 1024 * 1024
f32 = jnp.float32
bf16 = jnp.bfloat16


def window_order(shifted):
    grid = np.arange(SIDE * SIDE).reshape(SIDE, SIDE)
    if shifted:
        grid = np.roll(grid, (-SHIFT, -SHIFT), axis=(0, 1))
    side_panes = SIDE // WIN
    return grid.reshape(side_panes, WIN, side_panes, WIN).transpose(0, 2, 1, 3).reshape(-1, CELLS)


def selection(shifted, images):
    source = np.full((images, PANES, SLOT), -1, np.int32)
    for i in range(images):
        source[i, :, :CELLS] = window_order(shifted) + i * ROWS
    wanted = jnp.asarray(source.reshape(-1, 1))
    return (wanted == jnp.arange(images * ROWS, dtype=jnp.int32)[None, :]).astype(bf16)


def lookup_onehot():
    places = np.arange(CELLS)
    rowpos, colpos = places // WIN, places % WIN
    lookup = (rowpos[:, None] - rowpos[None, :] + WIN - 1) * (2 * WIN - 1) + (
        colpos[:, None] - colpos[None, :] + WIN - 1
    )
    full = np.full((SLOT, SLOT), -1, np.int32)
    full[:CELLS, :CELLS] = lookup
    entries = jnp.arange((2 * WIN - 1) ** 2, dtype=jnp.int32)
    return (entries[:, None] == jnp.asarray(full.reshape(1, -1))).astype(bf16)


def pane_mask(shifted):
    pad = np.zeros((SLOT, SLOT), np.float32)
    pad[:, CELLS:] = -1e30
    if not shifted:
        return pad[None]
    coords = np.arange(SIDE)
    stripe = (coords >= SIDE - WIN).astype(int) + (coords >= SIDE - SHIFT).astype(int)
    region = (stripe[:, None] * 3 + stripe[None, :]).reshape(-1)
    side_panes = SIDE // WIN
    per = region.reshape(side_panes, WIN, side_panes, WIN).transpose(0, 2, 1, 3).reshape(-1, CELLS)
    out = np.repeat(pad[None], PANES, axis=0)
    out[:, :CELLS, :CELLS] = np.where(per[:, :, None] != per[:, None, :], -100.0, 0.0)
    return out


def dot(left, right, lc, rc):
    return lax.dot_general(left, right, (((lc,), (rc,)), ((), ())), preferred_element_type=f32)


def unit_norm(hidden):
    centered = hidden - jnp.mean(hidden, axis=-1, keepdims=True)
    inverse = lax.rsqrt(jnp.mean(centered * centered, axis=-1, keepdims=True) + norm_eps)
    return centered * inverse, inverse


def norm_back(upstream, normed, inverse, gain):
    d_normed = upstream * gain
    source = inverse * (
        d_normed
        - jnp.mean(d_normed, axis=-1, keepdims=True)
        - normed * jnp.mean(d_normed * normed, axis=-1, keepdims=True)
    )
    return source, jnp.sum(upstream * normed, axis=0, keepdims=True), jnp.sum(
        upstream, axis=0, keepdims=True
    )


def head_masks(width):
    lane = lax.broadcasted_iota(jnp.int32, (1, width), 1) // HEAD_DIM
    return [lane == head for head in range(width // HEAD_DIM)]


def spread(value, masks):
    zero = jnp.zeros_like(value)
    return jnp.concatenate([jnp.where(mask, value, zero) for mask in masks], axis=0)


def gather_heads(stacked, masks):
    total = None
    for head, mask in enumerate(masks):
        part = jnp.where(mask, stacked[head * SLOT : (head + 1) * SLOT], 0.0)
        total = part if total is None else total + part
    return total


def call(kernel, outs, *args, scratch=(), scalars=0):
    specs = [pl.BlockSpec(memory_space=pltpu.SMEM)] * scalars
    specs += [pl.BlockSpec(memory_space=pltpu.VMEM)] * (len(args) - scalars)
    return pl.pallas_call(
        kernel,
        in_specs=specs,
        out_shape=[jax.ShapeDtypeStruct(shape, dtype) for shape, dtype in outs],
        scratch_shapes=[pltpu.VMEM(shape, dtype) for shape, dtype in scratch],
        compiler_params=pltpu.CompilerParams(vmem_limit_bytes=VMEM_BYTES),
    )(*args)


def load_images(images_ref, buffer, images, first=0):
    cells, width = images_ref.shape[1:]
    for i in range(images):
        buffer[i * ROWS : i * ROWS + cells, :] = images_ref[first + i]
        buffer[i * ROWS + cells : (i + 1) * ROWS, :] = jnp.zeros((ROWS - cells, width), f32)


def store_images(value, out, images):
    cells = out.shape[1]
    for i in range(images):
        out[i] = value[i * ROWS : i * ROWS + cells, :]


def attn_fwd(layer, gains, offsets, source, weights, biases, pos, pick, cuts):
    first = layer == 0
    win_rows, rows = pick.shape
    *weights, at = weights
    width = weights[0].shape[0]
    panes = win_rows // SLOT
    local = biases[0].shape[2]
    heads = local // HEAD_DIM
    masks_n = pos.shape[0]
    factor = HEAD_DIM ** (-0.5)
    n_src = len(source)

    def kernel(*refs):
        src = refs[:n_src]
        gain_ref, off_ref, w0, w1, b0, b1, pos_ref, pick_ref = refs[n_src : n_src + 8]
        h_ref, a_ref, q_ref, k_ref, v_ref, prob_ref, mixed_ref = refs[n_src + 8 : n_src + 15]
        part_refs, mw_ref = refs[n_src + 15 : -1], refs[-1]
        if first:
            load_images(src[0], h_ref, rows // ROWS)
            hidden = h_ref[...]
        else:
            hidden = src[0][...] + (
                src[1][...].astype(f32) + src[2][...].astype(f32) + off_ref[layer - 1, 3:4]
            )
            h_ref[...] = hidden
        normed, _ = unit_norm(hidden)
        a = (normed * gain_ref[layer, 0:1] + off_ref[layer, 0:1]).astype(bf16)
        a_ref[...] = a
        a_win = dot(pick_ref[...], a, 1, 0).astype(bf16)
        for g, (w, bias_ref) in enumerate(((w0, b0), (w1, b1))):
            proj = dot(a_win, w[:, at : at + 3 * local], 1, 0)
            q = ((proj[:, :local] + bias_ref[layer, 0:1]) * factor).astype(bf16)
            k = proj[:, local : 2 * local].astype(bf16)
            v = (proj[:, 2 * local :] + bias_ref[layer, 1:2]).astype(bf16)
            q_ref[g] = q.reshape(panes, SLOT, local)
            k_ref[g] = k.reshape(panes, SLOT, local)
            v_ref[g] = v.reshape(panes, SLOT, local)
        masks = head_masks(local)

        def step(w, carry):
            for g in range(GROUPS):
                q, k, v = q_ref[g, w], k_ref[g, w], v_ref[g, w]
                score = dot(spread(q, masks), k, 1, 1) + pos_ref[w % masks_n if masks_n > 1 else 0, g]
                top = jnp.max(score, axis=-1, keepdims=True)
                grown = jnp.exp(score - top)
                prob = grown * (1.0 / jnp.sum(grown, axis=-1, keepdims=True))
                prob_ref[w, g] = prob
                mixed = gather_heads(dot(prob.astype(bf16), v, 1, 0), masks)
                mw_ref[w, :, g * local : (g + 1) * local] = mixed.astype(bf16)
            return carry

        lax.fori_loop(0, panes, step, 0, unroll=UNROLL)
        mixed = dot(pick_ref[...], mw_ref[...].reshape(win_rows, GROUPS * local), 0, 0).astype(bf16)
        mixed_ref[...] = mixed
        part = None
        for g, w in enumerate((w0, w1)):
            term = dot(mixed[:, g * local : (g + 1) * local], w[:, at + 3 * local : at + 4 * local], 1, 1)
            part = term if part is None else part + term
        for i, part_ref in enumerate(part_refs):
            part_ref[...] = part[i * rows // cuts : (i + 1) * rows // cuts].astype(bf16)

    outs = [
        ((rows, width), f32),
        ((rows, width), bf16),
        ((GROUPS, panes, SLOT, local), bf16),
        ((GROUPS, panes, SLOT, local), bf16),
        ((GROUPS, panes, SLOT, local), bf16),
        ((panes, GROUPS, heads * SLOT, SLOT), f32),
        ((rows, GROUPS * local), bf16),
    ] + [((rows // cuts, width), bf16)] * cuts
    return call(
        kernel,
        outs,
        *source,
        gains,
        offsets,
        *weights,
        *biases,
        pos,
        pick,
        scratch=[((panes, SLOT, GROUPS * local), bf16)],
    )


def mlp_fwd(layer, cut_index, hidden, own, recv, gains, offsets, weights, wide_biases):
    *weights, at = weights
    rows, width = own.shape
    first = cut_index * rows
    local = wide_biases[0].shape[1]

    def kernel(
        h_ref, own_ref, recv_ref, gain_ref, off_ref, w0, w1, b0, b1, h1_ref, c_ref, z_ref, s_ref, p_ref
    ):
        h1 = h_ref[first : first + rows] + (own_ref[...].astype(f32) + recv_ref[...].astype(f32) + off_ref[layer, 2:3])
        h1_ref[...] = h1
        normed, _ = unit_norm(h1)
        c = (normed * gain_ref[layer, 1:2] + off_ref[layer, 1:2]).astype(bf16)
        c_ref[...] = c
        part = None
        for g, (w, bias_ref) in enumerate(((w0, b0), (w1, b1))):
            u = dot(c, w[:, at : at + local], 1, 0) + bias_ref[layer : layer + 1, :]
            cdf = 0.5 * (1.0 + lax.erf(u * 0.7071067811865476))
            density = jnp.exp(-0.5 * u * u) * 0.3989422804014327
            z = (u * cdf).astype(bf16)
            z_ref[:, g * local : (g + 1) * local] = z
            s_ref[:, g * local : (g + 1) * local] = (cdf + u * density).astype(bf16)
            term = dot(z, w[:, at + local : at + 2 * local], 1, 1)
            part = term if part is None else part + term
        p_ref[...] = part.astype(bf16)

    outs = [
        ((rows, width), f32),
        ((rows, width), bf16),
        ((rows, GROUPS * local), bf16),
        ((rows, GROUPS * local), bf16),
        ((rows, width), bf16),
    ]
    return call(kernel, outs, hidden, own, recv, gains, offsets, *weights, *wide_biases)


def mlp_bwd(layer, last, cut_index, source, gains, offsets, slope, weights):
    *weights, at = weights
    rows, width = source[3].shape
    local = slope.shape[1] // GROUPS
    n_src = len(source)

    def kernel(*refs):
        src = refs[:n_src]
        gain_ref, off_ref, s_ref, w0, w1 = refs[n_src : n_src + 5]
        g_ref, gb_ref, du_ref, p_ref, sum_ref = refs[n_src + 5 : n_src + 10]
        sum_ref[...] = jnp.zeros_like(sum_ref)
        if last:
            place_ref, count_ref = src[:2]
            images = rows // ROWS
            load_images(src[2], g_ref, images, cut_index * images)
            result = src[3][...] + (src[4][...].astype(f32) + src[5][...].astype(f32) + off_ref[layer, 3:4])
            out_ref = refs[n_src + 10]
            cells = out_ref.shape[1]
            for i in range(images):
                slot = place_ref[0] * src[2].shape[0] + cut_index * images + i
                keep = jnp.where(slot < count_ref[0], 1.0, 0.0)
                out_ref[i] = result[i * ROWS : i * ROWS + cells, :] * keep
                g_ref[i * ROWS : (i + 1) * ROWS, :] = g_ref[i * ROWS : (i + 1) * ROWS, :] * keep
            grad = g_ref[...]
        else:
            normed, inverse = unit_norm(src[3][...])
            upstream = src[1][...].astype(f32) + src[2][...].astype(f32)
            first_grad, d_gain, d_off = norm_back(
                upstream, normed, inverse, gain_ref[layer + 1, 0:1]
            )
            grad = src[0][...] + first_grad
            sum_ref[1:2, :] = d_gain
            sum_ref[2:3, :] = d_off
            g_ref[...] = grad
        sum_ref[0:1, :] = jnp.sum(grad, axis=0, keepdims=True)
        grad_b = grad.astype(bf16)
        gb_ref[...] = grad_b
        part = None
        for g, w in enumerate((w0, w1)):
            du = dot(grad_b, w[:, at + local : at + 2 * local], 1, 0) * s_ref[:, g * local : (g + 1) * local].astype(f32)
            sum_ref[3 + g : 4 + g, :local] = jnp.sum(du, axis=0, keepdims=True)
            du_b = du.astype(bf16)
            du_ref[:, g * local : (g + 1) * local] = du_b
            term = dot(du_b, w[:, at : at + local], 1, 1)
            part = term if part is None else part + term
        p_ref[...] = part.astype(bf16)

    outs = [
        ((rows, width), f32),
        ((rows, width), bf16),
        ((rows, GROUPS * local), bf16),
        ((rows, width), bf16),
        ((8, width), f32),
    ]
    if last:
        outs.append(((rows // ROWS, source[2].shape[1], width), f32))
    return call(kernel, outs, *source, gains, offsets, slope, *weights, scalars=2 if last else 0)


def grad_outs(width, cols, halves):
    if not halves:
        return [((width, cols), bf16)] * 2
    half = width // halves
    return [((half, cols), bf16), ((half, cols), bf16), ((halves, half, cols), bf16)]


def cut(full, outs, place_ref, halves, slab):
    if not halves:
        outs[0][...] = full[...]
        return
    deep = full.shape[0] // (halves * slab)
    for x in range(halves):
        for z in range(deep):
            block = (z ^ place_ref[1]) * halves + (x ^ place_ref[2])
            start = pl.multiple_of(block * slab, slab)
            target = outs[x] if len(outs) > 1 else outs[0].at[x]
            target[z * slab : (z + 1) * slab, :] = full[pl.ds(start, slab), :]


def mlp_grads(place, c, du_b, z, grad_b, halves, slab):
    width = c[0].shape[1]
    local = z[0].shape[1] // GROUPS
    cuts = len(c)

    def kernel(place_ref, *refs):
        c_refs, du_refs = refs[:cuts], refs[cuts : 2 * cuts]
        z_refs, g_refs = refs[2 * cuts : 3 * cuts], refs[3 * cuts : 4 * cuts]
        outs = refs[4 * cuts :]
        full = outs[-1]

        def over_rows(lefts, rights, cols):
            return sum(dot(a[...], b[:, cols], 0, 0) for a, b in zip(lefts, rights))

        for g, out in enumerate((outs[:-2], outs[-2:-1])):
            cols = slice(g * local, (g + 1) * local)
            full[:, :local] = over_rows(c_refs, du_refs, cols).astype(bf16)
            full[:, local:] = over_rows(g_refs, z_refs, cols).astype(bf16)
            cut(full, out, place_ref, halves, slab)

    return call(
        kernel,
        grad_outs(width, 2 * local, halves),
        place,
        *c,
        *du_b,
        *z,
        *grad_b,
        scratch=[((width, 2 * local), bf16)],
        scalars=1,
    )


def attn_bwd(layer, grad, own, recv, h1, gains, weights, q, k, v, prob, pick):
    win_rows, rows = pick.shape
    width = grad[0].shape[1]
    cuts = len(grad)
    panes = win_rows // SLOT
    *weights, at = weights
    local = q.shape[3]
    heads = local // HEAD_DIM
    factor = HEAD_DIM ** (-0.5)

    def kernel(*refs):
        g_refs, own_refs = refs[:cuts], refs[cuts : 2 * cuts]
        recv_refs, h1_refs = refs[2 * cuts : 3 * cuts], refs[3 * cuts : 4 * cuts]
        gain_ref, w0, w1, q_ref, k_ref, v_ref, prob_ref, pick_ref = refs[4 * cuts : 4 * cuts + 8]
        dh_ref, dhb_ref, dp_ref, part_ref, sum_ref, ds_ref = refs[4 * cuts + 8 : 4 * cuts + 14]
        dm_ref, dw_ref, bias_ref = refs[4 * cuts + 14 :]

        def whole(parts):
            return jnp.concatenate(parts, axis=0) if cuts > 1 else parts[0]

        normed, inverse = unit_norm(whole([r[...] for r in h1_refs]))
        upstream = whole(
            [a[...].astype(f32) + b[...].astype(f32) for a, b in zip(own_refs, recv_refs)]
        )
        d_mid, d_gain, d_off = norm_back(upstream, normed, inverse, gain_ref[layer, 1:2])
        dh1 = whole([r[...] for r in g_refs]) + d_mid
        dh_ref[...] = dh1
        sum_ref[...] = jnp.zeros_like(sum_ref)
        sum_ref[0:1, :] = d_gain
        sum_ref[1:2, :] = d_off
        sum_ref[2:3, :] = jnp.sum(dh1, axis=0, keepdims=True)
        dh_b = dh1.astype(bf16)
        dhb_ref[...] = dh_b
        for g, w in enumerate((w0, w1)):
            d_mixed = dot(dh_b, w[:, at + 3 * local : at + 4 * local], 1, 0).astype(bf16)
            d_win = dot(pick_ref[...], d_mixed, 1, 0).astype(bf16)
            dm_ref[g] = d_win.reshape(panes, SLOT, local)
        ds_ref[...] = jnp.zeros_like(ds_ref)
        bias_ref[...] = jnp.zeros_like(bias_ref)
        masks = head_masks(local)

        def step(w, carry):
            for g in range(GROUPS):
                keys, values = k_ref[g, w], v_ref[g, w]
                d_out = spread(dm_ref[g, w], masks)
                queries = spread(q_ref[g, w], masks)
                probs = prob_ref[w, g]
                d_prob = dot(d_out, values, 1, 1)
                d_value = dot(probs.astype(bf16), d_out, 0, 0)
                d_score = probs * (d_prob - jnp.sum(probs * d_prob, axis=-1, keepdims=True))
                ds_ref[g] += d_score
                d_score_b = d_score.astype(bf16)
                d_query = gather_heads(dot(d_score_b, keys, 1, 0), masks) * factor
                d_key = dot(d_score_b, queries, 0, 0)
                base = g * 3 * local
                dw_ref[w, :, base : base + local] = d_query.astype(bf16)
                dw_ref[w, :, base + local : base + 2 * local] = d_key.astype(bf16)
                dw_ref[w, :, base + 2 * local : base + 3 * local] = d_value.astype(bf16)
                bias_ref[0:1, g * local : (g + 1) * local] += jnp.sum(d_query, axis=0, keepdims=True)
                bias_ref[1:2, g * local : (g + 1) * local] += jnp.sum(d_value, axis=0, keepdims=True)
            return carry

        lax.fori_loop(0, panes, step, 0)
        sum_ref[3:4, : GROUPS * local] = bias_ref[0:1, :]
        sum_ref[4:5, : GROUPS * local] = bias_ref[1:2, :]
        d_proj = dot(
            pick_ref[...], dw_ref[...].reshape(win_rows, GROUPS * 3 * local), 0, 0
        ).astype(bf16)
        dp_ref[...] = d_proj
        part = None
        for g, w in enumerate((w0, w1)):
            term = dot(d_proj[:, g * 3 * local : (g + 1) * 3 * local], w[:, at : at + 3 * local], 1, 1)
            part = term if part is None else part + term
        part_ref[...] = part.astype(bf16)

    outs = [
        ((rows, width), f32),
        ((rows, width), bf16),
        ((rows, GROUPS * 3 * local), bf16),
        ((rows, width), bf16),
        ((8, width), f32),
        ((GROUPS, heads * SLOT, SLOT), f32),
    ]
    return call(
        kernel,
        outs,
        *grad,
        *own,
        *recv,
        *h1,
        gains,
        *weights,
        q,
        k,
        v,
        prob,
        pick,
        scratch=[
            ((GROUPS, panes, SLOT, local), bf16),
            ((panes, SLOT, GROUPS * 3 * local), bf16),
            ((8, GROUPS * local), f32),
        ],
    )


def attn_grads(place, a, d_proj, mixed, dh_b, halves, slab):
    width = a.shape[1]
    local = mixed.shape[1] // GROUPS

    def kernel(place_ref, a_ref, dp_ref, m_ref, g_ref, *outs):
        full = outs[-1]
        for g, out in enumerate((outs[:-2], outs[-2:-1])):
            full[:, : 3 * local] = dot(
                a_ref[...], dp_ref[:, g * 3 * local : (g + 1) * 3 * local], 0, 0
            ).astype(bf16)
            full[:, 3 * local :] = dot(
                g_ref[...], m_ref[:, g * local : (g + 1) * local], 0, 0
            ).astype(bf16)
            cut(full, out, place_ref, halves, slab)

    return call(
        kernel,
        grad_outs(width, 4 * local, halves),
        place,
        a,
        d_proj,
        mixed,
        dh_b,
        scratch=[((width, 4 * local), bf16)],
        scalars=1,
    )


def tail(dh1, own, recv, hidden, gains, cells):
    rows, width = dh1.shape
    images = rows // ROWS

    def kernel(d_ref, own_ref, recv_ref, h_ref, gain_ref, o_ref, sum_ref):
        normed, inverse = unit_norm(h_ref[...])
        upstream = own_ref[...].astype(f32) + recv_ref[...].astype(f32)
        first_grad, d_gain, d_off = norm_back(upstream, normed, inverse, gain_ref[0, 0:1])
        store_images(d_ref[...] + first_grad, o_ref, images)
        sum_ref[...] = jnp.zeros_like(sum_ref)
        sum_ref[1:2, :] = d_gain
        sum_ref[2:3, :] = d_off

    outs = [((images, cells, width), f32), ((8, width), f32)]
    return call(kernel, outs, dh1, own, recv, hidden, gains)


def order(blocks, place, member):
    rows, cols = blocks[0].shape

    def kernel(place_ref, *refs):
        out = refs[-1]
        for s in range(len(blocks)):
            start = pl.multiple_of((place_ref[member] ^ s) * rows, rows)
            out[pl.ds(start, rows), :] = refs[s][...]

    outs = [((rows * len(blocks), cols), blocks[0].dtype)]
    return call(kernel, outs, place, *blocks, scalars=1)[0]


def pack(inwards, outwards, widening, narrowing):
    layers, _, slab, local = inwards.shape
    hidden = widening.shape[2]

    def kernel(in_ref, out_ref, wide_ref, narrow_ref, *packed):
        for l in range(layers):
            part_a, part_b = packed[2 * l : 2 * l + 2]
            for j in range(3):
                part_a[:, j * local : (j + 1) * local] = in_ref[l, j].astype(bf16)
            part_a[:, 3 * local :] = out_ref[l].astype(bf16)
            part_b[:, :hidden] = wide_ref[l].astype(bf16)
            part_b[:, hidden:] = narrow_ref[l].astype(bf16)

    outs = [((slab, 4 * local), bf16), ((slab, 2 * hidden), bf16)] * layers
    return call(kernel, outs, inwards, outwards, widening, narrowing)


def adam_all(parts, states):
    layers = len(parts)
    flat = [p for groups in parts for terms in groups for p in terms]

    def kernel(*refs):
        blocks, refs = refs[: len(flat)], refs[len(flat) :]
        ins, outs = refs[:12], refs[12:]

        def update(member, index, gradient):
            weight, mean, square = (r[index] for r in ins[3 * member : 3 * member + 3])
            new = (gradient,) + adam_update(weight, gradient, mean, square, decay_rate)
            for ref, value in zip(outs[4 * member : 4 * member + 4], new):
                ref[index] = value

        used = 0
        for l in range(layers):
            sums = []
            for terms in parts[l]:
                sums.append(tree([r[...].astype(f32) for r in blocks[used : used + len(terms)]]))
                used += len(terms)
            total = jnp.concatenate(sums, axis=1) if len(sums) > 1 else sums[0]
            at = 0
            for member in range(4):
                shape = ins[3 * member].shape
                for j in range(shape[1] if len(shape) == 4 else 1):
                    index = (l, j) if len(shape) == 4 else (l,)
                    update(member, index, total[:, at : at + shape[-1]])
                    at += shape[-1]

    outs = [(state[0].shape, f32) for state in states for _ in range(4)]
    res = call(kernel, outs, *flat, *[v for state in states for v in state])
    return [res[4 * m : 4 * m + 4] for m in range(4)]


def join(place, own, recv):
    count = len(own)
    _, cells, width = own[0].shape
    each = own[0].shape[0]
    images = count * each

    def kernel(place_ref, *refs):
        out_ref = refs[-1]
        lower = place_ref[0] == 0
        for i in range(images):
            mine = refs[i // each][i % each]
            theirs = refs[count + i // each][i % each]
            out_ref[:, i, :] = jnp.where(lower, mine, theirs)
            out_ref[:, images + i, :] = jnp.where(lower, theirs, mine)

    outs = [((cells, 2 * images, width), f32)]
    return call(kernel, outs, place, *own, *recv, scalars=1)[0]


def small_rows(layers, heads):
    per = 8 + heads
    return per, -(-layers * per // 8) * 8


def small_pack(sums_mlp, sums_attn, sums_tail, tables, local):
    layers = len(tables)
    heads = tables[0].shape[0] // GROUPS
    entries = tables[0].shape[1]
    width = sums_mlp[0].shape[1]
    per, rows = small_rows(layers, heads)

    def kernel(*refs):
        ins, outs = refs[:-GROUPS], refs[-GROUPS:]
        for g, out in enumerate(outs):
            out[...] = jnp.zeros_like(out)
            for l in range(layers):
                mlp, attn, late, table = ins[4 * l : 4 * l + 4]
                base = l * per
                out[base : base + 1, :] = late[1:2, :]
                out[base + 1 : base + 2, :] = attn[0:1, :]
                out[base + 2 : base + 3, :] = late[2:3, :]
                out[base + 3 : base + 4, :] = attn[1:2, :]
                out[base + 4 : base + 5, :] = attn[2:3, :]
                out[base + 5 : base + 6, :] = mlp[0:1, :]
                out[base + 6 : base + 7, :] = mlp[3 + g : 4 + g, :]
                out[base + 7 : base + 8, :local] = attn[3:4, g * local : (g + 1) * local]
                out[base + 7 : base + 8, local : 2 * local] = attn[4:5, g * local : (g + 1) * local]
                out[base + 8 : base + 8 + heads, :entries] = table[g * heads : (g + 1) * heads, :]

    flat = [v for quad in zip(sums_mlp, sums_attn, sums_tail, tables) for v in quad]
    return call(kernel, [((rows, width), f32)] * GROUPS, *flat)


def small_adam(total, states):
    layers, _, local = states[0][0].shape
    heads, entries = states[1][0].shape[1:]
    hidden = states[2][0].shape[1]
    width = states[3][0].shape[2]
    per, _ = small_rows(layers, heads)

    def kernel(total_ref, *refs):
        ins, outs = refs[:15], refs[15:]

        def update(member, index, gradient):
            weight, mean, square = (r[index] for r in ins[3 * member : 3 * member + 3])
            new = (gradient,) + adam_update(weight, gradient, mean, square, 0.0)
            for ref, value in zip(outs[4 * member : 4 * member + 4], new):
                ref[index] = value

        for l in range(layers):
            base = l * per
            for row in range(2):
                update(
                    0,
                    (l, slice(row, row + 1)),
                    total_ref[base + 7 : base + 8, row * local : (row + 1) * local],
                )
            update(1, (l,), total_ref[base + 8 : base + 8 + heads, :entries])
            update(2, (slice(l, l + 1),), total_ref[base + 6 : base + 7, :hidden])
            update(3, (l,), total_ref[base : base + 2, :width])
            update(4, (l,), total_ref[base + 2 : base + 6, :width])

    outs = [(state[0].shape, f32) for state in states for _ in range(4)]
    res = call(kernel, outs, total, *[v for state in states for v in state])
    return [res[4 * m : 4 * m + 4] for m in range(5)]


def adam_update(weight, gradient, moment_one, second, decay_on):
    first_new = beta_one * moment_one + (1.0 - beta_one) * gradient
    second_new = beta_two * second + (1.0 - beta_two) * gradient * gradient
    first_hat = first_new / (1.0 - beta_one**STEP)
    second_hat = second_new / (1.0 - beta_two**STEP)
    updated = weight - learn_rate * (
        first_hat / (jnp.sqrt(second_hat) + adam_eps) + decay_on * weight
    )
    return (updated, first_new, second_new)


def turn(x):
    return jnp.swapaxes(x, 1, 2)


def tree(parts):
    while len(parts) > 1:
        parts = [parts[i] + parts[i + 1] for i in range(0, len(parts), 2)]
    return parts[0]


def step(*args):
    (tokens, cotangent, counts), params = args[:3], list(args[3:12])
    first_moments, second_moments = list(args[12:21]), list(args[21:30])
    inwards, inbias, relative, outwards, widening, widebias, narrowing, gains, offsets = params
    layer_total = inwards.shape[0]
    slots, cells, _ = tokens.shape
    images = slots // 2
    local = inwards.shape[3]
    heads = local // HEAD_DIM
    slab = inwards.shape[2]
    n_x = lax.axis_size("x")
    n_z = lax.axis_size("z")
    direct = n_x == 2 and n_x * n_z <= DIRECT_MAX and n_z & (n_z - 1) == 0
    halves = n_x if direct else 0
    c_index = lax.axis_index("c")
    place = jnp.stack(
        [
            c_index,
            lax.axis_index("z"),
            lax.axis_index("x"),
            lax.axis_index("z") * n_x + lax.axis_index("x"),
        ]
    ).astype(jnp.int32)
    dp = ("z", "x")

    def swap(x, axis):
        return lax.ppermute(x, axis, [(0, 1), (1, 0)])

    def swap_each(parts):
        received = []
        for x in parts:
            received.append(swap(x, "y"))
        return received

    def xor_z(x, s):
        return lax.ppermute(x, "z", [(i, i ^ s) for i in range(n_z)])

    def xor_dp(x, s):
        return lax.ppermute(x, dp, [(i, i ^ s) for i in range(n_x * n_z)])

    def gather_now(p):
        if not direct:
            return lax.all_gather(p, dp, axis=0, tiled=True)
        blocks = [p] + [xor_dp(p, s) for s in range(1, n_x * n_z)]
        return order(blocks, place, 3)

    def gather_staged(p):
        if not direct:
            return lax.all_gather(p, dp, axis=0, tiled=True)
        away = swap(p, "x")
        pair = order([p, away], place, 2)
        blocks = [pair] + [xor_z(pair, s) for s in range(1, n_z)]
        return order(blocks, place, 1)

    def scatter_half(own, other):
        recv = swap(other, "c")
        if not direct:
            return (own[0].astype(f32) + recv.astype(f32)).astype(bf16)
        away = (own[1].astype(f32) + recv[1].astype(f32)).astype(bf16)
        back = swap(away, "x")
        return own[0].astype(f32) + recv[0].astype(f32) + back.astype(f32)

    def scatter_rest(halves_of):
        joined = jnp.concatenate(halves_of, axis=1) if len(halves_of) > 1 else halves_of[0]
        near = joined.astype(bf16)
        if not direct:
            return [lax.psum_scatter(near, dp, scatter_dimension=0, tiled=True)]
        return [near[:slab]] + [xor_z(near[s * slab : (s + 1) * slab], s) for s in range(1, n_z)]

    def sum_dp(x):
        if not direct:
            return lax.psum(x, dp)
        x = x + swap(x, "x")
        return tree([x if s == 0 else xor_z(x, s) for s in range(n_z)])

    shards = pack(inwards, turn(outwards), widening, turn(narrowing))
    whole = []
    for i, shard in enumerate(shards):
        full = gather_staged(shard) if i else gather_now(shard)
        whole.append((full, swap(full, "c"), 0))
    weights_a, weights_b = whole[0::2], whole[1::2]

    tables = turn(relative)
    biases = (inbias, swap(inbias, "c"))
    wide_biases = (widebias, swap(widebias, "c"))
    tables = jnp.concatenate([tables, swap(tables, "c")], axis=1)
    lookup = lookup_onehot()
    pos = []
    for l in range(layer_total):
        mask = pane_mask(l % 2 == 1)
        upper = lax.reduce_precision(tables[l], 8, 7)
        middle = lax.reduce_precision(tables[l] - upper, 8, 7)
        terms = jnp.concatenate([upper, middle, tables[l] - upper - middle], axis=0)
        terms = dot(terms.astype(bf16), lookup, 1, 0).reshape(3, -1, SLOT * SLOT)
        spread_bias = (terms[0] + terms[1] + terms[2]).reshape(GROUPS, heads, SLOT, SLOT)
        full = spread_bias[None] + jnp.asarray(mask)[:, None, None]
        pos.append(full.reshape(mask.shape[0], GROUPS, heads * SLOT, SLOT))
    picks = []
    for l in range(min(layer_total, 2)):
        picks.append(selection(l % 2 == 1, images))

    saved = []
    source = (lax.dynamic_slice_in_dim(tokens, c_index * images, images, 0),)
    for l in range(layer_total):
        cuts = images if l == layer_total - 1 else 1
        hidden, a, q, k, v, prob, mixed, *own = attn_fwd(
            l, gains, offsets, source, weights_a[l], biases, pos[l], picks[l % 2], cuts
        )
        recv = swap_each(own)
        res = []
        for i in range(cuts):
            res.append(
                mlp_fwd(l, i, hidden, own[i], recv[i], gains, offsets, weights_b[l], wide_biases)
            )
        h1, c, z, slope, own = ([r[m] for r in res] for m in range(5))
        recv = swap_each(own)
        source = (h1[0], own[0], recv[0])
        saved.append((hidden, a, q, k, v, prob, mixed, h1, c, z, slope))

    cot_mine = lax.dynamic_slice_in_dim(cotangent, c_index * images, images, 0)
    back = [(place, counts, cot_mine) + terms for terms in zip(h1, own, recv)]
    sums_mlp, sums_attn, score_sums = [None] * layer_total, [None] * layer_total, [None] * layer_total
    grads = [None] * layer_total
    sums_tail = [None] * layer_total
    for l in reversed(range(layer_total)):
        hidden, a, q, k, v, prob, mixed, h1, c, z, slope = saved[l]
        last = l == layer_total - 1
        res = []
        for i, terms in enumerate(back):
            res.append(mlp_bwd(l, last, i, terms, gains, offsets, slope[i], weights_b[l]))
        grad, grad_b, du_b, own, sums = ([r[m] for r in res] for m in range(5))
        sums_mlp[l] = sum(sums[1:], sums[0])
        if last:
            out_mine = [r[5] for r in res]
        else:
            sums_tail[l + 1] = sums_mlp[l]
        recv = swap_each(own)
        pair = mlp_grads(place, c, du_b, z, grad_b, halves, slab)
        half_b = scatter_half(pair[:-1], pair[-1])
        dh1, dh_b, d_proj, part_in, sums_attn[l], score_sums[l] = attn_bwd(
            l, grad, own, recv, h1, gains, weights_a[l], q, k, v, prob, picks[l % 2]
        )
        back = [(dh1, part_in, swap(part_in, "y"), hidden)]
        pair = attn_grads(place, a, d_proj, mixed, dh_b, halves, slab)
        half_a = scatter_half(pair[:-1], pair[-1])
        if l:
            grads[l] = [scatter_rest([half_a, half_b])]
        else:
            grads[l] = [scatter_rest([half_a]), scatter_rest([half_b])]
    grad_mine, sums_tail[0] = tail(*back[0], gains, cells)

    def both_halves(x):
        recv = [swap(part, "c") for part in x]
        return jnp.swapaxes(join(place, x, recv), 0, 1)

    output = both_halves(out_mine)
    grad_tokens = both_halves([grad_mine])

    tables = []
    for l in range(layer_total):
        flat = score_sums[l].reshape(GROUPS * heads, SLOT * SLOT)
        upper = lax.reduce_precision(flat, 8, 7)
        both = jnp.concatenate([upper, flat - upper], axis=0).astype(bf16)
        both = dot(both, lookup, 1, 1)
        tables.append(both[: GROUPS * heads] + both[GROUPS * heads :])
    own_rows, other_rows = small_pack(sums_mlp, sums_attn, sums_tail, tables, local)
    other_rows = swap(other_rows, "c")
    total = sum_dp(own_rows + other_rows)

    def states(m):
        return params[m], first_moments[m], second_moments[m]

    results = [None] * len(params)
    matrices = [states(0), [turn(v) for v in states(3)], states(4), [turn(v) for v in states(6)]]
    updated = adam_all(grads, matrices)
    for m, result in zip((0, 3, 4, 6), updated):
        results[m] = [turn(v) for v in result] if m in (3, 6) else result
    small = [states(1), [turn(v) for v in states(2)], states(5), states(7), states(8)]
    updated = small_adam(total, small)
    for m, result in zip((1, 2, 5, 7, 8), updated):
        results[m] = [turn(v) for v in result] if m == 2 else result
    return (output, grad_tokens) + tuple(r[kind] for kind in range(4) for r in results)


def solution(mesh):
    n_dp, n_mp = mesh.shape["dp"], mesh.shape["mp"]
    inner = Mesh(
        mesh.devices.reshape(n_dp // 2, 2, n_mp // 2, 2), ("z", "x", "y", "c")
    )
    dp = ("z", "x")
    mp = ("y", "c")
    batch = P(dp, None, None)
    member_specs = (
        P(None, None, dp, mp),
        P(None, None, mp),
        P(None, None, mp),
        P(None, mp, dp),
        P(None, dp, mp),
        P(None, mp),
        P(None, mp, dp),
        P(),
        P(),
    )
    in_specs = (batch, batch, P(dp)) + member_specs * 3
    out_specs = (batch, batch) + member_specs * 4
    return jax.shard_map(step, mesh=inner, in_specs=in_specs, out_specs=out_specs, check_vma=False)
```

```python
import jax
import jax.numpy as jnp
import numpy as np
from jax import lax
from jax.experimental import pallas as pl
from jax.experimental.pallas import tpu as pltpu
from jax.sharding import Mesh
from jax.sharding import PartitionSpec as P


HEAD_DIM = 32
WIN = 7
SIDE = 14
SHIFT = 3
STEP = 3

norm_eps = 1e-05
beta_one = 0.9
beta_two = 0.999
learn_rate = 0.02
decay_rate = 0.05
adam_eps = 1e-08

CELLS = WIN * WIN
PANES = (SIDE // WIN) ** 2
SLOT = 64
GROUPS = 2
DIRECT_MAX = 8
UNROLL = 2
ROWS = -(-SIDE * SIDE // 8) * 8
VMEM_BYTES = 60 * 1024 * 1024
f32 = jnp.float32
bf16 = jnp.bfloat16


def window_order(shifted):
    grid = np.arange(SIDE * SIDE).reshape(SIDE, SIDE)
    if shifted:
        grid = np.roll(grid, (-SHIFT, -SHIFT), axis=(0, 1))
    side_panes = SIDE // WIN
    return grid.reshape(side_panes, WIN, side_panes, WIN).transpose(0, 2, 1, 3).reshape(-1, CELLS)


def selection(shifted):
    source = np.full((PANES, SLOT), -1, np.int32)
    source[:, :CELLS] = window_order(shifted)
    wanted = jnp.asarray(source.reshape(1, -1))
    return (wanted == jnp.arange(ROWS, dtype=jnp.int32)[:, None]).astype(bf16)


def to_panes(pick, rows):
    images = rows.shape[0] // ROWS
    parts = [dot(pick, rows[i * ROWS : (i + 1) * ROWS].astype(bf16), 0, 0) for i in range(images)]
    return jnp.concatenate(parts, axis=0).astype(bf16)


def from_panes(pick, panes_ref):
    panes, _, cols = panes_ref.shape
    parts = [
        dot(pick, panes_ref[i : i + PANES].reshape(PANES * SLOT, cols), 1, 0)
        for i in range(0, panes, PANES)
    ]
    return jnp.concatenate(parts, axis=0).astype(bf16)


def lookup_onehot():
    places = np.arange(CELLS)
    rowpos, colpos = places // WIN, places % WIN
    lookup = (rowpos[:, None] - rowpos[None, :] + WIN - 1) * (2 * WIN - 1) + (
        colpos[:, None] - colpos[None, :] + WIN - 1
    )
    full = np.full((SLOT, SLOT), -1, np.int32)
    full[:CELLS, :CELLS] = lookup
    entries = jnp.arange((2 * WIN - 1) ** 2, dtype=jnp.int32)
    return (entries[:, None] == jnp.asarray(full.reshape(1, -1))).astype(bf16)


def pane_mask(shifted):
    pad = np.zeros((SLOT, SLOT), np.float32)
    pad[:, CELLS:] = -1e30
    if not shifted:
        return pad[None]
    coords = np.arange(SIDE)
    stripe = (coords >= SIDE - WIN).astype(int) + (coords >= SIDE - SHIFT).astype(int)
    region = (stripe[:, None] * 3 + stripe[None, :]).reshape(-1)
    side_panes = SIDE // WIN
    per = region.reshape(side_panes, WIN, side_panes, WIN).transpose(0, 2, 1, 3).reshape(-1, CELLS)
    out = np.repeat(pad[None], PANES, axis=0)
    out[:, :CELLS, :CELLS] = np.where(per[:, :, None] != per[:, None, :], -100.0, 0.0)
    return out


def dot(left, right, lc, rc):
    return lax.dot_general(left, right, (((lc,), (rc,)), ((), ())), preferred_element_type=f32)


def unit_norm(hidden):
    centered = hidden - jnp.mean(hidden, axis=-1, keepdims=True)
    inverse = lax.rsqrt(jnp.mean(centered * centered, axis=-1, keepdims=True) + norm_eps)
    return centered * inverse, inverse


def norm_back(upstream, normed, inverse, gain):
    d_normed = upstream * gain
    source = inverse * (
        d_normed
        - jnp.mean(d_normed, axis=-1, keepdims=True)
        - normed * jnp.mean(d_normed * normed, axis=-1, keepdims=True)
    )
    return source, jnp.sum(upstream * normed, axis=0, keepdims=True), jnp.sum(
        upstream, axis=0, keepdims=True
    )


def head_masks(width):
    lane = lax.broadcasted_iota(jnp.int32, (1, width), 1) // HEAD_DIM
    return [lane == head for head in range(width // HEAD_DIM)]


def spread(value, masks):
    zero = jnp.zeros_like(value)
    return jnp.concatenate([jnp.where(mask, value, zero) for mask in masks], axis=0)


def gather_heads(stacked, masks):
    total = None
    for head, mask in enumerate(masks):
        part = jnp.where(mask, stacked[head * SLOT : (head + 1) * SLOT], 0.0)
        total = part if total is None else total + part
    return total


def call(kernel, outs, *args, scratch=(), scalars=0):
    specs = [pl.BlockSpec(memory_space=pltpu.SMEM)] * scalars
    specs += [pl.BlockSpec(memory_space=pltpu.VMEM)] * (len(args) - scalars)
    return pl.pallas_call(
        kernel,
        in_specs=specs,
        out_shape=[jax.ShapeDtypeStruct(shape, dtype) for shape, dtype in outs],
        scratch_shapes=[pltpu.VMEM(shape, dtype) for shape, dtype in scratch],
        compiler_params=pltpu.CompilerParams(vmem_limit_bytes=VMEM_BYTES),
    )(*args)


def load_images(images_ref, buffer, images, first=0):
    cells, width = images_ref.shape[1:]
    for i in range(images):
        buffer[i * ROWS : i * ROWS + cells, :] = images_ref[first + i]
        buffer[i * ROWS + cells : (i + 1) * ROWS, :] = jnp.zeros((ROWS - cells, width), f32)


def store_images(value, out, images):
    cells = out.shape[1]
    for i in range(images):
        out[i] = value[i * ROWS : i * ROWS + cells, :]


def attn_fwd(layer, gains, offsets, source, weights, biases, pos, pick, cuts):
    first = layer == 0
    images = source[0].shape[0] if first else source[0].shape[0] // ROWS
    rows, panes = images * ROWS, images * PANES
    *weights, at = weights
    width = weights[0].shape[0]
    local = biases[0].shape[2]
    heads = local // HEAD_DIM
    masks_n = pos.shape[0]
    factor = HEAD_DIM ** (-0.5)
    n_src = len(source)

    def kernel(*refs):
        src = refs[:n_src]
        gain_ref, off_ref, w0, w1, b0, b1, pos_ref, pick_ref = refs[n_src : n_src + 8]
        h_ref, a_ref, q_ref, k_ref, v_ref, prob_ref, mixed_ref = refs[n_src + 8 : n_src + 15]
        part_refs, mw_ref = refs[n_src + 15 : -1], refs[-1]
        if first:
            load_images(src[0], h_ref, rows // ROWS)
            hidden = h_ref[...]
        else:
            hidden = src[0][...] + (
                src[1][...].astype(f32) + src[2][...].astype(f32) + off_ref[layer - 1, 3:4]
            )
            h_ref[...] = hidden
        normed, _ = unit_norm(hidden)
        a = normed * gain_ref[layer, 0:1] + off_ref[layer, 0:1]
        a_ref[...] = a.astype(bf16)
        a_win = to_panes(pick_ref[...], a)
        for g, (w, bias_ref) in enumerate(((w0, b0), (w1, b1))):
            proj = dot(a_win, w[:, at : at + 3 * local], 1, 0)
            q = ((proj[:, :local] + bias_ref[layer, 0:1]) * factor).astype(bf16)
            k = proj[:, local : 2 * local].astype(bf16)
            v = (proj[:, 2 * local :] + bias_ref[layer, 1:2]).astype(bf16)
            q_ref[g] = q.reshape(panes, SLOT, local)
            k_ref[g] = k.reshape(panes, SLOT, local)
            v_ref[g] = v.reshape(panes, SLOT, local)
        masks = head_masks(local)

        def step(w, carry):
            for g in range(GROUPS):
                q, k, v = q_ref[g, w], k_ref[g, w], v_ref[g, w]
                score = dot(spread(q, masks), k, 1, 1) + pos_ref[w % masks_n if masks_n > 1 else 0, g]
                top = jnp.max(score, axis=-1, keepdims=True)
                grown = jnp.exp(score - top)
                prob = grown * (1.0 / jnp.sum(grown, axis=-1, keepdims=True))
                prob_ref[w, g] = prob
                mixed = gather_heads(dot(prob.astype(bf16), v, 1, 0), masks)
                mw_ref[w, :, g * local : (g + 1) * local] = mixed.astype(bf16)
            return carry

        lax.fori_loop(0, panes, step, 0, unroll=UNROLL)
        mixed = from_panes(pick_ref[...], mw_ref)
        mixed_ref[...] = mixed
        part = None
        for g, w in enumerate((w0, w1)):
            term = dot(mixed[:, g * local : (g + 1) * local], w[:, at + 3 * local : at + 4 * local], 1, 1)
            part = term if part is None else part + term
        for i, part_ref in enumerate(part_refs):
            part_ref[...] = part[i * rows // cuts : (i + 1) * rows // cuts].astype(bf16)

    outs = [
        ((rows, width), f32),
        ((rows, width), bf16),
        ((GROUPS, panes, SLOT, local), bf16),
        ((GROUPS, panes, SLOT, local), bf16),
        ((GROUPS, panes, SLOT, local), bf16),
        ((panes, GROUPS, heads * SLOT, SLOT), f32),
        ((rows, GROUPS * local), bf16),
    ] + [((rows // cuts, width), bf16)] * cuts
    return call(
        kernel,
        outs,
        *source,
        gains,
        offsets,
        *weights,
        *biases,
        pos,
        pick,
        scratch=[((panes, SLOT, GROUPS * local), bf16)],
    )


def mlp_fwd(layer, cut_index, hidden, own, recv, gains, offsets, weights, wide_biases):
    *weights, at = weights
    rows, width = own.shape
    first = cut_index * rows
    local = wide_biases[0].shape[1]

    def kernel(
        h_ref, own_ref, recv_ref, gain_ref, off_ref, w0, w1, b0, b1, h1_ref, c_ref, z_ref, s_ref, p_ref
    ):
        h1 = h_ref[first : first + rows] + (own_ref[...].astype(f32) + recv_ref[...].astype(f32) + off_ref[layer, 2:3])
        h1_ref[...] = h1
        normed, _ = unit_norm(h1)
        c = (normed * gain_ref[layer, 1:2] + off_ref[layer, 1:2]).astype(bf16)
        c_ref[...] = c
        part = None
        for g, (w, bias_ref) in enumerate(((w0, b0), (w1, b1))):
            u = dot(c, w[:, at : at + local], 1, 0) + bias_ref[layer : layer + 1, :]
            cdf = 0.5 * (1.0 + lax.erf(u * 0.7071067811865476))
            density = jnp.exp(-0.5 * u * u) * 0.3989422804014327
            z = (u * cdf).astype(bf16)
            z_ref[:, g * local : (g + 1) * local] = z
            s_ref[:, g * local : (g + 1) * local] = (cdf + u * density).astype(bf16)
            term = dot(z, w[:, at + local : at + 2 * local], 1, 1)
            part = term if part is None else part + term
        p_ref[...] = part.astype(bf16)

    outs = [
        ((rows, width), f32),
        ((rows, width), bf16),
        ((rows, GROUPS * local), bf16),
        ((rows, GROUPS * local), bf16),
        ((rows, width), bf16),
    ]
    return call(kernel, outs, hidden, own, recv, gains, offsets, *weights, *wide_biases)


def mlp_bwd(layer, last, cut_index, source, gains, offsets, slope, weights):
    *weights, at = weights
    rows, width = source[3].shape
    local = slope.shape[1] // GROUPS
    n_src = len(source)

    def kernel(*refs):
        src = refs[:n_src]
        gain_ref, off_ref, s_ref, w0, w1 = refs[n_src : n_src + 5]
        g_ref, gb_ref, du_ref, p_ref, sum_ref = refs[n_src + 5 : n_src + 10]
        sum_ref[...] = jnp.zeros_like(sum_ref)
        if last:
            place_ref, count_ref = src[:2]
            images = rows // ROWS
            load_images(src[2], g_ref, images, cut_index * images)
            result = src[3][...] + (src[4][...].astype(f32) + src[5][...].astype(f32) + off_ref[layer, 3:4])
            out_ref = refs[n_src + 10]
            cells = out_ref.shape[1]
            for i in range(images):
                slot = place_ref[0] * src[2].shape[0] + cut_index * images + i
                keep = jnp.where(slot < count_ref[0], 1.0, 0.0)
                out_ref[i] = result[i * ROWS : i * ROWS + cells, :] * keep
                g_ref[i * ROWS : (i + 1) * ROWS, :] = g_ref[i * ROWS : (i + 1) * ROWS, :] * keep
            grad = g_ref[...]
        else:
            normed, inverse = unit_norm(src[3][...])
            upstream = src[1][...].astype(f32) + src[2][...].astype(f32)
            first_grad, d_gain, d_off = norm_back(
                upstream, normed, inverse, gain_ref[layer + 1, 0:1]
            )
            grad = src[0][...] + first_grad
            sum_ref[1:2, :] = d_gain
            sum_ref[2:3, :] = d_off
            g_ref[...] = grad
        sum_ref[0:1, :] = jnp.sum(grad, axis=0, keepdims=True)
        grad_b = grad.astype(bf16)
        gb_ref[...] = grad_b
        part = None
        for g, w in enumerate((w0, w1)):
            du = dot(grad_b, w[:, at + local : at + 2 * local], 1, 0) * s_ref[:, g * local : (g + 1) * local].astype(f32)
            sum_ref[3 + g : 4 + g, :local] = jnp.sum(du, axis=0, keepdims=True)
            du_b = du.astype(bf16)
            du_ref[:, g * local : (g + 1) * local] = du_b
            term = dot(du_b, w[:, at : at + local], 1, 1)
            part = term if part is None else part + term
        p_ref[...] = part.astype(bf16)

    outs = [
        ((rows, width), f32),
        ((rows, width), bf16),
        ((rows, GROUPS * local), bf16),
        ((rows, width), bf16),
        ((8, width), f32),
    ]
    if last:
        outs.append(((rows // ROWS, source[2].shape[1], width), f32))
    return call(kernel, outs, *source, gains, offsets, slope, *weights, scalars=2 if last else 0)


def grad_outs(width, cols, halves):
    if not halves:
        return [((width, cols), bf16)] * 2
    half = width // halves
    return [((half, cols), bf16), ((half, cols), bf16), ((halves, half, cols), bf16)]


def cut(full, outs, place_ref, halves, slab):
    if not halves:
        outs[0][...] = full[...]
        return
    deep = full.shape[0] // (halves * slab)
    for x in range(halves):
        for z in range(deep):
            block = (z ^ place_ref[1]) * halves + (x ^ place_ref[2])
            start = pl.multiple_of(block * slab, slab)
            target = outs[x] if len(outs) > 1 else outs[0].at[x]
            target[z * slab : (z + 1) * slab, :] = full[pl.ds(start, slab), :]


def mlp_grads(place, c, du_b, z, grad_b, halves, slab):
    width = c[0].shape[1]
    local = z[0].shape[1] // GROUPS
    cuts = len(c)

    def kernel(place_ref, *refs):
        c_refs, du_refs = refs[:cuts], refs[cuts : 2 * cuts]
        z_refs, g_refs = refs[2 * cuts : 3 * cuts], refs[3 * cuts : 4 * cuts]
        outs = refs[4 * cuts :]
        full = outs[-1]

        def over_rows(lefts, rights, cols):
            return sum(dot(a[...], b[:, cols], 0, 0) for a, b in zip(lefts, rights))

        for g, out in enumerate((outs[:-2], outs[-2:-1])):
            cols = slice(g * local, (g + 1) * local)
            full[:, :local] = over_rows(c_refs, du_refs, cols).astype(bf16)
            full[:, local:] = over_rows(g_refs, z_refs, cols).astype(bf16)
            cut(full, out, place_ref, halves, slab)

    return call(
        kernel,
        grad_outs(width, 2 * local, halves),
        place,
        *c,
        *du_b,
        *z,
        *grad_b,
        scratch=[((width, 2 * local), bf16)],
        scalars=1,
    )


def attn_bwd(layer, grad, own, recv, h1, gains, weights, q, k, v, prob, pick):
    width = grad[0].shape[1]
    cuts = len(grad)
    rows = cuts * grad[0].shape[0]
    panes = rows // ROWS * PANES
    *weights, at = weights
    local = q.shape[3]
    heads = local // HEAD_DIM
    factor = HEAD_DIM ** (-0.5)

    def kernel(*refs):
        g_refs, own_refs = refs[:cuts], refs[cuts : 2 * cuts]
        recv_refs, h1_refs = refs[2 * cuts : 3 * cuts], refs[3 * cuts : 4 * cuts]
        gain_ref, w0, w1, q_ref, k_ref, v_ref, prob_ref, pick_ref = refs[4 * cuts : 4 * cuts + 8]
        dh_ref, dhb_ref, dp_ref, part_ref, sum_ref, ds_ref = refs[4 * cuts + 8 : 4 * cuts + 14]
        dm_ref, dw_ref, bias_ref = refs[4 * cuts + 14 :]

        def whole(parts):
            return jnp.concatenate(parts, axis=0) if cuts > 1 else parts[0]

        normed, inverse = unit_norm(whole([r[...] for r in h1_refs]))
        upstream = whole(
            [a[...].astype(f32) + b[...].astype(f32) for a, b in zip(own_refs, recv_refs)]
        )
        d_mid, d_gain, d_off = norm_back(upstream, normed, inverse, gain_ref[layer, 1:2])
        dh1 = whole([r[...] for r in g_refs]) + d_mid
        dh_ref[...] = dh1
        sum_ref[...] = jnp.zeros_like(sum_ref)
        sum_ref[0:1, :] = d_gain
        sum_ref[1:2, :] = d_off
        sum_ref[2:3, :] = jnp.sum(dh1, axis=0, keepdims=True)
        dh_b = dh1.astype(bf16)
        dhb_ref[...] = dh_b
        for g, w in enumerate((w0, w1)):
            d_mixed = dot(dh_b, w[:, at + 3 * local : at + 4 * local], 1, 0)
            dm_ref[g] = to_panes(pick_ref[...], d_mixed).reshape(panes, SLOT, local)
        ds_ref[...] = jnp.zeros_like(ds_ref)
        bias_ref[...] = jnp.zeros_like(bias_ref)
        masks = head_masks(local)

        def step(w, carry):
            for g in range(GROUPS):
                keys, values = k_ref[g, w], v_ref[g, w]
                d_out = spread(dm_ref[g, w], masks)
                queries = spread(q_ref[g, w], masks)
                probs = prob_ref[w, g]
                d_prob = dot(d_out, values, 1, 1)
                d_value = dot(probs.astype(bf16), d_out, 0, 0)
                d_score = probs * (d_prob - jnp.sum(probs * d_prob, axis=-1, keepdims=True))
                ds_ref[g] += d_score
                d_score_b = d_score.astype(bf16)
                d_query = gather_heads(dot(d_score_b, keys, 1, 0), masks) * factor
                d_key = dot(d_score_b, queries, 0, 0)
                base = g * 3 * local
                dw_ref[w, :, base : base + local] = d_query.astype(bf16)
                dw_ref[w, :, base + local : base + 2 * local] = d_key.astype(bf16)
                dw_ref[w, :, base + 2 * local : base + 3 * local] = d_value.astype(bf16)
                bias_ref[0:1, g * local : (g + 1) * local] += jnp.sum(d_query, axis=0, keepdims=True)
                bias_ref[1:2, g * local : (g + 1) * local] += jnp.sum(d_value, axis=0, keepdims=True)
            return carry

        lax.fori_loop(0, panes, step, 0)
        sum_ref[3:4, : GROUPS * local] = bias_ref[0:1, :]
        sum_ref[4:5, : GROUPS * local] = bias_ref[1:2, :]
        d_proj = from_panes(pick_ref[...], dw_ref)
        dp_ref[...] = d_proj
        part = None
        for g, w in enumerate((w0, w1)):
            term = dot(d_proj[:, g * 3 * local : (g + 1) * 3 * local], w[:, at : at + 3 * local], 1, 1)
            part = term if part is None else part + term
        part_ref[...] = part.astype(bf16)

    outs = [
        ((rows, width), f32),
        ((rows, width), bf16),
        ((rows, GROUPS * 3 * local), bf16),
        ((rows, width), bf16),
        ((8, width), f32),
        ((GROUPS, heads * SLOT, SLOT), f32),
    ]
    return call(
        kernel,
        outs,
        *grad,
        *own,
        *recv,
        *h1,
        gains,
        *weights,
        q,
        k,
        v,
        prob,
        pick,
        scratch=[
            ((GROUPS, panes, SLOT, local), bf16),
            ((panes, SLOT, GROUPS * 3 * local), bf16),
            ((8, GROUPS * local), f32),
        ],
    )


def attn_grads(place, a, d_proj, mixed, dh_b, halves, slab):
    width = a.shape[1]
    local = mixed.shape[1] // GROUPS

    def kernel(place_ref, a_ref, dp_ref, m_ref, g_ref, *outs):
        full = outs[-1]
        for g, out in enumerate((outs[:-2], outs[-2:-1])):
            full[:, : 3 * local] = dot(
                a_ref[...], dp_ref[:, g * 3 * local : (g + 1) * 3 * local], 0, 0
            ).astype(bf16)
            full[:, 3 * local :] = dot(
                g_ref[...], m_ref[:, g * local : (g + 1) * local], 0, 0
            ).astype(bf16)
            cut(full, out, place_ref, halves, slab)

    return call(
        kernel,
        grad_outs(width, 4 * local, halves),
        place,
        a,
        d_proj,
        mixed,
        dh_b,
        scratch=[((width, 4 * local), bf16)],
        scalars=1,
    )


def tail(dh1, own, recv, hidden, gains, cells):
    rows, width = dh1.shape
    images = rows // ROWS

    def kernel(d_ref, own_ref, recv_ref, h_ref, gain_ref, o_ref, sum_ref):
        normed, inverse = unit_norm(h_ref[...])
        upstream = own_ref[...].astype(f32) + recv_ref[...].astype(f32)
        first_grad, d_gain, d_off = norm_back(upstream, normed, inverse, gain_ref[0, 0:1])
        store_images(d_ref[...] + first_grad, o_ref, images)
        sum_ref[...] = jnp.zeros_like(sum_ref)
        sum_ref[1:2, :] = d_gain
        sum_ref[2:3, :] = d_off

    outs = [((images, cells, width), f32), ((8, width), f32)]
    return call(kernel, outs, dh1, own, recv, hidden, gains)


def order(blocks, place, member):
    rows, cols = blocks[0].shape

    def kernel(place_ref, *refs):
        out = refs[-1]
        for s in range(len(blocks)):
            start = pl.multiple_of((place_ref[member] ^ s) * rows, rows)
            out[pl.ds(start, rows), :] = refs[s][...]

    outs = [((rows * len(blocks), cols), blocks[0].dtype)]
    return call(kernel, outs, place, *blocks, scalars=1)[0]


def pack(inwards, outwards, widening, narrowing):
    layers, _, slab, local = inwards.shape
    hidden = widening.shape[2]

    def kernel(in_ref, out_ref, wide_ref, narrow_ref, *packed):
        for l in range(layers):
            part_a, part_b = packed[2 * l : 2 * l + 2]
            for j in range(3):
                part_a[:, j * local : (j + 1) * local] = in_ref[l, j].astype(bf16)
            part_a[:, 3 * local :] = out_ref[l].astype(bf16)
            part_b[:, :hidden] = wide_ref[l].astype(bf16)
            part_b[:, hidden:] = narrow_ref[l].astype(bf16)

    outs = [((slab, 4 * local), bf16), ((slab, 2 * hidden), bf16)] * layers
    return call(kernel, outs, inwards, outwards, widening, narrowing)


def adam_all(parts, states):
    layers = len(parts)
    flat = [p for groups in parts for terms in groups for p in terms]

    def kernel(*refs):
        blocks, refs = refs[: len(flat)], refs[len(flat) :]
        ins, outs = refs[:12], refs[12:]

        def update(member, index, gradient):
            weight, mean, square = (r[index] for r in ins[3 * member : 3 * member + 3])
            new = (gradient,) + adam_update(weight, gradient, mean, square, decay_rate)
            for ref, value in zip(outs[4 * member : 4 * member + 4], new):
                ref[index] = value

        used = 0
        for l in range(layers):
            sums = []
            for terms in parts[l]:
                sums.append(tree([r[...].astype(f32) for r in blocks[used : used + len(terms)]]))
                used += len(terms)
            total = jnp.concatenate(sums, axis=1) if len(sums) > 1 else sums[0]
            at = 0
            for member in range(4):
                shape = ins[3 * member].shape
                for j in range(shape[1] if len(shape) == 4 else 1):
                    index = (l, j) if len(shape) == 4 else (l,)
                    update(member, index, total[:, at : at + shape[-1]])
                    at += shape[-1]

    outs = [(state[0].shape, f32) for state in states for _ in range(4)]
    res = call(kernel, outs, *flat, *[v for state in states for v in state])
    return [res[4 * m : 4 * m + 4] for m in range(4)]


def join(place, own, recv):
    count = len(own)
    _, cells, width = own[0].shape
    each = own[0].shape[0]
    images = count * each

    def kernel(place_ref, *refs):
        out_ref = refs[-1]
        lower = place_ref[0] == 0
        for i in range(images):
            mine = refs[i // each][i % each]
            theirs = refs[count + i // each][i % each]
            out_ref[:, i, :] = jnp.where(lower, mine, theirs)
            out_ref[:, images + i, :] = jnp.where(lower, theirs, mine)

    outs = [((cells, 2 * images, width), f32)]
    return call(kernel, outs, place, *own, *recv, scalars=1)[0]


def small_rows(layers, heads):
    per = 8 + heads
    return per, -(-layers * per // 8) * 8


def small_pack(sums_mlp, sums_attn, sums_tail, tables, local):
    layers = len(tables)
    heads = tables[0].shape[0] // GROUPS
    entries = tables[0].shape[1]
    width = sums_mlp[0].shape[1]
    per, rows = small_rows(layers, heads)

    def kernel(*refs):
        ins, outs = refs[:-GROUPS], refs[-GROUPS:]
        for g, out in enumerate(outs):
            out[...] = jnp.zeros_like(out)
            for l in range(layers):
                mlp, attn, late, table = ins[4 * l : 4 * l + 4]
                base = l * per
                out[base : base + 1, :] = late[1:2, :]
                out[base + 1 : base + 2, :] = attn[0:1, :]
                out[base + 2 : base + 3, :] = late[2:3, :]
                out[base + 3 : base + 4, :] = attn[1:2, :]
                out[base + 4 : base + 5, :] = attn[2:3, :]
                out[base + 5 : base + 6, :] = mlp[0:1, :]
                out[base + 6 : base + 7, :] = mlp[3 + g : 4 + g, :]
                out[base + 7 : base + 8, :local] = attn[3:4, g * local : (g + 1) * local]
                out[base + 7 : base + 8, local : 2 * local] = attn[4:5, g * local : (g + 1) * local]
                out[base + 8 : base + 8 + heads, :entries] = table[g * heads : (g + 1) * heads, :]

    flat = [v for quad in zip(sums_mlp, sums_attn, sums_tail, tables) for v in quad]
    return call(kernel, [((rows, width), f32)] * GROUPS, *flat)


def small_adam(total, states):
    layers, _, local = states[0][0].shape
    heads, entries = states[1][0].shape[1:]
    hidden = states[2][0].shape[1]
    width = states[3][0].shape[2]
    per, _ = small_rows(layers, heads)

    def kernel(total_ref, *refs):
        ins, outs = refs[:15], refs[15:]

        def update(member, index, gradient):
            weight, mean, square = (r[index] for r in ins[3 * member : 3 * member + 3])
            new = (gradient,) + adam_update(weight, gradient, mean, square, 0.0)
            for ref, value in zip(outs[4 * member : 4 * member + 4], new):
                ref[index] = value

        for l in range(layers):
            base = l * per
            for row in range(2):
                update(
                    0,
                    (l, slice(row, row + 1)),
                    total_ref[base + 7 : base + 8, row * local : (row + 1) * local],
                )
            update(1, (l,), total_ref[base + 8 : base + 8 + heads, :entries])
            update(2, (slice(l, l + 1),), total_ref[base + 6 : base + 7, :hidden])
            update(3, (l,), total_ref[base : base + 2, :width])
            update(4, (l,), total_ref[base + 2 : base + 6, :width])

    outs = [(state[0].shape, f32) for state in states for _ in range(4)]
    res = call(kernel, outs, total, *[v for state in states for v in state])
    return [res[4 * m : 4 * m + 4] for m in range(5)]


def adam_update(weight, gradient, moment_one, second, decay_on):
    first_new = beta_one * moment_one + (1.0 - beta_one) * gradient
    second_new = beta_two * second + (1.0 - beta_two) * gradient * gradient
    first_hat = first_new / (1.0 - beta_one**STEP)
    second_hat = second_new / (1.0 - beta_two**STEP)
    updated = weight - learn_rate * (
        first_hat / (jnp.sqrt(second_hat) + adam_eps) + decay_on * weight
    )
    return (updated, first_new, second_new)


def turn(x):
    return jnp.swapaxes(x, 1, 2)


def tree(parts):
    while len(parts) > 1:
        parts = [parts[i] + parts[i + 1] for i in range(0, len(parts), 2)]
    return parts[0]


def step(*args):
    (tokens, cotangent, counts), params = args[:3], list(args[3:12])
    first_moments, second_moments = list(args[12:21]), list(args[21:30])
    inwards, inbias, relative, outwards, widening, widebias, narrowing, gains, offsets = params
    layer_total = inwards.shape[0]
    slots, cells, _ = tokens.shape
    images = slots // 2
    local = inwards.shape[3]
    heads = local // HEAD_DIM
    slab = inwards.shape[2]
    n_x = lax.axis_size("x")
    n_z = lax.axis_size("z")
    direct = n_x == 2 and n_x * n_z <= DIRECT_MAX and n_z & (n_z - 1) == 0
    halves = n_x if direct else 0
    c_index = lax.axis_index("c")
    place = jnp.stack(
        [
            c_index,
            lax.axis_index("z"),
            lax.axis_index("x"),
            lax.axis_index("z") * n_x + lax.axis_index("x"),
        ]
    ).astype(jnp.int32)
    dp = ("z", "x")

    def swap(x, axis):
        return lax.ppermute(x, axis, [(0, 1), (1, 0)])

    def swap_each(parts):
        received = []
        for x in parts:
            received.append(swap(x, "y"))
        return received

    def xor_z(x, s):
        return lax.ppermute(x, "z", [(i, i ^ s) for i in range(n_z)])

    def xor_dp(x, s):
        return lax.ppermute(x, dp, [(i, i ^ s) for i in range(n_x * n_z)])

    def gather_now(p):
        if not direct:
            return lax.all_gather(p, dp, axis=0, tiled=True)
        blocks = [p] + [xor_dp(p, s) for s in range(1, n_x * n_z)]
        return order(blocks, place, 3)

    def gather_staged(p):
        if not direct:
            return lax.all_gather(p, dp, axis=0, tiled=True)
        away = swap(p, "x")
        pair = order([p, away], place, 2)
        blocks = [pair] + [xor_z(pair, s) for s in range(1, n_z)]
        return order(blocks, place, 1)

    def scatter_half(own, other):
        recv = swap(other, "c")
        if not direct:
            return (own[0].astype(f32) + recv.astype(f32)).astype(bf16)
        away = (own[1].astype(f32) + recv[1].astype(f32)).astype(bf16)
        back = swap(away, "x")
        return own[0].astype(f32) + recv[0].astype(f32) + back.astype(f32)

    def scatter_rest(halves_of):
        joined = jnp.concatenate(halves_of, axis=1) if len(halves_of) > 1 else halves_of[0]
        near = joined.astype(bf16)
        if not direct:
            return [lax.psum_scatter(near, dp, scatter_dimension=0, tiled=True)]
        return [near[:slab]] + [xor_z(near[s * slab : (s + 1) * slab], s) for s in range(1, n_z)]

    def sum_dp(x):
        if not direct:
            return lax.psum(x, dp)
        x = x + swap(x, "x")
        return tree([x if s == 0 else xor_z(x, s) for s in range(n_z)])

    shards = pack(inwards, turn(outwards), widening, turn(narrowing))
    whole = []
    for i, shard in enumerate(shards):
        full = gather_staged(shard) if i else gather_now(shard)
        whole.append((full, swap(full, "c"), 0))
    weights_a, weights_b = whole[0::2], whole[1::2]

    tables = turn(relative)
    biases = (inbias, swap(inbias, "c"))
    wide_biases = (widebias, swap(widebias, "c"))
    tables = jnp.concatenate([tables, swap(tables, "c")], axis=1)
    lookup = lookup_onehot()
    pos = []
    for l in range(layer_total):
        mask = pane_mask(l % 2 == 1)
        upper = lax.reduce_precision(tables[l], 8, 7)
        middle = lax.reduce_precision(tables[l] - upper, 8, 7)
        terms = jnp.concatenate([upper, middle, tables[l] - upper - middle], axis=0)
        terms = dot(terms.astype(bf16), lookup, 1, 0).reshape(3, -1, SLOT * SLOT)
        spread_bias = (terms[0] + terms[1] + terms[2]).reshape(GROUPS, heads, SLOT, SLOT)
        full = spread_bias[None] + jnp.asarray(mask)[:, None, None]
        pos.append(full.reshape(mask.shape[0], GROUPS, heads * SLOT, SLOT))
    picks = []
    for l in range(min(layer_total, 2)):
        picks.append(selection(l % 2 == 1))

    saved = []
    source = (lax.dynamic_slice_in_dim(tokens, c_index * images, images, 0),)
    for l in range(layer_total):
        cuts = images if l == layer_total - 1 else 1
        hidden, a, q, k, v, prob, mixed, *own = attn_fwd(
            l, gains, offsets, source, weights_a[l], biases, pos[l], picks[l % 2], cuts
        )
        recv = swap_each(own)
        res = []
        for i in range(cuts):
            res.append(
                mlp_fwd(l, i, hidden, own[i], recv[i], gains, offsets, weights_b[l], wide_biases)
            )
        h1, c, z, slope, own = ([r[m] for r in res] for m in range(5))
        recv = swap_each(own)
        source = (h1[0], own[0], recv[0])
        saved.append((hidden, a, q, k, v, prob, mixed, h1, c, z, slope))

    cot_mine = lax.dynamic_slice_in_dim(cotangent, c_index * images, images, 0)
    back = [(place, counts, cot_mine) + terms for terms in zip(h1, own, recv)]
    sums_mlp, sums_attn, score_sums = [None] * layer_total, [None] * layer_total, [None] * layer_total
    grads = [None] * layer_total
    sums_tail = [None] * layer_total
    for l in reversed(range(layer_total)):
        hidden, a, q, k, v, prob, mixed, h1, c, z, slope = saved[l]
        last = l == layer_total - 1
        res = []
        for i, terms in enumerate(back):
            res.append(mlp_bwd(l, last, i, terms, gains, offsets, slope[i], weights_b[l]))
        grad, grad_b, du_b, own, sums = ([r[m] for r in res] for m in range(5))
        sums_mlp[l] = sum(sums[1:], sums[0])
        if last:
            out_mine = [r[5] for r in res]
        else:
            sums_tail[l + 1] = sums_mlp[l]
        recv = swap_each(own)
        pair = mlp_grads(place, c, du_b, z, grad_b, halves, slab)
        half_b = scatter_half(pair[:-1], pair[-1])
        dh1, dh_b, d_proj, part_in, sums_attn[l], score_sums[l] = attn_bwd(
            l, grad, own, recv, h1, gains, weights_a[l], q, k, v, prob, picks[l % 2]
        )
        back = [(dh1, part_in, swap(part_in, "y"), hidden)]
        pair = attn_grads(place, a, d_proj, mixed, dh_b, halves, slab)
        half_a = scatter_half(pair[:-1], pair[-1])
        if l:
            grads[l] = [scatter_rest([half_a, half_b])]
        else:
            grads[l] = [scatter_rest([half_a]), scatter_rest([half_b])]
    grad_mine, sums_tail[0] = tail(*back[0], gains, cells)

    def both_halves(x):
        recv = [swap(part, "c") for part in x]
        return jnp.swapaxes(join(place, x, recv), 0, 1)

    output = both_halves(out_mine)
    grad_tokens = both_halves([grad_mine])

    tables = []
    for l in range(layer_total):
        flat = score_sums[l].reshape(GROUPS * heads, SLOT * SLOT)
        upper = lax.reduce_precision(flat, 8, 7)
        both = jnp.concatenate([upper, flat - upper], axis=0).astype(bf16)
        both = dot(both, lookup, 1, 1)
        tables.append(both[: GROUPS * heads] + both[GROUPS * heads :])
    own_rows, other_rows = small_pack(sums_mlp, sums_attn, sums_tail, tables, local)
    other_rows = swap(other_rows, "c")
    total = sum_dp(own_rows + other_rows)

    def states(m):
        return params[m], first_moments[m], second_moments[m]

    results = [None] * len(params)
    matrices = [states(0), [turn(v) for v in states(3)], states(4), [turn(v) for v in states(6)]]
    updated = adam_all(grads, matrices)
    for m, result in zip((0, 3, 4, 6), updated):
        results[m] = [turn(v) for v in result] if m in (3, 6) else result
    small = [states(1), [turn(v) for v in states(2)], states(5), states(7), states(8)]
    updated = small_adam(total, small)
    for m, result in zip((1, 2, 5, 7, 8), updated):
        results[m] = [turn(v) for v in result] if m == 2 else result
    return (output, grad_tokens) + tuple(r[kind] for kind in range(4) for r in results)


def solution(mesh):
    n_dp, n_mp = mesh.shape["dp"], mesh.shape["mp"]
    inner = Mesh(
        mesh.devices.reshape(n_dp // 2, 2, n_mp // 2, 2), ("z", "x", "y", "c")
    )
    dp = ("z", "x")
    mp = ("y", "c")
    batch = P(dp, None, None)
    member_specs = (
        P(None, None, dp, mp),
        P(None, None, mp),
        P(None, None, mp),
        P(None, mp, dp),
        P(None, dp, mp),
        P(None, mp),
        P(None, mp, dp),
        P(),
        P(),
    )
    in_specs = (batch, batch, P(dp)) + member_specs * 3
    out_specs = (batch, batch) + member_specs * 4
    return jax.shard_map(step, mesh=inner, in_specs=in_specs, out_specs=out_specs, check_vma=False)
```
